32 devices in a mesh: dev: 32 (over z, y, x, core).
Axes of the slice: x: 2, y: 2, z: 4, core: 2. Of those that a mesh axis runs over, the one named last changes fastest.
Arguments:
- displacement: float32 [3, 131072], P(None, 'dev'), may hold values from -2 to 2
- send_node: int32 [262144], P('dev'), may hold values from -1 to 4095, as said below
- member_slot: int32 [128, 1024], P('dev'), may hold values from 0 to 8191, as said below
- inverse_part: bfloat16 [128, 1024, 1024], P('dev'), may hold values from -0.09375 to 0.09375
- source_coord: float32 [128, 3, 1024], P('dev'), may hold values from 0 to 1
- target_coord: float32 [128, 3, 1024], P('dev'), may hold values from 0 to 1
- unity_weight: float32 [128, 1024], P('dev'), may hold values from 0.1 to 1
- result_pick: int32 [262144], P('dev'), may hold values from -1 to 4095, as said below
- receive_vertex: int32 [262144], P('dev'), may hold values from 0 to 8191
- mesh_before: float32 [3, 512, 96, 512], P(None, 'dev'), may hold values from -6 to 6
Outputs:
- mesh_motion: float32 [3, 512, 96, 512], P(None, 'dev')
The draws below stay inside these ranges and needn't reach their ends.
Inputs may be any that keep to these rules, and one draw needn't show every extreme that they name: `send_node`: each device's entries form 32 blocks of 256, block e for cluster owner e; in each block the live entries (0 or more) come first and -1 fills the rest; each block has at least one live entry and each device has one block with all 256 live. `member_slot`: every entry names a live slot of send_node sent to the cluster's owner. `result_pick`: each device's entries form 32 blocks of 256, block e for fluid owner e; in each block the live entries (0 or more) come first and -1 fills the rest; each block has at least one live entry and each device has one block with all 256 live.
All inputs are finite; a program needn't handle non-finite values.
Results may differ from the reference program's by a relative error of at most 0.00043.
Values sent between devices are 32-bit elements; how exact they have to be, the bound alone decides.
No kernel may reach another device: no remote copies, remote signals or barrier semaphores. Data moves between devices by JAX's collectives and lax.ppermute only.
A program may use at most 128 MiB of HBM per device.

```python
import jax
import jax.numpy as jnp
from jax import lax

NODE_DEV = 4096
CL_DEV = 4
CP = 1024
FT = 1024
GX = 16
GY = 96
GZ = 512
SCAP = 256
RCAP = 256
FIV = 8192
NODES = 131072
CLUSTERS = 128
NX = 512
N_DEV = 32


def slot_counts(key, capacity):
    low = max(1, capacity // 4)
    load = jax.random.randint(jax.random.fold_in(key, 1), (N_DEV,), 1, 5)
    high = jnp.maximum(low, load * capacity // 4)
    raw = jax.random.randint(jax.random.fold_in(key, 2), (N_DEV, N_DEV), 0, 1 << 20)
    counts = low + raw % (high[None, :] - low + 1)
    offset = jax.random.randint(jax.random.fold_in(key, 3), (), 0, N_DEV)
    rows = jnp.arange(N_DEV, dtype=jnp.int32)
    full = rows[None, :] == (rows[:, None] + offset) % N_DEV
    return jnp.where(full, capacity, counts).astype(jnp.int32)


def draw_send_node(key, part):
    base = jax.random.fold_in(key, 101)
    counts = slot_counts(base, SCAP)
    nodes = jax.random.randint(jax.random.fold_in(base, 4), (N_DEV, N_DEV, SCAP), 0, NODE_DEV)
    live = jnp.arange(SCAP, dtype=jnp.int32)[None, None, :] < counts[:, :, None]
    return jnp.where(live, nodes, -1).reshape(-1).astype(jnp.int32)


def draw_member_slot(key, part):
    base = jax.random.fold_in(key, 101)
    counts = slot_counts(base, SCAP)
    source = jax.random.randint(jax.random.fold_in(base, 5), (N_DEV, CL_DEV, CP), 0, N_DEV)
    raw = jax.random.randint(jax.random.fold_in(base, 6), (N_DEV, CL_DEV, CP), 0, 1 << 20)
    owner = jnp.arange(N_DEV, dtype=jnp.int32)[:, None, None]
    live = counts[source, owner]
    slot = source * SCAP + raw % live
    return slot.reshape(N_DEV * CL_DEV, CP).astype(jnp.int32)


def draw_result_pick(key, part):
    base = jax.random.fold_in(key, 202)
    counts = slot_counts(base, RCAP)
    picks = jax.random.randint(jax.random.fold_in(base, 4), (N_DEV, N_DEV, RCAP), 0, CL_DEV * FT)
    live = jnp.arange(RCAP, dtype=jnp.int32)[None, None, :] < counts[:, :, None]
    return jnp.where(live, picks, -1).reshape(-1).astype(jnp.int32)


def with_ends(values, rng, least, top_value):
    spot = [jax.random.randint(jax.random.fold_in(rng, axis), (), 0, length) for axis, length in enumerate(values.shape)]
    longest = values.shape.index(max(values.shape))
    neighbour = spot[:longest] + [(spot[longest] + 1) % values.shape[longest]] + spot[longest + 1:]
    return values.at[tuple(spot)].set(least).at[tuple(neighbour)].set(top_value)


def levels(own_key, dims, pieces, low, high):
    gain, own = 1.0, jax.random.fold_in(own_key, 6)
    for dim, blocks in pieces:
        steps = jnp.exp(jax.random.uniform(jax.random.fold_in(own, dim), (blocks,), jnp.float32, low / len(pieces), high / len(pieces)))
        gain = gain * jnp.repeat(steps, dims[dim] // blocks).reshape([-1 if axis == dim else 1 for axis in range(len(dims))])
    return gain


def scatter_about(key, dims, width, limit, cuts=(), kind=jnp.bfloat16):
    values = jax.random.normal(key, dims, jnp.float32) * width
    if len(cuts) > 0:
        values = levels(key, dims, cuts, -0.22, 0.18) * values
    return jnp.clip(values, min=-limit, max=limit).astype(kind)


def setup_inputs(seed: int = 0) -> dict:
    key_of = jax.random.split(jax.random.key(seed), 11)
    displacement = scatter_about(key_of[0], (3, NODES), 0.25, 2.0, ((1, 32),), jnp.float32)
    send_node = draw_send_node(jax.random.fold_in(key_of[10], 71), 0)
    member_slot = draw_member_slot(jax.random.fold_in(key_of[10], 71), 0)
    inverse_part = scatter_about(key_of[3], (CLUSTERS, CP, CP), (4 * CP) ** -0.5, 0.09375, ((0, 32),))
    source_coord = jnp.clip(1.0 * jax.random.uniform(key_of[4], (CLUSTERS, 3, CP), jnp.float32) ** levels(key_of[4], (CLUSTERS, 3, CP), ((0, 32),), -0.2, 0.2), 0.0, 1.0)
    target_coord = jnp.clip(1.0 * jax.random.uniform(key_of[5], (CLUSTERS, 3, FT), jnp.float32) ** levels(key_of[5], (CLUSTERS, 3, FT), ((0, 32),), -0.2, 0.2), 0.0, 1.0)
    unity_weight = jnp.clip(0.1 + 0.9 * jax.random.uniform(key_of[6], (CLUSTERS, FT), jnp.float32) ** levels(key_of[6], (CLUSTERS, FT), ((0, 32),), -0.2, 0.2), 0.1, 1.0)
    result_pick = draw_result_pick(jax.random.fold_in(key_of[10], 71), 0)
    receive_vertex = with_ends(jax.random.randint(key_of[8], (N_DEV * N_DEV * RCAP,), 0, FIV), jax.random.fold_in(key_of[8], 1), 0, FIV - 1).astype(jnp.int32)
    mesh_before = scatter_about(key_of[9], (3, NX, GY, GZ), 1.0, 6.0, ((1, 32),), jnp.float32)
    return {"displacement": displacement, "send_node": send_node, "member_slot": member_slot, "inverse_part": inverse_part, "source_coord": source_coord, "target_coord": target_coord, "unity_weight": unity_weight, "result_pick": result_pick, "receive_vertex": receive_vertex, "mesh_before": mesh_before}


relax_rate = 0.8
kernel_sharpness = 8.0


def relax(field):
    padded = jnp.pad(field, ((0, 0), (1, 1), (1, 1), (1, 1)))
    beside = padded[:, 2:, 1:-1, 1:-1] + padded[:, :-2, 1:-1, 1:-1]
    beside = beside + padded[:, 1:-1, 2:, 1:-1] + padded[:, 1:-1, :-2, 1:-1]
    beside = beside + padded[:, 1:-1, 1:-1, 2:] + padded[:, 1:-1, 1:-1, :-2]
    moved = field + relax_rate * (beside * (1.0 / 6.0) - field)
    yrows = lax.broadcasted_iota(jnp.int32, field.shape, 2)
    return jnp.where(yrows == 0, field, moved)


def one_cluster(inputs):
    members, inverse, source, target, weight = inputs
    coupling = lax.dot_general(members.astype(jnp.bfloat16), inverse, (((1,), (1,)), ((), ())), preferred_element_type=jnp.float32)
    coefficient = members + coupling
    gap = target[0][:, None] - source[0][None, :]
    spread = gap * gap
    gap = target[1][:, None] - source[1][None, :]
    spread = spread + gap * gap
    gap = target[2][:, None] - source[2][None, :]
    spread = spread + gap * gap
    kernel = jnp.exp(-kernel_sharpness * spread)
    contrib = lax.dot_general(coefficient, kernel, (((1,), (1,)), ((), ())), precision=lax.Precision.HIGHEST, preferred_element_type=jnp.float32)
    return contrib * weight[None, :]


def reference(displacement, send_node, member_slot, inverse_part, source_coord, target_coord, unity_weight, result_pick, receive_vertex, mesh_before):
    count = N_DEV
    plan = send_node.reshape(count, count, SCAP)
    source_dev = jnp.arange(count, dtype=jnp.int32)[:, None, None]
    global_node = (source_dev * NODE_DEV + jnp.maximum(plan, 0)).astype(jnp.int32)
    sent = jnp.where(plan[None] >= 0, displacement[:, global_node], 0.0)
    received = sent.transpose(0, 2, 1, 3).reshape(3, count * count * SCAP)
    owner = (jnp.arange(CLUSTERS, dtype=jnp.int32) // CL_DEV)[:, None]
    flat_slot = (owner * (count * SCAP) + member_slot).astype(jnp.int32)
    members = received[:, flat_slot].transpose(1, 0, 2)
    contrib = lax.map(one_cluster, (members, inverse_part, source_coord, target_coord, unity_weight))
    contrib = contrib.reshape(count, CL_DEV, 3, FT).transpose(0, 2, 1, 3).reshape(count, 3, CL_DEV * FT)
    picks = result_pick.reshape(count, 1, count * RCAP)
    taken = jnp.take_along_axis(contrib, jnp.broadcast_to(jnp.maximum(picks, 0), (count, 3, count * RCAP)), axis=2)
    taken = jnp.where(picks >= 0, taken, 0.0)
    taken = taken.reshape(count, 3, count, RCAP).transpose(1, 2, 0, 3).reshape(3, count * count * RCAP)
    receiver = (jnp.arange(count, dtype=jnp.int32) * FIV)[:, None]
    target_index = (receiver + receive_vertex.reshape(count, count * RCAP)).reshape(-1).astype(jnp.int32)
    interface = jnp.zeros((3, count * FIV), jnp.float32).at[:, target_index].add(taken)
    interface = interface.reshape(3, count * GX, GZ)
    yrows = lax.broadcasted_iota(jnp.int32, mesh_before.shape, 2)
    start_field = jnp.where(yrows == 0, interface[:, :, None, :], mesh_before)
    return relax(relax(start_field))
```

```python
import math

import jax
import jax.numpy as jnp
from jax import lax
from jax.experimental import pallas as pl
from jax.experimental.pallas import tpu as pltpu
from jax.sharding import PartitionSpec as P

LANES = 128
SUB = 8
share = 0.8 / 6.0
keep = 0.2 / share
sharpness = 8.0
VMEM = pl.BlockSpec(memory_space=pltpu.VMEM)
ANY = pl.BlockSpec(memory_space=pl.ANY)
SMEM = pl.BlockSpec(memory_space=pltpu.SMEM)
f32 = jnp.float32
bf16 = jnp.bfloat16


def params(limit, **more):
    return pltpu.CompilerParams(vmem_limit_bytes=limit << 20, **more)


def lane_gather(row, lane):
    return jnp.take_along_axis(row, lane, axis=1, mode="promise_in_bounds")


def gather_rows(row_of, blocks, index_of, groups):
    index = [index_of(g) for g in range(groups)]
    high = [lax.shift_right_arithmetic(i, 7) for i in index]
    low = [jnp.bitwise_and(i, LANES - 1) for i in index]
    out = [[jnp.zeros((SUB, LANES), f32) for _ in range(3)] for _ in range(groups)]
    for block in range(blocks):
        rows = [jnp.broadcast_to(row_of(k, block), (SUB, LANES)) for k in range(3)]
        for g in range(groups):
            here = high[g] == block
            for k in range(3):
                out[g][k] = jnp.where(here, lane_gather(rows[k], low[g]), out[g][k])
    return out


def packed_place(k, row, per):
    return row // per, k * per + row % per


def store_rows(out_ref, g, values, per):
    for k in range(3):
        for s in range(SUB):
            row = g * SUB + s
            if per:
                d, r = packed_place(k, row, per)
                out_ref[d, r : r + 1, :] = values[k][s : s + 1, :]
            else:
                out_ref[k, row : row + 1, :] = values[k][s : s + 1, :]


def packed_row(ref, k, row, per):
    if per:
        d, r = packed_place(k, row, per)
        return ref[d, r : r + 1, :]
    return ref[k, row : row + 1, :]


def pick_body(table_ref, index_ref, out_ref, *, per):
    groups = index_ref.shape[0] // SUB
    blocks = table_ref.shape[1] // LANES
    half = max(1, groups // 2)
    for first in range(0, groups, half):
        got = gather_rows(
            lambda k, b: table_ref[k : k + 1, b * LANES : (b + 1) * LANES],
            blocks,
            lambda g: index_ref[(first + g) * SUB : (first + g + 1) * SUB, :],
            half,
        )
        for g in range(half):
            store_rows(out_ref, first + g, got[g], per)


def kernel_body(source_ref, target_ref, high_ref, low_ref, turned):
    clusters, _, points = source_ref.shape
    scale = math.sqrt(sharpness * math.log2(math.e))
    step = 16
    for c in range(clusters):
        rows = jnp.concatenate([source_ref[c] * scale, jnp.zeros((SUB - 3, points), f32)], axis=0)
        turned[...] = jnp.transpose(rows)
        goal = [target_ref[c, k : k + 1, :] * scale for k in range(3)]

        def body(i, _, c=c, goal=goal):
            at = pl.multiple_of(i * step, step)
            part = turned[pl.ds(at, step), :]
            gap = goal[0] - part[:, 0:1]
            spread = gap * gap
            gap = goal[1] - part[:, 1:2]
            spread = spread + gap * gap
            gap = goal[2] - part[:, 2:3]
            spread = spread + gap * gap
            value = jnp.exp2(-spread)
            high = value.astype(bf16)
            high_ref[c, pl.ds(at, step), :] = high
            low_ref[c, pl.ds(at, step), :] = (value - high.astype(f32)).astype(bf16)
            return 0

        lax.fori_loop(0, points // step, body, 0)


def result_body(
    arrived_ref, slot_ref, inverse_ref, high_ref, low_ref, weight_ref, pick_ref, out_ref, inverse, members, results, sems, *, per_in, per_out
):
    clusters, points = slot_ref.shape
    verts = weight_ref.shape[1]
    copies = [pltpu.make_async_copy(inverse_ref.at[c], inverse.at[c], sems.at[c]) for c in range(clusters)]
    for copy in copies:
        copy.start()
    fold = SUB // clusters
    groups = points // LANES // fold
    blocks = (arrived_ref.shape[0] * per_in) if per_in else arrived_ref.shape[1]
    got = gather_rows(
        lambda k, b: packed_row(arrived_ref, k, b, per_in),
        blocks,
        lambda g: jnp.concatenate(
            [slot_ref[:, (g * fold + j) * LANES : (g * fold + j + 1) * LANES] for j in range(fold)], axis=0
        ),
        groups,
    )
    members[...] = jnp.zeros(members.shape, f32)
    for g in range(groups):
        for j in range(fold):
            at = (g * fold + j) * LANES
            for c in range(clusters):
                for k in range(3):
                    s = j * clusters + c
                    members[c, k : k + 1, at : at + LANES] = got[g][k][s : s + 1, :]
    for c in range(clusters):
        copies[c].wait()
        mine = members[c]
        coupling = lax.dot_general(
            mine.astype(bf16), inverse[c], (((1,), (1,)), ((), ())), preferred_element_type=f32
        )
        coefficient = mine + coupling
        c_high = coefficient.astype(bf16)
        c_low = (coefficient - c_high.astype(f32)).astype(bf16)
        both = jnp.concatenate([c_high, c_low], axis=0)
        first = jnp.dot(both, high_ref[c], preferred_element_type=f32)
        second = jnp.dot(c_high, low_ref[c], preferred_element_type=f32)
        total = first[:SUB] + (first[SUB:] + second)
        results[c] = total * weight_ref[c : c + 1, :]
    per_cluster = verts // LANES
    groups = pick_ref.shape[0] // SUB
    half = max(1, groups // 2)
    for start in range(0, groups, half):
        got = gather_rows(
            lambda k, b: results[
                b // per_cluster, k : k + 1, (b % per_cluster) * LANES : (b % per_cluster + 1) * LANES
            ],
            clusters * per_cluster,
            lambda g: pick_ref[(start + g) * SUB : (start + g + 1) * SUB, :],
            half,
        )
        for g in range(half):
            store_rows(out_ref, start + g, got[g], per_out)


def mesh_body(edge_ref, mesh_ref, left_ref, right_ref, out_ref, field, swept, stage, in_sems, side_sems, out_sems, *, batch):
    comps, width, height, depth = mesh_ref.shape
    tiles = depth // LANES
    strips = height // SUB
    slots = stage.shape[0]

    def columns(j):
        return pl.ds(j * LANES, LANES)

    def load(k, b):
        found = []
        for j in range(tiles):
            found.append(
                pltpu.make_async_copy(
                    mesh_ref.at[k, pl.ds(b * batch, batch), :, columns(j)],
                    field.at[k, pl.ds(2 + b * batch, batch), j, pl.ds(SUB, height), :],
                    in_sems.at[k, b, j],
                )
            )
        return found

    def sides(k):
        found = []
        for j in range(tiles):
            for side, (ref, at) in enumerate(((left_ref, 0), (right_ref, 2 + width))):
                found.append(
                    pltpu.make_async_copy(
                        ref.at[k, :, :, columns(j)],
                        field.at[k, pl.ds(at, 2), j, pl.ds(SUB, height), :],
                        side_sems.at[k, j, side],
                    )
                )
        return found

    for k in range(comps):
        for copy in sides(k):
            copy.start()
        for b in range(width // batch):
            for copy in load(k, b):
                copy.start()

    blank = jnp.zeros((SUB, LANES), f32)
    for j in range(tiles):
        for x in range(width + 2):
            swept[x, j, SUB + height : 2 * SUB + height, :] = blank
        for x in range(width + 4):
            for k in range(comps):
                field[k, x, j, SUB + height : 2 * SUB + height, :] = blank

    lane = lax.broadcasted_iota(jnp.int32, (SUB, LANES), 1)
    row = lax.broadcasted_iota(jnp.int32, (SUB, LANES), 0)
    is_first = lane == 0
    is_last = lane == LANES - 1
    wall = row == 0
    above_wall = row == 1

    def sweep(center, before, after, put):
        for y in range(strips):
            at = SUB + y * SUB
            mid = [center[j, pl.ds(at, SUB), :] for j in range(tiles)]
            down = [pltpu.roll(m, 1, 1) for m in mid]
            up = [pltpu.roll(m, LANES - 1, 1) for m in mid]
            for j in range(tiles):
                lower = center[j, pl.ds(at - 1, SUB), :]
                if y == 0:
                    lower = jnp.where(row < 2, 0.0, lower)
                near = (before[j, pl.ds(at, SUB), :] + after[j, pl.ds(at, SUB), :]) + (
                    center[j, pl.ds(at + 1, SUB), :] + lower
                )
                back = jnp.where(is_first, down[j - 1] if j else 0.0, down[j])
                fore = jnp.where(is_last, up[j + 1] if j + 1 < tiles else 0.0, up[j])
                value = (near + (back + fore)) + keep * mid[j]
                if y == 0:
                    value = jnp.where(wall, 0.0, value)
                put(j, y, value)

    def first_sweep(k, x):
        def put(j, y, value):
            swept[x, j, pl.ds(SUB + y * SUB, SUB), :] = value

        sweep(field.at[k, x + 1], field.at[k, x], field.at[k, x + 2], put)

    def flush(k, x, slot):
        return pltpu.make_async_copy(stage.at[slot], out_ref.at[k, x], out_sems.at[slot])

    def component(k, _):
        for copy in sides(k):
            copy.wait()
        for copy in load(k, 0):
            copy.wait()
        first_sweep(k, 0)

        @pl.when(edge_ref[0] == 0)
        def _():
            swept[0] = jnp.zeros(swept.shape[1:], f32)

        first_sweep(k, 1)

        def step(x, _):
            @pl.when(jnp.logical_and((x + 1) % batch == 0, x + 1 < width))
            def _():
                for copy in load(k, (x + 1) // batch):
                    copy.wait()

            first_sweep(k, x + 2)

            @pl.when(jnp.logical_and(x + 2 == width + 1, edge_ref[1] == 0))
            def _():
                swept[width + 1] = jnp.zeros(swept.shape[1:], f32)

            turn = k * width + x
            slot = turn % slots

            @pl.when(turn >= slots)
            def _():
                flush(k, x, slot).wait()

            def put(j, y, value):
                stage[slot, y * SUB : (y + 1) * SUB, j * LANES : (j + 1) * LANES] = value * (share * share)

            sweep(swept.at[x + 1], swept.at[x], swept.at[x + 2], put)
            flush(k, x, slot).start()
            return 0

        lax.fori_loop(0, width, step, 0)
        return 0

    lax.fori_loop(0, comps, component, 0)
    for slot in range(slots):
        flush(0, 0, slot).wait()


def scatter_body(returned_ref, vertex_ref, inter_ref, left_ref, right_ref, rows_sc, ones_sc, *, per, width):
    rows, _ = vertex_ref.shape
    blocks = inter_ref.shape[1]
    tiles = blocks // width
    line = lax.broadcasted_iota(jnp.int32, (blocks, LANES), 0)
    home = (line % width) * tiles + line // width
    lane = lax.broadcasted_iota(jnp.int32, (LANES, LANES), 0)
    for row in range(rows):
        vertex = vertex_ref[row : row + 1, :]
        high = lax.shift_right_arithmetic(vertex, 7)
        low = jnp.bitwise_and(vertex, LANES - 1)
        span = slice(row * LANES, (row + 1) * LANES)
        ones_sc[:, span] = jnp.where(lane == low, 1.0, 0.0).astype(bf16)
        here = home == high
        for k in range(3):
            value = packed_row(returned_ref, k, row, per)
            part = value
            for piece in range(3):
                top = part.astype(bf16).astype(f32)
                at = (piece * 3 + k) * blocks
                rows_sc[at : at + blocks, span] = jnp.where(here, top, 0.0).astype(bf16)
                part = part - top
    total = lax.dot_general(
        rows_sc[...], ones_sc[...], (((1,), (1,)), ((), ())), preferred_element_type=f32
    )
    size = 3 * blocks
    total = total[:size] + (total[size : 2 * size] + total[2 * size :])
    for k in range(3):
        inter_ref[k] = total[k * blocks : (k + 1) * blocks]
        for j in range(tiles):
            at = k * blocks + j * width
            q = k * tiles + j
            left_ref[q : q + 1, :] = total[at : at + 1]
            right_ref[q : q + 1, :] = total[at + width - 1 : at + width]


def finish_body(base_ref, inter_ref, left_ref, right_ref, out_ref):
    k = pl.program_id(0)
    _, width, _, depth = base_ref.shape
    tiles = depth // LANES
    lane = lax.broadcasted_iota(jnp.int32, (width, LANES), 1)
    parts = [inter_ref[0, j * width : (j + 1) * width, :] for j in range(tiles)]
    down = [pltpu.roll(p, 1, 1) for p in parts]
    up = [pltpu.roll(p, LANES - 1, 1) for p in parts]
    line = lax.broadcasted_iota(jnp.int32, (width, LANES), 0)
    for j in range(tiles):
        mid = parts[j]
        back = jnp.where(lane == 0, down[j - 1] if j else 0.0, down[j])
        fore = jnp.where(lane == LANES - 1, up[j + 1] if j + 1 < tiles else 0.0, up[j])
        q = k * tiles + j
        prev = jnp.where(line == 0, left_ref[pl.ds(q, 1), :], pltpu.roll(mid, 1, 0))
        after = jnp.where(line == width - 1, right_ref[pl.ds(q, 1), :], pltpu.roll(mid, width - 1, 0))
        near = ((prev + after) + (back + fore)) * (share * share)
        one = mid * (1.2 * share) + near
        two = mid * (share * share)
        span = slice(j * LANES, (j + 1) * LANES)
        for x in range(width):
            base = base_ref[0, x, :, span]
            row = lax.broadcasted_iota(jnp.int32, base.shape, 0)
            add = jnp.where(row == 1, one[x : x + 1], jnp.where(row == 2, two[x : x + 1], 0.0))
            out_ref[0, x, :, span] = jnp.where(row == 0, mid[x : x + 1], base + add)


def exchange(packed, per, cap):
    if per:
        return lax.all_to_all(packed, "dev", split_axis=0, concat_axis=0, tiled=True)
    count = lax.axis_size("dev")
    split = packed.reshape(3, count, cap)
    moved = lax.all_to_all(split, "dev", split_axis=1, concat_axis=1, tiled=True)
    return moved.reshape(packed.shape)


def local(
    displacement,
    send_node,
    member_slot,
    inverse_part,
    source_coord,
    target_coord,
    unity_weight,
    result_pick,
    receive_vertex,
    mesh_before,
):
    count = lax.axis_size("dev")
    place = lax.axis_index("dev")
    send_cap = send_node.shape[0] // count
    result_cap = result_pick.shape[0] // count
    send_per = send_cap // LANES if send_cap % LANES == 0 else 0
    result_per = result_cap // LANES if result_cap % LANES == 0 else 0
    clusters, points = member_slot.shape
    verts = unity_weight.shape[1]
    comps, width, height, depth = mesh_before.shape
    tiles = depth // LANES
    blocks = width * tiles

    def packed_shape(per, size):
        shape = (count, 3 * per, LANES) if per else (3, size // LANES, LANES)
        return jax.ShapeDtypeStruct(shape, f32)

    up = [(i, i + 1) for i in range(count - 1)]
    down = [(i + 1, i) for i in range(count - 1)]

    outgoing = pl.pallas_call(
        lambda *refs: pick_body(*refs, per=send_per),
        out_shape=packed_shape(send_per, send_node.shape[0]),
        in_specs=[VMEM, VMEM],
        out_specs=VMEM,
        compiler_params=params(4),
        name="pick_nodes",
    )(displacement, send_node.reshape(-1, LANES))
    arrived = exchange(outgoing, send_per, send_cap)

    halo_left = lax.ppermute(mesh_before[:, width - 2 :], "dev", up)
    halo_right = lax.ppermute(mesh_before[:, :2], "dev", down)

    pair = jax.ShapeDtypeStruct((clusters, points, verts), bf16)
    kernel_high, kernel_low = pl.pallas_call(
        kernel_body,
        out_shape=(pair, pair),
        in_specs=[VMEM, VMEM],
        out_specs=(VMEM, VMEM),
        scratch_shapes=[pltpu.VMEM((points, SUB), f32)],
        compiler_params=params(24),
        name="rbf_matrix",
    )(source_coord, target_coord)

    outgoing_results = pl.pallas_call(
        lambda *refs: result_body(*refs, per_in=send_per, per_out=result_per),
        out_shape=packed_shape(result_per, result_pick.shape[0]),
        in_specs=[VMEM, VMEM, ANY, VMEM, VMEM, VMEM, VMEM],
        out_specs=VMEM,
        scratch_shapes=[
            pltpu.VMEM((clusters, points, points), bf16),
            pltpu.VMEM((clusters, SUB, points), f32),
            pltpu.VMEM((clusters, SUB, verts), f32),
            pltpu.SemaphoreType.DMA((clusters,)),
        ],
        compiler_params=params(40),
        name="cluster_results",
    )(arrived, member_slot, inverse_part, kernel_high, kernel_low, unity_weight, result_pick.reshape(-1, LANES))
    returned = exchange(outgoing_results, result_per, result_cap)

    edges = jnp.stack([place, count - 1 - place]).astype(jnp.int32)
    batch = 4 if width % 4 == 0 else 1
    slots = 4
    base = pl.pallas_call(
        lambda *refs: mesh_body(*refs, batch=batch),
        out_shape=jax.ShapeDtypeStruct(mesh_before.shape, f32),
        in_specs=[SMEM, ANY, ANY, ANY],
        out_specs=ANY,
        scratch_shapes=[
            pltpu.VMEM((comps, width + 4, tiles, height + 2 * SUB, LANES), f32),
            pltpu.VMEM((width + 2, tiles, height + 2 * SUB, LANES), f32),
            pltpu.VMEM((slots, height, depth), f32),
            pltpu.SemaphoreType.DMA((comps, width // batch, tiles)),
            pltpu.SemaphoreType.DMA((comps, tiles, 2)),
            pltpu.SemaphoreType.DMA((slots,)),
        ],
        compiler_params=params(32),
        name="sweeps",
    )(edges, mesh_before, halo_left, halo_right)

    slots_in = receive_vertex.shape[0]
    edge_shape = jax.ShapeDtypeStruct((3 * tiles, LANES), f32)
    interface, first, last = pl.pallas_call(
        lambda *refs: scatter_body(*refs, per=result_per, width=width),
        out_shape=(jax.ShapeDtypeStruct((3, blocks, LANES), f32), edge_shape, edge_shape),
        in_specs=[VMEM, VMEM],
        out_specs=(VMEM, VMEM, VMEM),
        scratch_shapes=[pltpu.VMEM((9 * blocks, slots_in), bf16), pltpu.VMEM((LANES, slots_in), bf16)],
        compiler_params=params(24),
        name="scatter",
    )(returned, receive_vertex.reshape(-1, LANES))

    from_left = lax.ppermute(last, "dev", up)
    from_right = lax.ppermute(first, "dev", down)

    wall = pl.BlockSpec((1, width, SUB, depth), lambda k: (k, 0, 0, 0))
    return pl.pallas_call(
        finish_body,
        out_shape=jax.ShapeDtypeStruct(mesh_before.shape, f32),
        grid=(comps,),
        in_specs=[wall, pl.BlockSpec((1, blocks, LANES), lambda k: (k, 0, 0)), VMEM, VMEM],
        out_specs=wall,
        input_output_aliases={0: 0},
        compiler_params=params(8),
        name="finish",
    )(base, interface, from_left, from_right)


def solution(mesh):
    in_specs = (
        P(None, "dev"),
        P("dev"),
        P("dev", None),
        P("dev", None, None),
        P("dev", None, None),
        P("dev", None, None),
        P("dev", None),
        P("dev"),
        P("dev"),
        P(None, "dev", None, None),
    )
    out_specs = P(None, "dev", None, None)
    return jax.shard_map(local, mesh=mesh, in_specs=in_specs, out_specs=out_specs, check_vma=False)
```

```python
import math

import jax
import jax.numpy as jnp
from jax import lax
from jax.experimental import pallas as pl
from jax.experimental.pallas import tpu as pltpu
from jax.sharding import PartitionSpec as P


LANES = 128
SUB = 8
share = 0.8 / 6.0
keep = 0.2 / share
sharpness = 8.0
AHEAD = 2
VMEM = pl.BlockSpec(memory_space=pltpu.VMEM)
ANY = pl.BlockSpec(memory_space=pl.ANY)
HBM = pl.BlockSpec(memory_space=pltpu.HBM)
SMEM = pl.BlockSpec(memory_space=pltpu.SMEM)
f32 = jnp.float32
bf16 = jnp.bfloat16


def in_hbm(value):
    return pltpu.with_memory_space_constraint(value, pltpu.HBM)


def params(limit, **more):
    return pltpu.CompilerParams(vmem_limit_bytes=limit << 20, **more)


def lane_gather(row, lane):
    return jnp.take_along_axis(row, lane, axis=1, mode="promise_in_bounds")


def gather_rows(row_of, blocks, index_of, groups):
    index = [index_of(g) for g in range(groups)]
    high = [lax.shift_right_arithmetic(i, 7) for i in index]
    low = [jnp.bitwise_and(i, LANES - 1) for i in index]
    out = [[jnp.zeros((SUB, LANES), f32) for _ in range(3)] for _ in range(groups)]
    for block in range(blocks):
        rows = [jnp.broadcast_to(row_of(k, block), (SUB, LANES)) for k in range(3)]
        for g in range(groups):
            here = high[g] == block
            for k in range(3):
                out[g][k] = jnp.where(here, lane_gather(rows[k], low[g]), out[g][k])
    return out


def packed_place(k, row, per):
    return row // per, k * per + row % per


def store_rows(out_ref, g, values, per):
    for k in range(3):
        for s in range(SUB):
            row = g * SUB + s
            if per:
                d, r = packed_place(k, row, per)
                out_ref[d, r : r + 1, :] = values[k][s : s + 1, :]
            else:
                out_ref[k, row : row + 1, :] = values[k][s : s + 1, :]


def packed_row(ref, k, row, per):
    if per:
        d, r = packed_place(k, row, per)
        return ref[d, r : r + 1, :]
    return ref[k, row : row + 1, :]


def pick_body(table_ref, index_ref, out_ref, *, per):
    groups = index_ref.shape[0] // SUB
    blocks = table_ref.shape[1] // LANES
    half = max(1, groups // 2)
    for first in range(0, groups, half):
        got = gather_rows(
            lambda k, b: table_ref[k : k + 1, b * LANES : (b + 1) * LANES],
            blocks,
            lambda g: index_ref[(first + g) * SUB : (first + g + 1) * SUB, :],
            half,
        )
        for g in range(half):
            store_rows(out_ref, first + g, got[g], per)


def pieces(value, count=3):
    found = []
    for _ in range(count):
        top = value.astype(bf16).astype(f32)
        found.append(top)
        value = value - top
    return found


def factor(points, target):
    square = points * points
    norm = jnp.broadcast_to(jnp.sum(square, axis=0, keepdims=True), square.shape)
    row = lax.broadcasted_iota(jnp.int32, square.shape, 0)
    a, b, c = pieces(norm)
    p, q, r = pieces(points)
    if target:
        edge = jnp.where(row < 3, -1.0, jnp.where(row == 3, -a, jnp.where(row == 4, -b, jnp.where(row == 5, -c, 0.0))))
        blocks = [2.0 * p, 2.0 * q, 2.0 * p, 2.0 * q, 2.0 * r, 2.0 * p, edge]
    else:
        edge = jnp.where(row == 0, a, jnp.where(row == 1, b, jnp.where(row == 2, c, jnp.where(row < 6, 1.0, 0.0))))
        blocks = [p, p, q, q, p, r, edge]
    blocks.append(jnp.zeros(square.shape, f32))
    return jnp.concatenate(blocks, axis=0)


def rbf_matrix(source, target, put):
    scale = math.sqrt(sharpness * math.log2(math.e))
    points = source[0].shape[1]
    step = LANES

    def centred(rows):
        blank = jnp.zeros((SUB - 3, rows[0].shape[1]), f32)
        return jnp.concatenate([(row - 0.5) * scale for row in rows] + [blank], axis=0)

    turned = jnp.transpose(factor(centred(source), False)).astype(bf16)
    right = factor(centred(target), True).astype(bf16)
    for at in range(0, points, step):
        value = jnp.exp2(jnp.dot(turned[at : at + step], right, preferred_element_type=f32))
        high = value.astype(bf16)
        put(at, step, high, (value - high.astype(f32)).astype(bf16))


def prepare_body(
    source_ref, target_ref, slot_ref, weight_ref, pick_ref, vertex_ref, mesh_ref,
    high_out, low_out, slot_out, weight_out, pick_out, vertex_out, source, target, head_out, tail_out,
    high, low, head, tail, sems, done,
):
    width = mesh_ref.shape[1]
    needed = [
        pltpu.make_async_copy(source_ref, source, sems.at[0]),
        pltpu.make_async_copy(target_ref, target, sems.at[1]),
    ]
    others = [
        pltpu.make_async_copy(slot_ref, slot_out, sems.at[4]),
        pltpu.make_async_copy(weight_ref, weight_out, sems.at[5]),
        pltpu.make_async_copy(pick_ref, pick_out, sems.at[6]),
        pltpu.make_async_copy(vertex_ref, vertex_out, sems.at[7]),
    ]
    side_in = [
        pltpu.make_async_copy(mesh_ref.at[:, pl.ds(0, 2)], head, sems.at[2]),
        pltpu.make_async_copy(mesh_ref.at[:, pl.ds(width - 2, 2)], tail, sems.at[3]),
    ]
    side_out = [
        pltpu.make_async_copy(head, head_out, sems.at[8]),
        pltpu.make_async_copy(tail, tail_out, sems.at[9]),
    ]
    for copy in needed + side_in + others:
        copy.start()
    for copy in needed:
        copy.wait()
    last = []
    for c in range(high_out.shape[0]):

        def put(at, step, upper, lower, c=c):
            high[c, at : at + step, :] = upper
            low[c, at : at + step, :] = lower

        rbf_matrix(*(tuple(ref[k, c : c + 1, :] for k in range(3)) for ref in (source, target)), put)
        last.append(pltpu.make_async_copy(high.at[c], high_out.at[c], done.at[0, c]))
        last.append(pltpu.make_async_copy(low.at[c], low_out.at[c], done.at[1, c]))
        for copy in last[-2:]:
            copy.start()
        if c == 0:
            for before, after in zip(side_in, side_out):
                before.wait()
                after.start()
    for copy in others + last + side_out:
        copy.wait()


def result_body(
    arrived_ref, slot_ref, source_ref, target_ref, inverse_ref, high_ref, low_ref, weight_ref, pick_ref,
    out_ref, inverse, high, low, members, results, sems, *, per_in, per_out, ahead,
):
    clusters, points = slot_ref.shape
    verts = weight_ref.shape[1]
    blocks = (arrived_ref.shape[0] * per_in) if per_in else arrived_ref.shape[1]
    per_cluster = verts // LANES
    groups = pick_ref.shape[0] // SUB
    fold = points // LANES // SUB
    order = list(range(ahead, clusters)) + list(range(ahead))
    copies = {}
    for c in order:
        copies[c] = [pltpu.make_async_copy(inverse_ref.at[c], inverse.at[c], sems.at[0, c])]
        if c < ahead:
            copies[c].append(pltpu.make_async_copy(high_ref.at[c], high.at[c], sems.at[1, c]))
            copies[c].append(pltpu.make_async_copy(low_ref.at[c], low.at[c], sems.at[2, c]))
        for copy in copies[c]:
            copy.start()
    members[...] = jnp.zeros(members.shape, f32)

    def gather_members(c):
        got = gather_rows(
            lambda k, b: packed_row(arrived_ref, k, b, per_in),
            blocks,
            lambda g: jnp.concatenate(
                [slot_ref[c : c + 1, (g * SUB + j) * LANES : (g * SUB + j + 1) * LANES] for j in range(SUB)], axis=0
            ),
            fold,
        )
        for g in range(fold):
            for j in range(SUB):
                at = (g * SUB + j) * LANES
                for k in range(3):
                    members[c, k : k + 1, at : at + LANES] = got[g][k][j : j + 1, :]

    def evaluate(c):
        mine = members[c]
        for copy in copies[c]:
            copy.wait()
        coupling = lax.dot_general(
            mine.astype(bf16), inverse[c], (((1,), (1,)), ((), ())), preferred_element_type=f32
        )
        coefficient = mine + coupling
        c_high = coefficient.astype(bf16)
        c_low = (coefficient - c_high.astype(f32)).astype(bf16)
        both = jnp.concatenate([c_high, c_low], axis=0)
        first = jnp.dot(both, high[c], preferred_element_type=f32)
        second = jnp.dot(c_high, low[c], preferred_element_type=f32)
        total = first[:SUB] + (first[SUB:] + second)
        results[c] = total * weight_ref[c : c + 1, :]

    for c in order:
        if c >= ahead:

            def put(at, step, upper, lower, c=c):
                high[c, at : at + step, :] = upper
                low[c, at : at + step, :] = lower

            rbf_matrix(*(tuple(ref[k, c : c + 1, :] for k in range(3)) for ref in (source_ref, target_ref)), put)
        gather_members(c)
        evaluate(c)
    half = max(1, groups // 2)
    for start in range(0, groups, half):
        got = gather_rows(
            lambda k, b: results[
                b // per_cluster, k : k + 1, (b % per_cluster) * LANES : (b % per_cluster + 1) * LANES
            ],
            clusters * per_cluster,
            lambda g: pick_ref[(start + g) * SUB : (start + g + 1) * SUB, :],
            half,
        )
        for g in range(half):
            store_rows(out_ref, start + g, got[g], per_out)


def mesh_body(_, edge_ref, mesh_ref, left_ref, right_ref, out_ref, field, ring, stage, in_sems, side_sems, out_sems, *, batch):
    comps, width, height, depth = mesh_ref.shape
    tiles = depth // LANES
    strips = height // SUB
    slots = len(stage)
    turns = len(ring)

    def columns(j):
        return pl.ds(j * LANES, LANES)

    def load(k, b):
        found = []
        for j in range(tiles):
            found.append(
                pltpu.make_async_copy(
                    mesh_ref.at[k, pl.ds(b * batch, batch), :, columns(j)],
                    field.at[k, pl.ds(2 + b * batch, batch), j, pl.ds(SUB, height), :],
                    in_sems.at[k, b, j],
                )
            )
        return found

    def sides(k):
        found = []
        for j in range(tiles):
            for side, (ref, at) in enumerate(((left_ref, 0), (right_ref, 2 + width))):
                found.append(
                    pltpu.make_async_copy(
                        ref.at[k, :, :, columns(j)],
                        field.at[k, pl.ds(at, 2), j, pl.ds(SUB, height), :],
                        side_sems.at[k, j, side],
                    )
                )
        return found

    for k in range(comps):
        for copy in sides(k):
            copy.start()
        for b in range(width // batch):
            for copy in load(k, b):
                copy.start()

    blank = jnp.zeros((SUB, LANES), f32)
    for j in range(tiles):
        for plane in ring:
            plane[j, SUB + height : 2 * SUB + height, :] = blank

    def clear(i, _):
        for j in range(tiles):
            field[i // (width + 4), i % (width + 4), j, SUB + height : 2 * SUB + height, :] = blank
        return 0

    lax.fori_loop(0, comps * (width + 4), clear, 0)

    lane = lax.broadcasted_iota(jnp.int32, (SUB, LANES), 1)
    row = lax.broadcasted_iota(jnp.int32, (SUB, LANES), 0)
    is_first = lane == 0
    is_last = lane == LANES - 1
    wall = row == 0

    def sweep_strip(y, center, before, after, put):
        at = SUB + y * SUB
        mid = [center[j, pl.ds(at, SUB), :] for j in range(tiles)]
        down = [pltpu.roll(m, 1, 1) for m in mid]
        up = [pltpu.roll(m, LANES - 1, 1) for m in mid]
        for j in range(tiles):
            lower = center[j, pl.ds(at - 1, SUB), :]
            if y == 0:
                lower = jnp.where(row < 2, 0.0, lower)
            near = (before[j, pl.ds(at, SUB), :] + after[j, pl.ds(at, SUB), :]) + (
                center[j, pl.ds(at + 1, SUB), :] + lower
            )
            near = near + keep * mid[j]
            back = jnp.where(is_first, down[j - 1] if j else 0.0, down[j])
            fore = jnp.where(is_last, up[j + 1] if j + 1 < tiles else 0.0, up[j])
            value = near + (back + fore)
            if y == 0:
                value = jnp.where(wall, 0.0, value)
            put(j, y, value)

    def flush(k, x, slot):
        return pltpu.make_async_copy(stage[slot], out_ref.at[k, x], out_sems.at[slot])

    def work(k, x, phase, second):
        def put_first(j, y, value):
            ring[phase % turns][j, pl.ds(SUB + y * SUB, SUB), :] = value

        def put_second(j, y, value):
            stage[phase % slots][y * SUB : (y + 1) * SUB, j * LANES : (j + 1) * LANES] = value * (share * share)

        for y in range(strips):
            sweep_strip(y, field.at[k, x + 1], field.at[k, x], field.at[k, x + 2], put_first)
            if second:
                sweep_strip(
                    y,
                    ring[(phase - 2) % turns],
                    ring[(phase - 3) % turns],
                    ring[(phase - 1) % turns],
                    put_second,
                )

    def zero(place):
        ring[place % turns][...] = jnp.zeros(ring[0].shape, f32)

    def component(k, _):
        for copy in sides(k):
            copy.wait()
        for copy in load(k, 0):
            copy.wait()
        for phase in range(3):
            work(k, phase, phase, False)
            if phase == 0:

                @pl.when(edge_ref[0] == 0)
                def _():
                    zero(0)

        def quad(i, _):
            for sub in range(turns):
                x = i * turns + sub + 3
                phase = sub + 3

                if phase % batch == 0:

                    @pl.when(x < width)
                    def _():
                        for copy in load(k, x // batch):
                            copy.wait()

                slot = phase % slots

                @pl.when(k * width + i * turns + sub >= slots)
                def _():
                    flush(k, 0, slot).wait()

                work(k, jnp.minimum(x, width + 1), phase, True)
                if sub == turns - 2:

                    @pl.when(jnp.logical_and(x == width + 1, edge_ref[1] == 0))
                    def _():
                        zero(phase)

                flush(k, i * turns + sub, slot).start()
            return 0

        lax.fori_loop(0, width // turns, quad, 0)
        return 0

    lax.fori_loop(0, comps, component, 0)
    for slot in range(slots):
        flush(0, 0, slot).wait()


def scatter_body(_, returned_ref, vertex_ref, inter_ref, left_ref, right_ref, rows_sc, ones_sc, *, per, width):
    rows, _ = vertex_ref.shape
    blocks = inter_ref.shape[1]
    tiles = blocks // width
    line = lax.broadcasted_iota(jnp.int32, (blocks, LANES), 0)
    home = (line % width) * tiles + line // width
    lane = lax.broadcasted_iota(jnp.int32, (LANES, LANES), 0)
    for row in range(rows):
        vertex = vertex_ref[row : row + 1, :]
        high = lax.shift_right_arithmetic(vertex, 7)
        low = jnp.bitwise_and(vertex, LANES - 1)
        span = slice(row * LANES, (row + 1) * LANES)
        ones_sc[:, span] = jnp.where(lane == low, 1.0, 0.0).astype(bf16)
        here = home == high
        for k in range(3):
            value = packed_row(returned_ref, k, row, per)
            part = value
            for piece in range(3):
                top = part.astype(bf16).astype(f32)
                at = (piece * 3 + k) * blocks
                rows_sc[at : at + blocks, span] = jnp.where(here, top, 0.0).astype(bf16)
                part = part - top
    total = lax.dot_general(
        rows_sc[...], ones_sc[...], (((1,), (1,)), ((), ())), preferred_element_type=f32
    )
    size = 3 * blocks
    total = total[:size] + (total[size : 2 * size] + total[2 * size :])
    for k in range(3):
        inter_ref[k] = total[k * blocks : (k + 1) * blocks]
        for j in range(tiles):
            at = k * blocks + j * width
            q = k * tiles + j
            left_ref[q : q + 1, :] = total[at : at + 1]
            right_ref[q : q + 1, :] = total[at + width - 1 : at + width]


def finish_body(base_ref, inter_ref, left_ref, right_ref, out_ref):
    k = pl.program_id(0)
    _, width, _, depth = base_ref.shape
    tiles = depth // LANES
    lane = lax.broadcasted_iota(jnp.int32, (width, LANES), 1)
    parts = [inter_ref[0, j * width : (j + 1) * width, :] for j in range(tiles)]
    down = [pltpu.roll(p, 1, 1) for p in parts]
    up = [pltpu.roll(p, LANES - 1, 1) for p in parts]
    line = lax.broadcasted_iota(jnp.int32, (width, LANES), 0)
    for j in range(tiles):
        mid = parts[j]
        back = jnp.where(lane == 0, down[j - 1] if j else 0.0, down[j])
        fore = jnp.where(lane == LANES - 1, up[j + 1] if j + 1 < tiles else 0.0, up[j])
        q = k * tiles + j
        prev = jnp.where(line == 0, left_ref[pl.ds(q, 1), :], pltpu.roll(mid, 1, 0))
        after = jnp.where(line == width - 1, right_ref[pl.ds(q, 1), :], pltpu.roll(mid, width - 1, 0))
        near = ((prev + after) + (back + fore)) * (share * share)
        one = mid * (1.2 * share) + near
        two = mid * (share * share)
        span = slice(j * LANES, (j + 1) * LANES)
        for x in range(width):
            base = base_ref[0, x, :, span]
            row = lax.broadcasted_iota(jnp.int32, base.shape, 0)
            add = jnp.where(row == 1, one[x : x + 1], jnp.where(row == 2, two[x : x + 1], 0.0))
            out_ref[0, x, :, span] = jnp.where(row == 0, mid[x : x + 1], base + add)


def exchange(packed, per, cap):
    if per:
        return lax.all_to_all(packed, "dev", split_axis=0, concat_axis=0, tiled=True)
    count = lax.axis_size("dev")
    split = packed.reshape(3, count, cap)
    moved = lax.all_to_all(split, "dev", split_axis=1, concat_axis=1, tiled=True)
    return moved.reshape(packed.shape)


def local(
    displacement,
    send_node,
    member_slot,
    inverse_part,
    source_coord,
    target_coord,
    unity_weight,
    result_pick,
    receive_vertex,
    mesh_before,
):
    count = lax.axis_size("dev")
    place = lax.axis_index("dev")
    send_cap = send_node.shape[0] // count
    result_cap = result_pick.shape[0] // count
    send_per = send_cap // LANES if send_cap % LANES == 0 else 0
    result_per = result_cap // LANES if result_cap % LANES == 0 else 0
    clusters, points = member_slot.shape
    verts = unity_weight.shape[1]
    comps, width, height, depth = mesh_before.shape
    tiles = depth // LANES
    blocks = width * tiles

    def packed_shape(per, size):
        shape = (count, 3 * per, LANES) if per else (3, size // LANES, LANES)
        return jax.ShapeDtypeStruct(shape, f32)

    up = [(i, i + 1) for i in range(count - 1)]
    down = [(i + 1, i) for i in range(count - 1)]

    field = in_hbm(mesh_before)
    outgoing = pl.pallas_call(
        lambda *refs: pick_body(*refs, per=send_per),
        out_shape=packed_shape(send_per, send_node.shape[0]),
        in_specs=[VMEM, VMEM],
        out_specs=VMEM,
        compiler_params=params(2),
        name="pick_nodes",
    )(displacement, send_node.reshape(-1, LANES))
    arrived = exchange(outgoing, send_per, send_cap)

    pair = jax.ShapeDtypeStruct((clusters, points, verts), bf16)
    ahead = min(clusters, AHEAD)
    pair = pltpu.HBM((ahead, points, verts), bf16)
    side = pltpu.HBM((comps, 2, height, depth), f32)
    source_turned = jnp.transpose(source_coord, (1, 0, 2))
    target_turned = jnp.transpose(target_coord, (1, 0, 2))
    small = (member_slot, unity_weight, result_pick.reshape(-1, LANES), receive_vertex.reshape(-1, LANES))
    (kernel_high, kernel_low, slots, weight, picks, vertices, source, target, head, tail) = pl.pallas_call(
        prepare_body,
        out_shape=(pair, pair)
        + tuple(pltpu.VMEM(x.shape, x.dtype) for x in small + (source_turned, target_turned))
        + (side, side),
        in_specs=[HBM] * 7,
        out_specs=(HBM,) * 2 + (VMEM,) * 6 + (HBM,) * 2,
        scratch_shapes=[
            pltpu.VMEM((ahead, points, verts), bf16),
            pltpu.VMEM((ahead, points, verts), bf16),
            pltpu.VMEM((comps, 2, height, depth), f32),
            pltpu.VMEM((comps, 2, height, depth), f32),
            pltpu.SemaphoreType.DMA((10,)),
            pltpu.SemaphoreType.DMA((2, ahead)),
        ],
        compiler_params=params(28),
        name="prepare",
    )(*map(in_hbm, (source_turned, target_turned) + small), field)
    halo_left = lax.ppermute(tail, "dev", up)
    halo_right = lax.ppermute(head, "dev", down)

    outgoing_results = pl.pallas_call(
        lambda *refs: result_body(*refs, per_in=send_per, per_out=result_per, ahead=ahead),
        out_shape=packed_shape(result_per, result_pick.shape[0]),
        in_specs=[VMEM] * 4 + [HBM] * 3 + [VMEM] * 2,
        out_specs=VMEM,
        scratch_shapes=[
            pltpu.VMEM(inverse_part.shape, bf16),
            pltpu.VMEM((clusters, points, verts), bf16),
            pltpu.VMEM((clusters, points, verts), bf16),
            pltpu.VMEM((clusters, SUB, points), f32),
            pltpu.VMEM((clusters, SUB, verts), f32),
            pltpu.SemaphoreType.DMA((3, clusters)),
        ],
        compiler_params=params(40),
        name="cluster_results",
    )(arrived, slots, source, target, in_hbm(inverse_part), in_hbm(kernel_high), in_hbm(kernel_low), weight, picks)
    returned = exchange(outgoing_results, result_per, result_cap)

    edges = jnp.stack([place, count - 1 - place]).astype(jnp.int32)
    batch = turns = 4
    if width % turns:
        raise ValueError("width")
    base = pl.pallas_call(
        lambda *refs: mesh_body(*refs, batch=batch),
        out_shape=jax.ShapeDtypeStruct(mesh_before.shape, f32),
        in_specs=[ANY, SMEM, HBM, ANY, ANY],
        out_specs=HBM,
        scratch_shapes=[
            pltpu.VMEM((comps, width + 4, tiles, height + 2 * SUB, LANES), f32),
            tuple(pltpu.VMEM((tiles, height + 2 * SUB, LANES), f32) for _ in range(turns)),
            tuple(pltpu.VMEM((height, depth), f32) for _ in range(turns)),
            pltpu.SemaphoreType.DMA((comps, width // batch, tiles)),
            pltpu.SemaphoreType.DMA((comps, tiles, 2)),
            pltpu.SemaphoreType.DMA((turns,)),
        ],
        compiler_params=params(24),
        name="sweeps",
    )(outgoing_results, edges, field, halo_left, halo_right)

    slots_in = receive_vertex.shape[0]
    edge_shape = jax.ShapeDtypeStruct((3 * tiles, LANES), f32)
    interface, first, last = pl.pallas_call(
        lambda *refs: scatter_body(*refs, per=result_per, width=width),
        out_shape=(jax.ShapeDtypeStruct((3, blocks, LANES), f32), edge_shape, edge_shape),
        in_specs=[HBM, VMEM, VMEM],
        out_specs=(VMEM, VMEM, VMEM),
        scratch_shapes=[pltpu.VMEM((9 * blocks, slots_in), bf16), pltpu.VMEM((LANES, slots_in), bf16)],
        compiler_params=params(16),
        name="scatter",
    )(in_hbm(base), returned, vertices)

    from_left = lax.ppermute(last, "dev", up)
    from_right = lax.ppermute(first, "dev", down)

    wall = pl.BlockSpec((1, width, SUB, depth), lambda k: (k, 0, 0, 0))
    return pl.pallas_call(
        finish_body,
        out_shape=jax.ShapeDtypeStruct(mesh_before.shape, f32),
        grid=(comps,),
        in_specs=[wall, pl.BlockSpec((1, blocks, LANES), lambda k: (k, 0, 0)), VMEM, VMEM],
        out_specs=wall,
        input_output_aliases={0: 0},
        compiler_params=params(8),
        name="finish",
    )(base, interface, from_left, from_right)


def solution(mesh):
    in_specs = (
        P(None, "dev"),
        P("dev"),
        P("dev", None),
        P("dev", None, None),
        P("dev", None, None),
        P("dev", None, None),
        P("dev", None),
        P("dev"),
        P("dev"),
        P(None, "dev", None, None),
    )
    out_specs = P(None, "dev", None, None)

    return jax.shard_map(local, mesh=mesh, in_specs=in_specs, out_specs=out_specs, check_vma=False)
```

```python
import math

import jax
import jax.numpy as jnp
from jax import lax
from jax.experimental import pallas as pl
from jax.experimental.pallas import tpu as pltpu
from jax.sharding import PartitionSpec as P


LANES = 128
SUB = 8
TALL = 16
WIDE = 256
share = 0.8 / 6.0
keep = 0.2 / share
sharpness = 8.0
AHEAD = 2
VMEM = pl.BlockSpec(memory_space=pltpu.VMEM)
ANY = pl.BlockSpec(memory_space=pl.ANY)
HBM = pl.BlockSpec(memory_space=pltpu.HBM)
SMEM = pl.BlockSpec(memory_space=pltpu.SMEM)
f32 = jnp.float32
bf16 = jnp.bfloat16


def in_hbm(value):
    return pltpu.with_memory_space_constraint(value, pltpu.HBM)


def params(limit, **more):
    return pltpu.CompilerParams(vmem_limit_bytes=limit << 20, **more)


def lane_gather(row, lane):
    return jnp.take_along_axis(row, lane, axis=1, mode="promise_in_bounds")


def gather_rows(row_of, blocks, index_of, groups):
    index = [index_of(g) for g in range(groups)]
    high = [lax.shift_right_arithmetic(i, 7) for i in index]
    low = [jnp.bitwise_and(i, LANES - 1) for i in index]
    out = [[jnp.zeros((SUB, LANES), f32) for _ in range(3)] for _ in range(groups)]
    for block in range(blocks):
        rows = [jnp.broadcast_to(row_of(k, block), (SUB, LANES)) for k in range(3)]
        for g in range(groups):
            here = high[g] == block
            for k in range(3):
                out[g][k] = jnp.where(here, lane_gather(rows[k], low[g]), out[g][k])
    return out


def packed_place(k, row, per):
    return row // per, k * per + row % per


def store_rows(out_ref, g, values, per):
    for k in range(3):
        for s in range(SUB):
            row = g * SUB + s
            if per:
                d, r = packed_place(k, row, per)
                out_ref[d, r : r + 1, :] = values[k][s : s + 1, :]
            else:
                out_ref[k, row : row + 1, :] = values[k][s : s + 1, :]


def packed_row(ref, k, row, per):
    if per:
        d, r = packed_place(k, row, per)
        return ref[d, r : r + 1, :]
    return ref[k, row : row + 1, :]


def pick_body(table_hbm, index_hbm, mesh_ref, out_ref, head_out, tail_out, table_ref, index_ref, head, tail, sems, *, per):
    width = mesh_ref.shape[1]
    needed = [
        pltpu.make_async_copy(index_hbm, index_ref, sems.at[0]),
        pltpu.make_async_copy(table_hbm, table_ref, sems.at[1]),
    ]
    side_in = [
        pltpu.make_async_copy(mesh_ref.at[:, pl.ds(0, 2)], head, sems.at[2]),
        pltpu.make_async_copy(mesh_ref.at[:, pl.ds(width - 2, 2)], tail, sems.at[3]),
    ]
    side_out = [
        pltpu.make_async_copy(head, head_out, sems.at[4]),
        pltpu.make_async_copy(tail, tail_out, sems.at[5]),
    ]
    for copy in needed + side_in:
        copy.start()
    for copy in needed:
        copy.wait()
    groups = index_ref.shape[0] // SUB
    blocks = table_ref.shape[1] // LANES
    half = max(1, groups // 2)
    for first in range(0, groups, half):
        got = gather_rows(
            lambda k, b: table_ref[k : k + 1, b * LANES : (b + 1) * LANES],
            blocks,
            lambda g: index_ref[(first + g) * SUB : (first + g + 1) * SUB, :],
            half,
        )
        for g in range(half):
            store_rows(out_ref, first + g, got[g], per)
        if first == 0:
            for before, after in zip(side_in, side_out):
                before.wait()
                after.start()
    for copy in side_out:
        copy.wait()


def pieces(value, count=3):
    found = []
    for _ in range(count):
        top = value.astype(bf16).astype(f32)
        found.append(top)
        value = value - top
    return found


def factor(points, target):
    square = points * points
    norm = jnp.broadcast_to(jnp.sum(square, axis=0, keepdims=True), square.shape)
    row = lax.broadcasted_iota(jnp.int32, square.shape, 0)
    a, b, c = pieces(norm)
    p, q, r = pieces(points)
    if target:
        edge = jnp.where(row < 3, -1.0, jnp.where(row == 3, -a, jnp.where(row == 4, -b, jnp.where(row == 5, -c, 0.0))))
        blocks = [2.0 * p, 2.0 * q, 2.0 * p, 2.0 * q, 2.0 * r, 2.0 * p, edge]
    else:
        edge = jnp.where(row == 0, a, jnp.where(row == 1, b, jnp.where(row == 2, c, jnp.where(row < 6, 1.0, 0.0))))
        blocks = [p, p, q, q, p, r, edge]
    blocks.append(jnp.zeros(square.shape, f32))
    return jnp.concatenate(blocks, axis=0)


def rbf_matrix(source, target, put):
    scale = math.sqrt(sharpness * math.log2(math.e))
    points = source[0].shape[1]
    step = LANES

    def centred(rows):
        blank = jnp.zeros((SUB - 3, rows[0].shape[1]), f32)
        return jnp.concatenate([(row - 0.5) * scale for row in rows] + [blank], axis=0)

    turned = jnp.transpose(factor(centred(source), False)).astype(bf16)
    right = factor(centred(target), True).astype(bf16)
    for at in range(0, points, step):
        value = jnp.exp2(jnp.dot(turned[at : at + step], right, preferred_element_type=f32))
        high = value.astype(bf16)
        put(at, step, high, (value - high.astype(f32)).astype(bf16))


def prepare_body(
    source_ref, target_ref, slot_ref, weight_ref, pick_ref, vertex_ref,
    high_out, low_out, slot_out, weight_out, pick_out, vertex_out, source, target, high, low, sems, done,
):
    needed = [
        pltpu.make_async_copy(source_ref, source, sems.at[0]),
        pltpu.make_async_copy(target_ref, target, sems.at[1]),
    ]
    others = [
        pltpu.make_async_copy(slot_ref, slot_out, sems.at[2]),
        pltpu.make_async_copy(weight_ref, weight_out, sems.at[3]),
        pltpu.make_async_copy(pick_ref, pick_out, sems.at[4]),
        pltpu.make_async_copy(vertex_ref, vertex_out, sems.at[5]),
    ]
    for copy in needed + others:
        copy.start()
    for copy in needed:
        copy.wait()
    last = []
    for c in range(high_out.shape[0]):

        def put(at, step, upper, lower, c=c):
            high[c, at : at + step, :] = upper
            low[c, at : at + step, :] = lower

        rbf_matrix(*(tuple(ref[k, c : c + 1, :] for k in range(3)) for ref in (source, target)), put)
        last.append(pltpu.make_async_copy(high.at[c], high_out.at[c], done.at[0, c]))
        last.append(pltpu.make_async_copy(low.at[c], low_out.at[c], done.at[1, c]))
        for copy in last[-2:]:
            copy.start()
    for copy in others + last:
        copy.wait()


def result_body(
    arrived_ref, slot_ref, source_ref, target_ref, inverse_ref, high_ref, low_ref, weight_ref, pick_ref,
    out_ref, inverse, high, low, members, results, sems, *, per_in, per_out, ahead,
):
    clusters, points = slot_ref.shape
    verts = weight_ref.shape[1]
    blocks = (arrived_ref.shape[0] * per_in) if per_in else arrived_ref.shape[1]
    per_cluster = verts // LANES
    groups = pick_ref.shape[0] // SUB
    fold = points // LANES // SUB
    order = list(range(ahead, clusters)) + list(range(ahead))
    copies = {}
    for c in order:
        copies[c] = [pltpu.make_async_copy(inverse_ref.at[c], inverse.at[c], sems.at[0, c])]
        if c < ahead:
            copies[c].append(pltpu.make_async_copy(high_ref.at[c], high.at[c], sems.at[1, c]))
            copies[c].append(pltpu.make_async_copy(low_ref.at[c], low.at[c], sems.at[2, c]))
        for copy in copies[c]:
            copy.start()
    members[...] = jnp.zeros(members.shape, f32)

    def gather_members(c):
        got = gather_rows(
            lambda k, b: packed_row(arrived_ref, k, b, per_in),
            blocks,
            lambda g: jnp.concatenate(
                [slot_ref[c : c + 1, (g * SUB + j) * LANES : (g * SUB + j + 1) * LANES] for j in range(SUB)], axis=0
            ),
            fold,
        )
        for g in range(fold):
            for j in range(SUB):
                at = (g * SUB + j) * LANES
                for k in range(3):
                    members[c, k : k + 1, at : at + LANES] = got[g][k][j : j + 1, :]

    def evaluate(c):
        mine = members[c]
        for copy in copies[c]:
            copy.wait()
        coupling = lax.dot_general(
            mine.astype(bf16), inverse[c], (((1,), (1,)), ((), ())), preferred_element_type=f32
        )
        coefficient = mine + coupling
        c_high = coefficient.astype(bf16)
        c_low = (coefficient - c_high.astype(f32)).astype(bf16)
        both = jnp.concatenate([c_high, c_low], axis=0)
        first = jnp.dot(both, high[c], preferred_element_type=f32)
        second = jnp.dot(c_high, low[c], preferred_element_type=f32)
        total = first[:SUB] + (first[SUB:] + second)
        results[c] = total * weight_ref[c : c + 1, :]

    for c in order:
        if c >= ahead:

            def put(at, step, upper, lower, c=c):
                high[c, at : at + step, :] = upper
                low[c, at : at + step, :] = lower

            rbf_matrix(*(tuple(ref[k, c : c + 1, :] for k in range(3)) for ref in (source_ref, target_ref)), put)
        gather_members(c)
        evaluate(c)
    half = max(1, groups // 2)
    for start in range(0, groups, half):
        got = gather_rows(
            lambda k, b: results[
                b // per_cluster, k : k + 1, (b % per_cluster) * LANES : (b % per_cluster + 1) * LANES
            ],
            clusters * per_cluster,
            lambda g: pick_ref[(start + g) * SUB : (start + g + 1) * SUB, :],
            half,
        )
        for g in range(half):
            store_rows(out_ref, start + g, got[g], per_out)


def mesh_body(_, edge_ref, mesh_ref, left_ref, right_ref, out_ref, field, ring, stage, in_sems, side_sems, out_sems, sums, *, batch):
    comps, width, height, depth = mesh_ref.shape
    tiles = depth // LANES
    strips = height // TALL
    share_tiles = WIDE // LANES
    units = len(sums)
    halves = depth // WIDE // units
    turns = len(ring)

    def columns(j):
        return pl.ds(j * LANES, LANES)

    def load(k, b):
        found = []
        for j in range(tiles):
            found.append(
                pltpu.make_async_copy(
                    mesh_ref.at[k, pl.ds(b * batch, batch), :, columns(j)],
                    field.at[k, pl.ds(2 + b * batch, batch), j, pl.ds(SUB, height), :],
                    in_sems.at[k, b, j],
                )
            )
        return found

    def sides(k):
        found = []
        for j in range(tiles):
            for side, (ref, at) in enumerate(((left_ref, 0), (right_ref, 2 + width))):
                found.append(
                    pltpu.make_async_copy(
                        ref.at[k, :, :, columns(j)],
                        field.at[k, pl.ds(at, 2), j, pl.ds(SUB, height), :],
                        side_sems.at[k, j, side],
                    )
                )
        return found

    for k in range(comps):
        for copy in sides(k):
            copy.start()
        for b in range(width // batch):
            for copy in load(k, b):
                copy.start()

    blank = jnp.zeros((SUB, LANES), f32)
    for j in range(tiles):
        for plane in ring:
            plane[j, SUB + height : 2 * SUB + height, :] = blank

    def clear(i, _):
        for j in range(tiles):
            field[i // (width + 4), i % (width + 4), j, SUB + height : 2 * SUB + height, :] = blank
        return 0

    lax.fori_loop(0, comps * (width + 4), clear, 0)

    lane = lax.broadcasted_iota(jnp.int32, (TALL, LANES), 1)
    row = lax.broadcasted_iota(jnp.int32, (TALL, LANES), 0)
    is_first = lane == 0
    is_last = lane == LANES - 1

    def terms(center, y, h):
        value = jnp.concatenate(
            [center[j, pl.ds(SUB + y * TALL, TALL), :] for j in range(h * share_tiles, (h + 1) * share_tiles)], axis=1
        )
        high = value.astype(bf16)
        return high, (value - high.astype(f32)).astype(bf16)

    def multiply(jobs):
        later = []
        for center, y, place in jobs:
            for h in range(depth // WIDE):
                high, low = terms(center, y, h)
                total = sums[h % units][place * halves + h // units]
                pltpu.matmul_acc_lhs(total, high)
                later.append((total, low))
        for total, low in later:
            pltpu.matmul_acc_lhs(total, low)

    def complete(center, before, after, y, place, put):
        at = SUB + y * TALL
        beside = []
        for h in range(depth // WIDE):
            beside.append(pltpu.matmul_pop(sums[h % units][place * halves + h // units]))
        for j in range(tiles):
            lower = center[j, pl.ds(at - 1, TALL), :]
            if y == 0:
                lower = jnp.where(row < 2, 0.0, lower)
            near = (before[j, pl.ds(at, TALL), :] + after[j, pl.ds(at, TALL), :]) + (
                center[j, pl.ds(at + 1, TALL), :] + lower
            )
            h, part = j // share_tiles, j % share_tiles
            value = near + beside[h][:, part * LANES : (part + 1) * LANES]
            if part == 0 and h:
                value = value + jnp.where(is_first, pltpu.roll(center[j - 1, pl.ds(at, TALL), :], 1, 1), 0.0)
            if part == share_tiles - 1 and j + 1 < tiles:
                value = value + jnp.where(is_last, pltpu.roll(center[j + 1, pl.ds(at, TALL), :], LANES - 1, 1), 0.0)
            if y == 0:
                value = jnp.where(row == 0, 0.0, value)
            put(j, y, value)

    line = lax.broadcasted_iota(jnp.int32, (WIDE, WIDE), 0)
    column = lax.broadcasted_iota(jnp.int32, (WIDE, WIDE), 1)
    apart = jnp.abs(line - column)
    band = jnp.where(apart == 0, keep, jnp.where(apart == 1, 1.0, 0.0)).astype(bf16)
    for unit in range(units):
        first = sums[unit][0]
        pltpu.matmul_push_rhs(band, 0, unit)
        pltpu.matmul_acc_lhs(first, jnp.zeros((TALL, WIDE), bf16), load_staged_rhs=0)
        stage[unit, 0:TALL, 0:WIDE] = pltpu.matmul_pop(first)

    def flush(k, x, slot):
        return pltpu.make_async_copy(stage.at[slot], out_ref.at[k, x], out_sems.at[slot])

    def work(k, x, phase, slot=None, gate=None):
        def put_first(j, y, value):
            if gate is not None:
                value = value * gate
            ring[phase % turns][j, pl.ds(SUB + y * TALL, TALL), :] = value

        def put_second(j, y, value):
            stage[slot, y * TALL : (y + 1) * TALL, j * LANES : (j + 1) * LANES] = value * (share * share)

        jobs = [(field.at[k, x + 1], field.at[k, x], field.at[k, x + 2], put_first)]
        if slot is not None:
            jobs.append((ring[(phase - 2) % turns], ring[(phase - 3) % turns], ring[(phase - 1) % turns], put_second))
        group = 3
        for y in range(0, strips + group, group):
            spot = y // group % 2 * 2 * group
            if y < strips:
                multiply([(job[0], y + n, spot + n * 2 + i) for n in range(group) for i, job in enumerate(jobs)])
            if y >= group:
                for n in range(group):
                    for i, (center, before, after, put) in enumerate(jobs):
                        complete(center, before, after, y - group + n, 2 * group - spot + n * 2 + i, put)

    def component(k, _):
        for copy in sides(k):
            copy.wait()
        for copy in load(k, 0):
            copy.wait()
        first_gate = jnp.where(edge_ref[0] == 0, 0.0, 1.0)
        for phase in range(3):
            work(k, phase, phase, None, first_gate if phase == 0 else None)

        def quad(i, _):
            @pl.when((i + 1) * turns < width)
            def _():
                for copy in load(k, i + 1):
                    copy.wait()

            turn = k * (width // turns) + i
            slots = (turn % 2) * turns

            @pl.when(turn >= 2)
            def _():
                for sub in range(turns):
                    flush(k, 0, slots + sub).wait()

            last_gate = jnp.where(jnp.logical_and((i + 1) * turns == width, edge_ref[1] == 0), 0.0, 1.0)
            for sub in range(turns):
                x = jnp.minimum(i * turns + sub + 3, width + 1)
                work(k, x, sub + 3, slots + sub, last_gate if sub == turns - 2 else None)
            for sub in range(turns):
                flush(k, i * turns + sub, slots + sub).start()
            return 0

        lax.fori_loop(0, width // turns, quad, 0)
        return 0

    lax.fori_loop(0, comps, component, 0)
    for slot in range(2 * turns):
        flush(0, 0, slot).wait()


def scatter_body(_, returned_ref, vertex_ref, inter_ref, left_ref, right_ref, rows_sc, ones_sc, *, per, width):
    rows, _ = vertex_ref.shape
    blocks = inter_ref.shape[1]
    tiles = blocks // width
    line = lax.broadcasted_iota(jnp.int32, (blocks, LANES), 0)
    home = (line % width) * tiles + line // width
    lane = lax.broadcasted_iota(jnp.int32, (LANES, LANES), 0)
    for row in range(rows):
        vertex = vertex_ref[row : row + 1, :]
        high = lax.shift_right_arithmetic(vertex, 7)
        low = jnp.bitwise_and(vertex, LANES - 1)
        span = slice(row * LANES, (row + 1) * LANES)
        ones_sc[:, span] = jnp.where(lane == low, 1.0, 0.0).astype(bf16)
        here = home == high
        for k in range(3):
            value = packed_row(returned_ref, k, row, per)
            part = value
            for piece in range(3):
                top = part.astype(bf16).astype(f32)
                at = (piece * 3 + k) * blocks
                rows_sc[at : at + blocks, span] = jnp.where(here, top, 0.0).astype(bf16)
                part = part - top
    total = lax.dot_general(
        rows_sc[...], ones_sc[...], (((1,), (1,)), ((), ())), preferred_element_type=f32
    )
    size = 3 * blocks
    total = total[:size] + (total[size : 2 * size] + total[2 * size :])
    for k in range(3):
        inter_ref[k] = total[k * blocks : (k + 1) * blocks]
        for j in range(tiles):
            at = k * blocks + j * width
            q = k * tiles + j
            left_ref[q : q + 1, :] = total[at : at + 1]
            right_ref[q : q + 1, :] = total[at + width - 1 : at + width]


def finish_body(base_ref, inter_ref, left_ref, right_ref, out_ref):
    k = pl.program_id(0)
    _, width, _, depth = base_ref.shape
    tiles = depth // LANES
    lane = lax.broadcasted_iota(jnp.int32, (width, LANES), 1)
    parts = [inter_ref[0, j * width : (j + 1) * width, :] for j in range(tiles)]
    down = [pltpu.roll(p, 1, 1) for p in parts]
    up = [pltpu.roll(p, LANES - 1, 1) for p in parts]
    line = lax.broadcasted_iota(jnp.int32, (width, LANES), 0)
    for j in range(tiles):
        mid = parts[j]
        back = jnp.where(lane == 0, down[j - 1] if j else 0.0, down[j])
        fore = jnp.where(lane == LANES - 1, up[j + 1] if j + 1 < tiles else 0.0, up[j])
        q = k * tiles + j
        prev = jnp.where(line == 0, left_ref[pl.ds(q, 1), :], pltpu.roll(mid, 1, 0))
        after = jnp.where(line == width - 1, right_ref[pl.ds(q, 1), :], pltpu.roll(mid, width - 1, 0))
        near = ((prev + after) + (back + fore)) * (share * share)
        one = mid * (1.2 * share) + near
        two = mid * (share * share)
        span = slice(j * LANES, (j + 1) * LANES)
        for x in range(width):
            base = base_ref[0, x, :, span]
            row = lax.broadcasted_iota(jnp.int32, base.shape, 0)
            add = jnp.where(row == 1, one[x : x + 1], jnp.where(row == 2, two[x : x + 1], 0.0))
            out_ref[0, x, :, span] = jnp.where(row == 0, mid[x : x + 1], base + add)


def exchange(packed, per, cap):
    if per:
        return lax.all_to_all(packed, "dev", split_axis=0, concat_axis=0, tiled=True)
    count = lax.axis_size("dev")
    split = packed.reshape(3, count, cap)
    moved = lax.all_to_all(split, "dev", split_axis=1, concat_axis=1, tiled=True)
    return moved.reshape(packed.shape)


def local(
    displacement,
    send_node,
    member_slot,
    inverse_part,
    source_coord,
    target_coord,
    unity_weight,
    result_pick,
    receive_vertex,
    mesh_before,
):
    count = lax.axis_size("dev")
    place = lax.axis_index("dev")
    send_cap = send_node.shape[0] // count
    result_cap = result_pick.shape[0] // count
    send_per = send_cap // LANES if send_cap % LANES == 0 else 0
    result_per = result_cap // LANES if result_cap % LANES == 0 else 0
    clusters, points = member_slot.shape
    verts = unity_weight.shape[1]
    comps, width, height, depth = mesh_before.shape
    tiles = depth // LANES
    blocks = width * tiles

    def packed_shape(per, size):
        shape = (count, 3 * per, LANES) if per else (3, size // LANES, LANES)
        return jax.ShapeDtypeStruct(shape, f32)

    up = [(i, i + 1) for i in range(count - 1)]
    down = [(i + 1, i) for i in range(count - 1)]

    field = in_hbm(mesh_before)
    side = (comps, 2, height, depth)
    node_rows = send_node.reshape(-1, LANES)
    outgoing, head, tail = pl.pallas_call(
        lambda *refs: pick_body(*refs, per=send_per),
        out_shape=(packed_shape(send_per, send_node.shape[0]), pltpu.HBM(side, f32), pltpu.HBM(side, f32)),
        in_specs=[HBM] * 3,
        out_specs=(VMEM, HBM, HBM),
        scratch_shapes=[
            pltpu.VMEM(displacement.shape, f32),
            pltpu.VMEM(node_rows.shape, jnp.int32),
            pltpu.VMEM(side, f32),
            pltpu.VMEM(side, f32),
            pltpu.SemaphoreType.DMA((6,)),
        ],
        compiler_params=params(6),
        name="pick_nodes",
    )(in_hbm(displacement), in_hbm(node_rows), field)
    arrived = exchange(outgoing, send_per, send_cap)
    halo_left = lax.ppermute(tail, "dev", up)
    halo_right = lax.ppermute(head, "dev", down)

    pair = jax.ShapeDtypeStruct((clusters, points, verts), bf16)
    ahead = min(clusters, AHEAD)
    pair = pltpu.HBM((ahead, points, verts), bf16)
    source_turned = jnp.transpose(source_coord, (1, 0, 2))
    target_turned = jnp.transpose(target_coord, (1, 0, 2))
    small = (member_slot, unity_weight, result_pick.reshape(-1, LANES), receive_vertex.reshape(-1, LANES))
    (kernel_high, kernel_low, slots, weight, picks, vertices, source, target) = pl.pallas_call(
        prepare_body,
        out_shape=(pair, pair)
        + tuple(pltpu.VMEM(x.shape, x.dtype) for x in small + (source_turned, target_turned)),
        in_specs=[HBM] * 6,
        out_specs=(HBM,) * 2 + (VMEM,) * 6,
        scratch_shapes=[
            pltpu.VMEM((ahead, points, verts), bf16),
            pltpu.VMEM((ahead, points, verts), bf16),
            pltpu.SemaphoreType.DMA((6,)),
            pltpu.SemaphoreType.DMA((2, ahead)),
        ],
        compiler_params=params(28),
        name="prepare",
    )(*map(in_hbm, (source_turned, target_turned) + small))

    outgoing_results = pl.pallas_call(
        lambda *refs: result_body(*refs, per_in=send_per, per_out=result_per, ahead=ahead),
        out_shape=packed_shape(result_per, result_pick.shape[0]),
        in_specs=[VMEM] * 4 + [HBM] * 3 + [VMEM] * 2,
        out_specs=VMEM,
        scratch_shapes=[
            pltpu.VMEM(inverse_part.shape, bf16),
            pltpu.VMEM((clusters, points, verts), bf16),
            pltpu.VMEM((clusters, points, verts), bf16),
            pltpu.VMEM((clusters, SUB, points), f32),
            pltpu.VMEM((clusters, SUB, verts), f32),
            pltpu.SemaphoreType.DMA((3, clusters)),
        ],
        compiler_params=params(40),
        name="cluster_results",
    )(arrived, slots, source, target, in_hbm(inverse_part), in_hbm(kernel_high), in_hbm(kernel_low), weight, picks)
    returned = exchange(outgoing_results, result_per, result_cap)

    edges = jnp.stack([place, count - 1 - place]).astype(jnp.int32)
    batch = turns = 4
    if width % turns or depth % (2 * WIDE) or height % TALL:
        raise ValueError("mesh shape")

    def with_sums(*refs):
        places = 12 * (depth // WIDE // 2)
        sums = tuple(tuple(pltpu.ACC(unit)((TALL, WIDE), f32) for _ in range(places)) for unit in range(2))
        pl.run_scoped(lambda *sums: mesh_body(*refs, sums, batch=batch), *sums)

    base = pl.pallas_call(
        with_sums,
        out_shape=jax.ShapeDtypeStruct(mesh_before.shape, f32),
        in_specs=[ANY, SMEM, HBM, ANY, ANY],
        out_specs=HBM,
        scratch_shapes=[
            pltpu.VMEM((comps, width + 4, tiles, height + 2 * SUB, LANES), f32),
            tuple(pltpu.VMEM((tiles, height + 2 * SUB, LANES), f32) for _ in range(turns)),
            pltpu.VMEM((2 * turns, height, depth), f32),
            pltpu.SemaphoreType.DMA((comps, width // batch, tiles)),
            pltpu.SemaphoreType.DMA((comps, tiles, 2)),
            pltpu.SemaphoreType.DMA((2 * turns,)),
        ],
        compiler_params=params(24),
        name="sweeps",
    )(outgoing_results, edges, field, halo_left, halo_right)

    slots_in = receive_vertex.shape[0]
    edge_shape = jax.ShapeDtypeStruct((3 * tiles, LANES), f32)
    interface, first, last = pl.pallas_call(
        lambda *refs: scatter_body(*refs, per=result_per, width=width),
        out_shape=(jax.ShapeDtypeStruct((3, blocks, LANES), f32), edge_shape, edge_shape),
        in_specs=[HBM, VMEM, VMEM],
        out_specs=(VMEM, VMEM, VMEM),
        scratch_shapes=[pltpu.VMEM((9 * blocks, slots_in), bf16), pltpu.VMEM((LANES, slots_in), bf16)],
        compiler_params=params(16),
        name="scatter",
    )(in_hbm(base), returned, vertices)

    from_left = lax.ppermute(last, "dev", up)
    from_right = lax.ppermute(first, "dev", down)

    wall = pl.BlockSpec((1, width, SUB, depth), lambda k: (k, 0, 0, 0))
    return pl.pallas_call(
        finish_body,
        out_shape=jax.ShapeDtypeStruct(mesh_before.shape, f32),
        grid=(comps,),
        in_specs=[wall, pl.BlockSpec((1, blocks, LANES), lambda k: (k, 0, 0)), VMEM, VMEM],
        out_specs=wall,
        input_output_aliases={0: 0},
        compiler_params=params(8),
        name="finish",
    )(base, interface, from_left, from_right)


def solution(mesh):
    in_specs = (
        P(None, "dev"),
        P("dev"),
        P("dev", None),
        P("dev", None, None),
        P("dev", None, None),
        P("dev", None, None),
        P("dev", None),
        P("dev"),
        P("dev"),
        P(None, "dev", None, None),
    )
    out_specs = P(None, "dev", None, None)

    return jax.shard_map(local, mesh=mesh, in_specs=in_specs, out_specs=out_specs, check_vma=False)
```

```python
import math

import jax
import jax.numpy as jnp
from jax import lax
from jax.experimental import pallas as pl
from jax.experimental.pallas import tpu as pltpu
from jax.sharding import PartitionSpec as P


LANES = 128
SUB = 8
TALL = 16
WIDE = 256
share = 0.8 / 6.0
keep = 0.2 / share
sharpness = 8.0
VMEM = pl.BlockSpec(memory_space=pltpu.VMEM)
ANY = pl.BlockSpec(memory_space=pl.ANY)
HBM = pl.BlockSpec(memory_space=pltpu.HBM)
SMEM = pl.BlockSpec(memory_space=pltpu.SMEM)
f32 = jnp.float32
bf16 = jnp.bfloat16


def in_hbm(value):
    return pltpu.with_memory_space_constraint(value, pltpu.HBM)


def params(limit, **more):
    return pltpu.CompilerParams(vmem_limit_bytes=limit << 20, **more)


def lane_gather(row, lane):
    return jnp.take_along_axis(row, lane, axis=1, mode="promise_in_bounds")


def gather_rows(row_of, blocks, index_of, groups):
    index = [index_of(g) for g in range(groups)]
    high = [lax.shift_right_arithmetic(i, 7) for i in index]
    low = [jnp.bitwise_and(i, LANES - 1) for i in index]
    out = [[jnp.zeros((SUB, LANES), f32) for _ in range(3)] for _ in range(groups)]
    for block in range(blocks):
        rows = [jnp.broadcast_to(row_of(k, block), (SUB, LANES)) for k in range(3)]
        for g in range(groups):
            here = high[g] == block
            for k in range(3):
                out[g][k] = jnp.where(here, lane_gather(rows[k], low[g]), out[g][k])
    return out


def slot_row(ref, k, row, per, group=0):
    if per:
        at = group * 3 * per + k * per + row % per
        return ref[row // per, at : at + 1, :]
    return ref[group * 3 + k, row : row + 1, :]


def store_rows(out_ref, g, values, per, beside=False):
    for k in range(3):
        for s in range(SUB):
            row = g * SUB + s
            value = values[k][s : s + 1, :]
            if per:
                d, at = row // per, k * per + row % per
                out_ref[d, at : at + 1, :] = value
                if beside and d + 1 < out_ref.shape[0]:
                    out_ref[d + 1, 3 * per + at : 3 * per + at + 1, :] = value
                if beside and d > 0:
                    out_ref[d - 1, 6 * per + at : 6 * per + at + 1, :] = value
            else:
                out_ref[k, row : row + 1, :] = value


def pick_body(
    table_hbm, index_hbm, mesh_ref, vertex_hbm, slot_hbm, weight_hbm, pick_hbm, source_hbm, target_hbm,
    out_ref, head, tail, vertex_ref, slot_ref, weight_ref, pick_ref, source_ref, target_ref,
    table_ref, index_ref, sems, side_sems, *, per,
):
    comps, width, height, depth = mesh_ref.shape
    tiles = depth // LANES
    pairs = (
        (index_hbm, index_ref), (table_hbm, table_ref), (vertex_hbm, vertex_ref), (slot_hbm, slot_ref),
        (weight_hbm, weight_ref), (pick_hbm, pick_ref), (source_hbm, source_ref), (target_hbm, target_ref),
    )
    needed = [pltpu.make_async_copy(a, b, sems.at[i]) for i, (a, b) in enumerate(pairs)]
    side = []
    for k in range(comps):
        for p in range(2):
            rows = pl.ds((k * 2 + p) * height, height)
            side.append(pltpu.make_async_copy(mesh_ref.at[k, p], head.at[rows], side_sems.at[0, k, p]))
            side.append(
                pltpu.make_async_copy(mesh_ref.at[k, width - 2 + p], tail.at[rows], side_sems.at[1, k, p])
            )
    for copy in needed + side:
        copy.start()
    for copy in needed[:2]:
        copy.wait()
    groups = index_ref.shape[0] // SUB
    blocks = table_ref.shape[1] // LANES
    half = max(1, groups // 2)
    for first in range(0, groups, half):
        got = gather_rows(
            lambda k, b: table_ref[k : k + 1, b * LANES : (b + 1) * LANES],
            blocks,
            lambda g: index_ref[(first + g) * SUB : (first + g + 1) * SUB, :],
            half,
        )
        for g in range(half):
            store_rows(out_ref, first + g, got[g], per)
    for copy in needed[2:]:
        copy.wait()
    start = comps * 2 * height
    for row in range(vertex_ref.shape[0]):
        value = vertex_ref[row : row + 1, :].astype(f32)
        at, j = start + row // tiles, row % tiles * LANES
        head[at : at + 1, j : j + LANES] = value
        tail[at : at + 1, j : j + LANES] = value
    for copy in side:
        copy.wait()


def pieces(value, count=3):
    found = []
    for _ in range(count):
        top = value.astype(bf16).astype(f32)
        found.append(top)
        value = value - top
    return found


def factor(points, target):
    square = points * points
    norm = jnp.broadcast_to(jnp.sum(square, axis=0, keepdims=True), square.shape)
    row = lax.broadcasted_iota(jnp.int32, square.shape, 0)
    a, b, c = pieces(norm)
    p, q, r = pieces(points)
    if target:
        edge = jnp.where(row < 3, -1.0, jnp.where(row == 3, -a, jnp.where(row == 4, -b, jnp.where(row == 5, -c, 0.0))))
        blocks = [2.0 * p, 2.0 * q, 2.0 * p, 2.0 * q, 2.0 * r, 2.0 * p, edge]
    else:
        edge = jnp.where(row == 0, a, jnp.where(row == 1, b, jnp.where(row == 2, c, jnp.where(row < 6, 1.0, 0.0))))
        blocks = [p, p, q, q, p, r, edge]
    blocks.append(jnp.zeros(square.shape, f32))
    return jnp.concatenate(blocks, axis=0)


def rbf_matrix(source, target, put):
    scale = math.sqrt(sharpness * math.log2(math.e))
    points = source[0].shape[1]
    step = LANES

    def centred(rows):
        blank = jnp.zeros((SUB - 3, rows[0].shape[1]), f32)
        return jnp.concatenate([(row - 0.5) * scale for row in rows] + [blank], axis=0)

    turned = jnp.transpose(factor(centred(source), False)).astype(bf16)
    right = factor(centred(target), True).astype(bf16)
    for at in range(0, points, step):
        value = jnp.exp2(jnp.dot(turned[at : at + step], right, preferred_element_type=f32))
        high = value.astype(bf16)
        put(at, step, high, (value - high.astype(f32)).astype(bf16))


def result_body(
    arrived_ref, slot_ref, source_ref, target_ref, inverse_ref, weight_ref, pick_ref,
    out_ref, inverse, high, low, members, results, sems, *, per_in, per_out,
):
    clusters, points = slot_ref.shape
    verts = weight_ref.shape[1]
    blocks = (arrived_ref.shape[0] * per_in) if per_in else arrived_ref.shape[1]
    per_cluster = verts // LANES
    groups = pick_ref.shape[0] // SUB
    fold = points // LANES // SUB
    copies = [pltpu.make_async_copy(inverse_ref.at[c], inverse.at[c], sems.at[c]) for c in range(clusters)]
    for copy in copies:
        copy.start()
    members[...] = jnp.zeros(members.shape, f32)

    def gather_members(c):
        got = gather_rows(
            lambda k, b: slot_row(arrived_ref, k, b, per_in),
            blocks,
            lambda g: jnp.concatenate(
                [slot_ref[c : c + 1, (g * SUB + j) * LANES : (g * SUB + j + 1) * LANES] for j in range(SUB)], axis=0
            ),
            fold,
        )
        for g in range(fold):
            for j in range(SUB):
                at = (g * SUB + j) * LANES
                for k in range(3):
                    members[c, k : k + 1, at : at + LANES] = got[g][k][j : j + 1, :]

    def joined(ref, c):
        return jnp.concatenate([ref[c, j] for j in range(per_cluster)], axis=1)

    def evaluate(c):
        mine = members[c]
        copies[c].wait()
        coupling = lax.dot_general(
            mine.astype(bf16), inverse[c], (((1,), (1,)), ((), ())), preferred_element_type=f32
        )
        coefficient = mine + coupling
        c_high = coefficient.astype(bf16)
        c_low = (coefficient - c_high.astype(f32)).astype(bf16)
        both = jnp.concatenate([c_high, c_low], axis=0)
        first = jnp.dot(both, joined(high, c), preferred_element_type=f32)
        second = jnp.dot(c_high, joined(low, c), preferred_element_type=f32)
        total = first[:SUB] + (first[SUB:] + second)
        results[c] = total * weight_ref[c : c + 1, :]

    for c in range(clusters):

        def put(at, step, upper, lower):
            for j in range(per_cluster):
                high[c, j, at : at + step, :] = upper[:, j * LANES : (j + 1) * LANES]
                low[c, j, at : at + step, :] = lower[:, j * LANES : (j + 1) * LANES]

        rbf_matrix(*(tuple(ref[k, c : c + 1, :] for k in range(3)) for ref in (source_ref, target_ref)), put)
        gather_members(c)
        evaluate(c)
    if per_out:
        blank = jnp.zeros((3 * per_out, LANES), f32)
        out_ref[0, 3 * per_out : 6 * per_out, :] = blank
        out_ref[out_ref.shape[0] - 1, 6 * per_out : 9 * per_out, :] = blank
    half = max(1, groups // 2)
    for start in range(0, groups, half):
        got = gather_rows(
            lambda k, b: results[
                b // per_cluster, k : k + 1, (b % per_cluster) * LANES : (b % per_cluster + 1) * LANES
            ],
            clusters * per_cluster,
            lambda g: pick_ref[(start + g) * SUB : (start + g + 1) * SUB, :],
            half,
        )
        for g in range(half):
            store_rows(out_ref, start + g, got[g], per_out, True)


def columns(j):
    return pl.ds(j * LANES, LANES)


def start_band(sums):
    line = lax.broadcasted_iota(jnp.int32, (WIDE, WIDE), 0)
    column = lax.broadcasted_iota(jnp.int32, (WIDE, WIDE), 1)
    apart = jnp.abs(line - column)
    band = jnp.where(apart == 0, keep, jnp.where(apart == 1, 1.0, 0.0)).astype(bf16)
    ends = []
    for unit in range(len(sums)):
        pltpu.matmul_push_rhs(band, 0, unit)
        pltpu.matmul_acc_lhs(sums[unit][0], jnp.zeros((TALL, WIDE), bf16), load_staged_rhs=0)
        ends.append(pltpu.matmul_pop(sums[unit][0]))
    return ends


def sweep_planes(jobs, height, depth, sums):
    tiles, strips = depth // LANES, height // TALL
    wides, part = depth // WIDE, WIDE // LANES
    units = len(sums)
    halves = wides // units
    lane = lax.broadcasted_iota(jnp.int32, (TALL, LANES), 1)
    row = lax.broadcasted_iota(jnp.int32, (TALL, LANES), 0)

    def place(spot, h):
        return sums[h % units][spot * halves + h // units]

    def multiply(todo):
        later = []
        for center, y, spot in todo:
            for h in range(wides):
                value = jnp.concatenate(
                    [center[j, pl.ds(SUB + y * TALL, TALL), :] for j in range(h * part, (h + 1) * part)], axis=1
                )
                high = value.astype(bf16)
                pltpu.matmul_acc_lhs(place(spot, h), high)
                later.append((place(spot, h), (value - high.astype(f32)).astype(bf16)))
        for total, low in later:
            pltpu.matmul_acc_lhs(total, low)

    def complete(center, before, after, y, spot, put):
        at = SUB + y * TALL
        beside = [pltpu.matmul_pop(place(spot, h)) for h in range(wides)]
        for j in range(tiles):
            lower = center[j, pl.ds(at - 1, TALL), :]
            if y == 0:
                lower = jnp.where(row < 2, 0.0, lower)
            near = (before[j, pl.ds(at, TALL), :] + after[j, pl.ds(at, TALL), :]) + (
                center[j, pl.ds(at + 1, TALL), :] + lower
            )
            h, p = j // part, j % part
            value = near + beside[h][:, p * LANES : (p + 1) * LANES]
            if p == 0 and h:
                value = value + jnp.where(lane == 0, pltpu.roll(center[j - 1, pl.ds(at, TALL), :], 1, 1), 0.0)
            if p == part - 1 and j + 1 < tiles:
                other = pltpu.roll(center[j + 1, pl.ds(at, TALL), :], LANES - 1, 1)
                value = value + jnp.where(lane == LANES - 1, other, 0.0)
            if y == 0:
                value = jnp.where(row == 0, 0.0, value)
            put(j, y, value)

    group = 3
    for y in range(0, strips + group, group):
        base = y // group % 2 * 2 * group
        if y < strips:
            multiply([(job[0], y + n, base + n * 2 + i) for n in range(group) for i, job in enumerate(jobs)])
        if y >= group:
            for n in range(group):
                for i, (center, before, after, put) in enumerate(jobs):
                    complete(center, before, after, y - group + n, 2 * group - base + n * 2 + i, put)


def mesh_body(_, mesh_ref, out_ref, field, ring, stage, in_sems, out_sems, sums):
    comps, width, height, depth = mesh_ref.shape
    tiles = depth // LANES
    turns = len(ring)
    quads = width // turns - 1

    def load(k, b):
        return [
            pltpu.make_async_copy(
                mesh_ref.at[k, pl.ds(b * turns, turns), :, columns(j)],
                field.at[k, pl.ds(b * turns, turns), j, pl.ds(SUB, height), :],
                in_sems.at[k, b, j],
            )
            for j in range(tiles)
        ]

    for k in range(comps):
        for b in range(width // turns):
            for copy in load(k, b):
                copy.start()

    blank = jnp.zeros((SUB, LANES), f32)
    for j in range(tiles):
        for plane in ring:
            plane[j, SUB + height : 2 * SUB + height, :] = blank

    def clear(i, _):
        for j in range(tiles):
            field[i // width, i % width, j, SUB + height : 2 * SUB + height, :] = blank
        return 0

    lax.fori_loop(0, comps * width, clear, 0)
    for unit, value in enumerate(start_band(sums)):
        stage[unit, 0:TALL, 0:WIDE] = value

    def flush(k, x, slot):
        return pltpu.make_async_copy(stage.at[slot], out_ref.at[k, x], out_sems.at[slot])

    def work(k, x, phase, slot=None):
        def put_first(j, y, value):
            ring[phase % turns][j, pl.ds(SUB + y * TALL, TALL), :] = value

        def put_second(j, y, value):
            stage[slot, y * TALL : (y + 1) * TALL, j * LANES : (j + 1) * LANES] = value * (share * share)

        jobs = [(field.at[k, x], field.at[k, x - 1], field.at[k, x + 1], put_first)]
        if slot is not None:
            jobs.append((ring[(phase - 2) % turns], ring[(phase - 3) % turns], ring[(phase - 1) % turns], put_second))
        sweep_planes(jobs, height, depth, sums)

    def component(k, _):
        for b in range(2):
            for copy in load(k, b):
                copy.wait()
        for phase in range(3):
            work(k, phase + 1, phase)

        def quad(i, _):
            @pl.when(i + 2 < width // turns)
            def _():
                for copy in load(k, i + 2):
                    copy.wait()

            turn = k * quads + i
            slots = (turn % 2) * turns

            @pl.when(turn >= 2)
            def _():
                for sub in range(turns):
                    flush(k, 0, slots + sub).wait()

            for sub in range(turns):
                work(k, jnp.minimum(i * turns + sub + 4, width - 2), sub + 3, slots + sub)
            for sub in range(turns):
                flush(k, i * turns + sub + 2, slots + sub).start()
            return 0

        lax.fori_loop(0, quads, quad, 0)
        return 0

    lax.fori_loop(0, comps, component, 0)
    for slot in range(2 * turns):
        flush(0, 0, slot).wait()


def edges_body(_, edge_ref, mesh_ref, left_ref, right_ref, out_ref, field, swept, stage, in_sems, out_sems, sums):
    comps, width, height, depth = mesh_ref.shape
    tiles = depth // LANES

    def outer(k):
        found = []
        for j in range(tiles):
            for side, ref in enumerate((left_ref, right_ref)):
                own, other = (2, 0) if side == 0 else (0, 4)
                found.append(
                    pltpu.make_async_copy(
                        mesh_ref.at[k, pl.ds(side * (width - 4), 4), :, columns(j)],
                        field.at[k, side, pl.ds(own, 4), j, pl.ds(SUB, height), :],
                        in_sems.at[k, j, side, 0],
                    )
                )
                for p in range(2):
                    found.append(
                        pltpu.make_async_copy(
                            ref.at[pl.ds((k * 2 + p) * height, height), columns(j)],
                            field.at[k, side, other + p, j, pl.ds(SUB, height), :],
                            in_sems.at[k, j, side, 1 + p],
                        )
                    )
        return found

    for k in range(comps):
        for copy in outer(k):
            copy.start()

    blank = jnp.zeros((SUB, LANES), f32)
    for j in range(tiles):
        for side in range(2):
            for p in range(4):
                swept[side][p][j, SUB + height : 2 * SUB + height, :] = blank

    def clear(i, _):
        for side in range(2):
            for p in range(6):
                for j in range(tiles):
                    field[i, side, p, j, SUB + height : 2 * SUB + height, :] = blank
        return 0

    lax.fori_loop(0, comps, clear, 0)
    for unit, value in enumerate(start_band(sums)):
        stage[0, unit, 0:TALL, 0:WIDE] = value
    gates = [jnp.where(edge_ref[side] == 0, 0.0, 1.0) for side in range(2)]

    def save(k):
        return [
            pltpu.make_async_copy(
                stage.at[k, side * 2 + p],
                out_ref.at[k, side * (width - 2) + p],
                out_sems.at[k, side, p],
            )
            for side in range(2)
            for p in range(2)
        ]

    def component(k, _):
        for copy in outer(k):
            copy.wait()
        for p in range(4):
            jobs = []
            for side in range(2):

                def put(j, y, value, side=side):
                    if p == side * 3:
                        value = value * gates[side]
                    swept[side][p][j, pl.ds(SUB + y * TALL, TALL), :] = value

                jobs.append((field.at[k, side, p + 1], field.at[k, side, p], field.at[k, side, p + 2], put))
            sweep_planes(jobs, height, depth, sums)
        for p in range(2):
            jobs = []
            for side in range(2):

                def put(j, y, value, side=side):
                    value = value * (share * share)
                    span = slice(j * LANES, (j + 1) * LANES)
                    stage[k, side * 2 + p, y * TALL : (y + 1) * TALL, span] = value

                jobs.append((swept[side][p + 1], swept[side][p], swept[side][p + 2], put))
            sweep_planes(jobs, height, depth, sums)
        for copy in save(k):
            copy.start()
        return 0

    lax.fori_loop(0, comps, component, 0)
    for k in range(comps):
        for copy in save(k):
            copy.wait()


def finish_body(
    base_ref, returned_ref, vertex_ref, left_ref, right_ref, out_ref,
    wall, left, right, split, high_sc, low_sc, rows_sc, ones_sc, sems, *, per,
):
    comps, width, _, depth = wall.shape
    tiles = depth // LANES
    rows = vertex_ref.shape[0]
    count = left.shape[0]
    start = left_ref.shape[0] - count
    fetch = [pltpu.make_async_copy(base_ref.at[k, :, pl.ds(0, SUB), :], wall.at[k], sems.at[k]) for k in range(comps)]
    beside = [
        pltpu.make_async_copy(left_ref.at[pl.ds(start, count), :], left, sems.at[comps]),
        pltpu.make_async_copy(right_ref.at[pl.ds(start, count), :], right, sems.at[comps + 1]),
    ]
    for copy in beside + fetch:
        copy.start()
    whole = returned_ref[...]
    top = whole.astype(bf16).astype(f32)
    split[0] = top
    split[1] = whole - top
    for copy in beside:
        copy.wait()

    def spread(row, size):
        tile = jnp.broadcast_to(row, (TALL, LANES)).astype(bf16)
        return jnp.concatenate([tile] * (size // TALL), axis=0)

    def lines(size):
        return lax.broadcasted_iota(jnp.int32, (size, LANES), 0)

    def gathered(vertices, group, home, lows):
        size = home.shape[0]
        shift = lows.bit_length() - 1
        vertices = jnp.concatenate(vertices, axis=0) if isinstance(vertices, list) else vertices
        high_sc[...] = lax.shift_right_arithmetic(vertices, shift).astype(f32)
        low_sc[...] = jnp.bitwise_and(vertices, lows - 1).astype(f32)
        home = home.astype(f32).astype(bf16)
        line = lines(lows).astype(f32).astype(bf16)
        one = jnp.ones((lows, LANES), bf16)
        nothing = jnp.zeros((lows, LANES), bf16)
        empty = jnp.zeros((size, LANES), bf16)
        for row in range(rows):
            match = line == spread(low_sc[row : row + 1, :], lows)
            ones_sc[row, :lows] = jnp.where(match, one, nothing)
            here = home == spread(high_sc[row : row + 1, :], size)
            for term in range(2):
                for k in range(comps):
                    value = spread(slot_row(split.at[term], k, row, per, group), size)
                    at = (term * comps + k) * size
                    rows_sc[row, at : at + size] = jnp.where(here, value, empty)
        total = lax.dot_general(
            jnp.concatenate([rows_sc[row, : 2 * comps * size] for row in range(rows)], axis=1),
            jnp.concatenate([ones_sc[row, :lows] for row in range(rows)], axis=1),
            (((1,), (1,)), ((), ())),
            preferred_element_type=f32,
        )
        total = total[: comps * size] + total[comps * size :]
        return [total[k * size : (k + 1) * size] for k in range(comps)]

    blocks = depth // WIDE
    line = lines(width * blocks)
    own = gathered(vertex_ref[...], 0, (line % width) * blocks + line // width, WIDE)
    line = lines(TALL)

    def unfold(ref):
        return [ref[at : at + 1, j * LANES : (j + 1) * LANES].astype(jnp.int32) for at in range(count) for j in range(tiles)]

    last = gathered(unfold(left), 1, jnp.where(line < tiles, (width - 1) * tiles + line, -1), LANES)
    first = gathered(unfold(right), 2, jnp.where(line < tiles, line, -1), LANES)

    lane = lax.broadcasted_iota(jnp.int32, (width, LANES), 1)
    line = lax.broadcasted_iota(jnp.int32, (width, LANES), 0)
    row = lax.broadcasted_iota(jnp.int32, (SUB, LANES), 0)
    flush = [pltpu.make_async_copy(wall.at[k], out_ref.at[k, :, pl.ds(0, SUB), :], sems.at[comps + 2 + k]) for k in range(comps)]
    per_wide = WIDE // LANES
    for k in range(comps):
        parts = []
        for j in range(tiles):
            block, lanes = j // per_wide * width, j % per_wide * LANES
            parts.append(own[k][block : block + width, lanes : lanes + LANES])
        down = [pltpu.roll(p, 1, 1) for p in parts]
        up = [pltpu.roll(p, LANES - 1, 1) for p in parts]
        fetch[k].wait()
        for j in range(tiles):
            mid = parts[j]
            back = jnp.where(lane == 0, down[j - 1] if j else 0.0, down[j])
            fore = jnp.where(lane == LANES - 1, up[j + 1] if j + 1 < tiles else 0.0, up[j])
            prev = jnp.where(line == 0, last[k][j : j + 1], pltpu.roll(mid, 1, 0))
            after = jnp.where(line == width - 1, first[k][j : j + 1], pltpu.roll(mid, width - 1, 0))
            near = ((prev + after) + (back + fore)) * (share * share)
            one = mid * (1.2 * share) + near
            two = mid * (share * share)
            span = slice(j * LANES, (j + 1) * LANES)
            for x in range(width):
                add = jnp.where(row == 1, one[x : x + 1], jnp.where(row == 2, two[x : x + 1], 0.0))
                wall[k, x, :, span] = jnp.where(row == 0, mid[x : x + 1], wall[k, x, :, span] + add)
        flush[k].start()
    for copy in flush:
        copy.wait()


def exchange(packed, per, cap, beside=False):
    if per:
        return lax.all_to_all(packed, "dev", split_axis=0, concat_axis=0, tiled=True)
    count = lax.axis_size("dev")
    split = packed.reshape(3, count, cap)
    if beside:
        blank = jnp.zeros((3, 1, cap), f32)
        before = jnp.concatenate([blank, split[:, :-1]], axis=1)
        after = jnp.concatenate([split[:, 1:], blank], axis=1)
        split = jnp.concatenate([split, before, after], axis=0)
    moved = lax.all_to_all(split, "dev", split_axis=1, concat_axis=1, tiled=True)
    return moved.reshape((split.shape[0],) + packed.shape[1:])


def local(
    displacement,
    send_node,
    member_slot,
    inverse_part,
    source_coord,
    target_coord,
    unity_weight,
    result_pick,
    receive_vertex,
    mesh_before,
):
    count = lax.axis_size("dev")
    place = lax.axis_index("dev")
    send_cap = send_node.shape[0] // count
    result_cap = result_pick.shape[0] // count
    send_per = send_cap // LANES if send_cap % LANES == 0 else 0
    result_per = result_cap // LANES if result_cap % LANES == 0 else 0
    clusters, points = member_slot.shape
    verts = unity_weight.shape[1]
    comps, width, height, depth = mesh_before.shape
    tiles = depth // LANES
    count_rows = receive_vertex.shape[0] // depth

    def packed_shape(per, size, parts=1):
        shape = (count, 3 * per * parts, LANES) if per else (3, size // LANES, LANES)
        return jax.ShapeDtypeStruct(shape, f32)

    up = [(i, i + 1) for i in range(count - 1)]
    down = [(i + 1, i) for i in range(count - 1)]

    field = in_hbm(mesh_before)
    side = pltpu.VMEM((comps * 2 * height + count_rows, depth), f32)
    node_rows = send_node.reshape(-1, LANES)
    small = (
        receive_vertex.reshape(-1, LANES),
        member_slot,
        unity_weight,
        result_pick.reshape(-1, LANES),
        jnp.transpose(source_coord, (1, 0, 2)),
        jnp.transpose(target_coord, (1, 0, 2)),
    )
    outgoing, head, tail, vertices, slots, weight, picks, source, target = pl.pallas_call(
        lambda *refs: pick_body(*refs, per=send_per),
        out_shape=(packed_shape(send_per, send_node.shape[0]), side, side)
        + tuple(pltpu.VMEM(x.shape, x.dtype) for x in small),
        in_specs=[HBM] * 9,
        out_specs=(VMEM,) * 9,
        scratch_shapes=[
            pltpu.VMEM(displacement.shape, f32),
            pltpu.VMEM(node_rows.shape, jnp.int32),
            pltpu.SemaphoreType.DMA((8,)),
            pltpu.SemaphoreType.DMA((2, comps, 2)),
        ],
        compiler_params=params(4),
        name="pick_nodes",
    )(in_hbm(displacement), in_hbm(node_rows), field, *map(in_hbm, small))
    arrived = exchange(outgoing, send_per, send_cap)
    halo_left = lax.ppermute(tail, "dev", up)
    halo_right = lax.ppermute(head, "dev", down)

    outgoing_results = pl.pallas_call(
        lambda *refs: result_body(*refs, per_in=send_per, per_out=result_per),
        out_shape=packed_shape(result_per, result_pick.shape[0], 3),
        in_specs=[VMEM] * 4 + [HBM] + [VMEM] * 2,
        out_specs=VMEM,
        scratch_shapes=[
            pltpu.VMEM(inverse_part.shape, bf16),
            pltpu.VMEM((clusters, verts // LANES, points, LANES), bf16),
            pltpu.VMEM((clusters, verts // LANES, points, LANES), bf16),
            pltpu.VMEM((clusters, SUB, points), f32),
            pltpu.VMEM((clusters, SUB, verts), f32),
            pltpu.SemaphoreType.DMA((clusters,)),
        ],
        compiler_params=params(40),
        name="cluster_results",
    )(arrived, slots, source, target, in_hbm(inverse_part), weight, picks)
    returned = exchange(outgoing_results, result_per, result_cap, True)

    edges = jnp.stack([place, count - 1 - place]).astype(jnp.int32)
    turns = 4
    if width % turns or width < 2 * turns or depth % (2 * WIDE) or height % TALL or tiles > TALL:
        raise ValueError("mesh shape")

    def with_sums(body):
        places = 12 * (depth // WIDE // 2)
        sums = tuple(tuple(pltpu.ACC(unit)((TALL, WIDE), f32) for _ in range(places)) for unit in range(2))
        return lambda *refs: pl.run_scoped(lambda *sums: body(*refs, sums), *sums)

    tall = height + 2 * SUB
    base = pl.pallas_call(
        with_sums(mesh_body),
        out_shape=jax.ShapeDtypeStruct(mesh_before.shape, f32),
        in_specs=[ANY, HBM],
        out_specs=HBM,
        scratch_shapes=[
            pltpu.VMEM((comps, width, tiles, tall, LANES), f32),
            tuple(pltpu.VMEM((tiles, tall, LANES), f32) for _ in range(turns)),
            pltpu.VMEM((2 * turns, height, depth), f32),
            pltpu.SemaphoreType.DMA((comps, width // turns, tiles)),
            pltpu.SemaphoreType.DMA((2 * turns,)),
        ],
        compiler_params=params(20),
        name="sweeps",
    )(outgoing_results, field)

    swept = pl.pallas_call(
        with_sums(edges_body),
        out_shape=jax.ShapeDtypeStruct(mesh_before.shape, f32),
        in_specs=[HBM, SMEM, HBM, ANY, ANY],
        out_specs=HBM,
        scratch_shapes=[
            pltpu.VMEM((comps, 2, 6, tiles, tall, LANES), f32),
            tuple(tuple(pltpu.VMEM((tiles, tall, LANES), f32) for _ in range(4)) for _ in range(2)),
            pltpu.VMEM((comps, 4, height, depth), f32),
            pltpu.SemaphoreType.DMA((comps, tiles, 2, 3)),
            pltpu.SemaphoreType.DMA((comps, 2, 2)),
        ],
        input_output_aliases={0: 0},
        compiler_params=params(20),
        name="edges",
    )(in_hbm(base), edges, field, halo_left, halo_right)

    slot_rows = receive_vertex.shape[0] // LANES
    size = width * (depth // WIDE)
    return pl.pallas_call(
        lambda *refs: finish_body(*refs, per=result_per),
        out_shape=jax.ShapeDtypeStruct(mesh_before.shape, f32),
        in_specs=[HBM, VMEM, VMEM, ANY, ANY],
        out_specs=HBM,
        scratch_shapes=[
            pltpu.VMEM((comps, width, SUB, depth), f32),
            pltpu.VMEM((count_rows, depth), f32),
            pltpu.VMEM((count_rows, depth), f32),
            pltpu.VMEM((2,) + returned.shape, f32),
            pltpu.VMEM((slot_rows, LANES), f32),
            pltpu.VMEM((slot_rows, LANES), f32),
            pltpu.VMEM((slot_rows, 2 * comps * max(size, TALL), LANES), bf16),
            pltpu.VMEM((slot_rows, WIDE, LANES), bf16),
            pltpu.SemaphoreType.DMA((2 * comps + 2,)),
        ],
        input_output_aliases={0: 0},
        compiler_params=params(24),
        name="finish",
    )(in_hbm(swept), returned, vertices, halo_left, halo_right)


def solution(mesh):
    in_specs = (
        P(None, "dev"),
        P("dev"),
        P("dev", None),
        P("dev", None, None),
        P("dev", None, None),
        P("dev", None, None),
        P("dev", None),
        P("dev"),
        P("dev"),
        P(None, "dev", None, None),
    )
    out_specs = P(None, "dev", None, None)

    return jax.shard_map(local, mesh=mesh, in_specs=in_specs, out_specs=out_specs, check_vma=False)
```

```python
import math

import jax
import jax.numpy as jnp
from jax import lax
from jax.experimental import pallas as pl
from jax.experimental.pallas import tpu as pltpu
from jax.sharding import PartitionSpec as P


LANES = 128
SUB = 8
TALL = 16
WIDE = 256
share = 0.8 / 6.0
keep = 0.2 / share
sharpness = 8.0
VMEM = pl.BlockSpec(memory_space=pltpu.VMEM)
ANY = pl.BlockSpec(memory_space=pl.ANY)
HBM = pl.BlockSpec(memory_space=pltpu.HBM)
SMEM = pl.BlockSpec(memory_space=pltpu.SMEM)
f32 = jnp.float32
bf16 = jnp.bfloat16


def in_hbm(value):
    return pltpu.with_memory_space_constraint(value, pltpu.HBM)


def params(limit, **more):
    return pltpu.CompilerParams(vmem_limit_bytes=limit << 20, **more)


def lane_gather(row, lane):
    return jnp.take_along_axis(row, lane, axis=1, mode="promise_in_bounds")


def gather_rows(row_of, blocks, index_of, groups):
    index = [index_of(g) for g in range(groups)]
    high = [lax.shift_right_arithmetic(i, 7) for i in index]
    low = [jnp.bitwise_and(i, LANES - 1) for i in index]
    out = [[jnp.zeros((SUB, LANES), f32) for _ in range(3)] for _ in range(groups)]
    for block in range(blocks):
        rows = [jnp.broadcast_to(row_of(k, block), (SUB, LANES)) for k in range(3)]
        for g in range(groups):
            here = high[g] == block
            for k in range(3):
                out[g][k] = jnp.where(here, lane_gather(rows[k], low[g]), out[g][k])
    return out


def slot_row(ref, k, row, per, group=0):
    if per:
        at = group * 3 * per + k * per + row % per
        return ref[row // per, at : at + 1, :]
    return ref[group * 3 + k, row : row + 1, :]


def store_rows(out_ref, g, values, per, beside=False):
    for k in range(3):
        for s in range(SUB):
            row = g * SUB + s
            value = values[k][s : s + 1, :]
            if per:
                d, at = row // per, k * per + row % per
                out_ref[d, at : at + 1, :] = value
                if beside and d + 1 < out_ref.shape[0]:
                    out_ref[d + 1, 3 * per + at : 3 * per + at + 1, :] = value
                if beside and d > 0:
                    out_ref[d - 1, 6 * per + at : 6 * per + at + 1, :] = value
            else:
                out_ref[k, row : row + 1, :] = value


def pick_body(
    table_hbm, index_hbm, mesh_ref, vertex_hbm, slot_hbm, weight_hbm, pick_hbm, source_hbm, target_hbm,
    out_ref, head_out, tail_out, vertex_ref, slot_ref, weight_ref, pick_ref, source_ref, target_ref,
    table_ref, index_ref, head, tail, sems, side_sems, *, per,
):
    comps, width, height, depth = mesh_ref.shape
    tiles = depth // LANES
    pairs = (
        (index_hbm, index_ref), (table_hbm, table_ref), (vertex_hbm, vertex_ref), (slot_hbm, slot_ref),
        (weight_hbm, weight_ref), (pick_hbm, pick_ref), (source_hbm, source_ref), (target_hbm, target_ref),
    )
    needed = [pltpu.make_async_copy(a, b, sems.at[i]) for i, (a, b) in enumerate(pairs)]
    side = []
    for k in range(comps):
        for p in range(2):
            rows = pl.ds((k * 2 + p) * height, height)
            side.append(pltpu.make_async_copy(mesh_ref.at[k, p], head.at[rows], side_sems.at[0, k, p]))
            side.append(
                pltpu.make_async_copy(mesh_ref.at[k, width - 2 + p], tail.at[rows], side_sems.at[1, k, p])
            )
    for copy in needed[:3] + side + needed[3:]:
        copy.start()
    for copy in needed[:2]:
        copy.wait()
    groups = index_ref.shape[0] // SUB
    blocks = table_ref.shape[1] // LANES
    half = max(1, groups // 2)
    for first in range(0, groups, half):
        got = gather_rows(
            lambda k, b: table_ref[k : k + 1, b * LANES : (b + 1) * LANES],
            blocks,
            lambda g: index_ref[(first + g) * SUB : (first + g + 1) * SUB, :],
            half,
        )
        for g in range(half):
            store_rows(out_ref, first + g, got[g], per)
        if first == 0:
            needed[2].wait()
            start = comps * 2 * height
            for row in range(vertex_ref.shape[0]):
                value = vertex_ref[row : row + 1, :].astype(f32)
                at, j = start + row // tiles, row % tiles * LANES
                head[at : at + 1, j : j + LANES] = value
                tail[at : at + 1, j : j + LANES] = value
            for copy in side:
                copy.wait()
            leave = [
                pltpu.make_async_copy(head, head_out, sems.at[8]),
                pltpu.make_async_copy(tail, tail_out, sems.at[9]),
            ]
            for copy in leave:
                copy.start()
    for copy in needed[3:] + leave:
        copy.wait()


def pieces(value, count=3):
    found = []
    for _ in range(count):
        top = value.astype(bf16).astype(f32)
        found.append(top)
        value = value - top
    return found


def factor(points, target):
    square = points * points
    norm = jnp.broadcast_to(jnp.sum(square, axis=0, keepdims=True), square.shape)
    row = lax.broadcasted_iota(jnp.int32, square.shape, 0)
    a, b, c = pieces(norm)
    p, q, r = pieces(points)
    if target:
        edge = jnp.where(row < 3, -1.0, jnp.where(row == 3, -a, jnp.where(row == 4, -b, jnp.where(row == 5, -c, 0.0))))
        blocks = [2.0 * p, 2.0 * q, 2.0 * p, 2.0 * q, 2.0 * r, 2.0 * p, edge]
    else:
        edge = jnp.where(row == 0, a, jnp.where(row == 1, b, jnp.where(row == 2, c, jnp.where(row < 6, 1.0, 0.0))))
        blocks = [p, p, q, q, p, r, edge]
    blocks.append(jnp.zeros(square.shape, f32))
    return jnp.concatenate(blocks, axis=0)


def rbf_factors(source, target):
    scale = math.sqrt(sharpness * math.log2(math.e))

    def centred(rows):
        blank = jnp.zeros((SUB - 3, rows[0].shape[1]), f32)
        return jnp.concatenate([(row - 0.5) * scale for row in rows] + [blank], axis=0)

    return jnp.transpose(factor(centred(source), False)).astype(bf16), factor(centred(target), True).astype(bf16)


def result_body(
    arrived_ref, slot_ref, source_ref, target_ref, inverse_ref, weight_ref, pick_ref,
    out_ref, inverse, members, results, sems, *, per_in, per_out,
):
    clusters, points = slot_ref.shape
    verts = weight_ref.shape[1]
    blocks = (arrived_ref.shape[0] * per_in) if per_in else arrived_ref.shape[1]
    per_cluster = verts // LANES
    groups = pick_ref.shape[0] // SUB
    fold = points // LANES // SUB
    copies = [pltpu.make_async_copy(inverse_ref.at[c], inverse.at[c], sems.at[c]) for c in range(clusters)]
    for copy in copies:
        copy.start()
    members[...] = jnp.zeros(members.shape, f32)

    def gather_members(c):
        got = gather_rows(
            lambda k, b: slot_row(arrived_ref, k, b, per_in),
            blocks,
            lambda g: jnp.concatenate(
                [slot_ref[c : c + 1, (g * SUB + j) * LANES : (g * SUB + j + 1) * LANES] for j in range(SUB)], axis=0
            ),
            fold,
        )
        for g in range(fold):
            for j in range(SUB):
                at = (g * SUB + j) * LANES
                for k in range(3):
                    members[c, k : k + 1, at : at + LANES] = got[g][k][j : j + 1, :]

    def evaluate(c):
        turned, right = rbf_factors(*(tuple(ref[k, c : c + 1, :] for k in range(3)) for ref in (source_ref, target_ref)))

        def block(at):
            value = jnp.exp2(jnp.dot(turned[at : at + WIDE], right, preferred_element_type=f32))
            high = value.astype(bf16)
            return high, (value - high.astype(f32)).astype(bf16)

        ready = block(0)
        mine = members[c]
        copies[c].wait()
        coupling = lax.dot_general(
            mine.astype(bf16), inverse[c], (((1,), (1,)), ((), ())), preferred_element_type=f32
        )
        coefficient = mine + coupling
        c_high = coefficient.astype(bf16)
        c_low = (coefficient - c_high.astype(f32)).astype(bf16)
        both = jnp.concatenate([c_high, c_low], axis=0)
        first = jnp.zeros((2 * SUB, verts), f32)
        second = jnp.zeros((SUB, verts), f32)
        for at in range(0, points, WIDE):
            high, low = ready
            if at + WIDE < points:
                ready = block(at + WIDE)
            first = first + jnp.dot(both[:, at : at + WIDE], high, preferred_element_type=f32)
            second = second + jnp.dot(c_high[:, at : at + WIDE], low, preferred_element_type=f32)
        total = first[:SUB] + (first[SUB:] + second)
        results[c] = total * weight_ref[c : c + 1, :]

    for c in range(clusters):
        gather_members(c)
        evaluate(c)
    if per_out:
        blank = jnp.zeros((3 * per_out, LANES), f32)
        out_ref[0, 3 * per_out : 6 * per_out, :] = blank
        out_ref[out_ref.shape[0] - 1, 6 * per_out : 9 * per_out, :] = blank
    half = max(1, groups // 2)
    for start in range(0, groups, half):
        got = gather_rows(
            lambda k, b: results[
                b // per_cluster, k : k + 1, (b % per_cluster) * LANES : (b % per_cluster + 1) * LANES
            ],
            clusters * per_cluster,
            lambda g: pick_ref[(start + g) * SUB : (start + g + 1) * SUB, :],
            half,
        )
        for g in range(half):
            store_rows(out_ref, start + g, got[g], per_out, True)


def columns(j):
    return pl.ds(j * LANES, LANES)


def start_band(sums):
    line = lax.broadcasted_iota(jnp.int32, (WIDE, WIDE), 0)
    column = lax.broadcasted_iota(jnp.int32, (WIDE, WIDE), 1)
    apart = jnp.abs(line - column)
    band = jnp.where(apart == 0, keep, jnp.where(apart == 1, 1.0, 0.0)).astype(bf16)
    ends = []
    for unit in range(len(sums)):
        pltpu.matmul_push_rhs(band, 0, unit)
        pltpu.matmul_acc_lhs(sums[unit][0], jnp.zeros((TALL, WIDE), bf16), load_staged_rhs=0)
        ends.append(pltpu.matmul_pop(sums[unit][0]))
    return ends


def sweep_planes(jobs, height, depth, sums):
    tiles, strips = depth // LANES, height // TALL
    wides, part = depth // WIDE, WIDE // LANES
    units = len(sums)
    halves = wides // units
    lane = lax.broadcasted_iota(jnp.int32, (TALL, LANES), 1)
    row = lax.broadcasted_iota(jnp.int32, (TALL, LANES), 0)

    def place(spot, h):
        return sums[h % units][spot * halves + h // units]

    def multiply(todo):
        later = []
        for center, y, spot in todo:
            for h in range(wides):
                value = jnp.concatenate(
                    [center[j, pl.ds(SUB + y * TALL, TALL), :] for j in range(h * part, (h + 1) * part)], axis=1
                )
                high = value.astype(bf16)
                pltpu.matmul_acc_lhs(place(spot, h), high)
                later.append((place(spot, h), (value - high.astype(f32)).astype(bf16)))
        for total, low in later:
            pltpu.matmul_acc_lhs(total, low)

    def complete(center, before, after, y, spot, put):
        at = SUB + y * TALL
        beside = [pltpu.matmul_pop(place(spot, h)) for h in range(wides)]
        for j in range(tiles):
            lower = center[j, pl.ds(at - 1, TALL), :]
            if y == 0:
                lower = jnp.where(row < 2, 0.0, lower)
            near = (before[j, pl.ds(at, TALL), :] + after[j, pl.ds(at, TALL), :]) + (
                center[j, pl.ds(at + 1, TALL), :] + lower
            )
            h, p = j // part, j % part
            value = near + beside[h][:, p * LANES : (p + 1) * LANES]
            if p == 0 and h:
                value = value + jnp.where(lane == 0, pltpu.roll(center[j - 1, pl.ds(at, TALL), :], 1, 1), 0.0)
            if p == part - 1 and j + 1 < tiles:
                other = pltpu.roll(center[j + 1, pl.ds(at, TALL), :], LANES - 1, 1)
                value = value + jnp.where(lane == LANES - 1, other, 0.0)
            if y == 0:
                value = jnp.where(row == 0, 0.0, value)
            put(j, y, value)

    group = 3
    for y in range(0, strips + group, group):
        base = y // group % 2 * 2 * group
        if y < strips:
            multiply([(job[0], y + n, base + n * 2 + i) for n in range(group) for i, job in enumerate(jobs)])
        if y >= group:
            for n in range(group):
                for i, (center, before, after, put) in enumerate(jobs):
                    complete(center, before, after, y - group + n, 2 * group - base + n * 2 + i, put)


def mesh_body(_, mesh_ref, out_ref, kept_out, field, ring, stage, kept, in_sems, out_sems, kept_sems, sums):
    comps, width, height, depth = mesh_ref.shape
    tiles = depth // LANES
    turns = len(ring)
    quads = width // turns - 1

    def load(k, b):
        return [
            pltpu.make_async_copy(
                mesh_ref.at[k, pl.ds(b * turns, turns), :, columns(j)],
                field.at[k, pl.ds(b * turns, turns), j, pl.ds(SUB, height), :],
                in_sems.at[k, b, j],
            )
            for j in range(tiles)
        ]

    for k in range(comps):
        for b in range(width // turns):
            for copy in load(k, b):
                copy.start()

    blank = jnp.zeros((SUB, LANES), f32)
    for j in range(tiles):
        for plane in ring:
            plane[j, SUB + height : 2 * SUB + height, :] = blank

    def clear(i, _):
        for j in range(tiles):
            field[i // width, i % width, j, SUB + height : 2 * SUB + height, :] = blank
        return 0

    lax.fori_loop(0, comps * width, clear, 0)
    for unit, value in enumerate(start_band(sums)):
        stage[unit, 0:TALL, 0:WIDE] = value

    def flush(k, x, slot):
        return pltpu.make_async_copy(stage.at[slot], out_ref.at[k, x], out_sems.at[slot])

    def keep_planes(k):
        return pltpu.make_async_copy(kept.at[k], kept_out.at[k], kept_sems.at[k])

    def work(k, x, phase, slot=None, copy_to=None):
        def put_first(j, y, value):
            ring[phase % turns][j, pl.ds(SUB + y * TALL, TALL), :] = value
            if copy_to is not None:
                kept[k, copy_to, j, pl.ds(y * TALL, TALL), :] = value

        def put_second(j, y, value):
            stage[slot, y * TALL : (y + 1) * TALL, j * LANES : (j + 1) * LANES] = value * (share * share)

        jobs = [(field.at[k, x], field.at[k, x - 1], field.at[k, x + 1], put_first)]
        if slot is not None:
            jobs.append((ring[(phase - 2) % turns], ring[(phase - 3) % turns], ring[(phase - 1) % turns], put_second))
        sweep_planes(jobs, height, depth, sums)

    def component(k, _):
        for b in range(2):
            for copy in load(k, b):
                copy.wait()
        for phase in range(3):
            work(k, phase + 1, phase, None, phase if phase < 2 else None)

        def quad(i, _):
            @pl.when(i + 2 < width // turns)
            def _():
                for copy in load(k, i + 2):
                    copy.wait()

            turn = k * quads + i
            slots = (turn % 2) * turns

            @pl.when(turn >= 2)
            def _():
                for sub in range(turns):
                    flush(k, 0, slots + sub).wait()

            for sub in range(turns):
                place = {1: 2, 2: 3}.get(sub)
                work(k, jnp.minimum(i * turns + sub + 4, width - 2), sub + 3, slots + sub, place)
            for sub in range(turns):
                flush(k, i * turns + sub + 2, slots + sub).start()
            return 0

        lax.fori_loop(0, quads, quad, 0)
        keep_planes(k).start()
        return 0

    lax.fori_loop(0, comps, component, 0)
    for slot in range(2 * turns):
        flush(0, 0, slot).wait()
    for k in range(comps):
        keep_planes(k).wait()


def edges_body(
    base_ref, edge_ref, mesh_ref, kept_ref, left_ref, right_ref, out_ref,
    field, fetched, computed, stage, in_sems, kept_sems, out_sems, sums,
):
    comps, width, height, depth = mesh_ref.shape
    tiles = depth // LANES

    def outer(k):
        found = []
        for side, ref in enumerate((left_ref, right_ref)):
            own, other = (2, 0) if side == 0 else (0, 2)
            for j in range(tiles):
                found.append(
                    pltpu.make_async_copy(
                        mesh_ref.at[k, pl.ds(side * (width - 2), 2), :, columns(j)],
                        field.at[k, side, pl.ds(own, 2), j, pl.ds(SUB, height), :],
                        in_sems.at[k, j, side, 0],
                    )
                )
                for p in range(2):
                    found.append(
                        pltpu.make_async_copy(
                            ref.at[pl.ds((k * 2 + p) * height, height), columns(j)],
                            field.at[k, side, other + p, j, pl.ds(SUB, height), :],
                            in_sems.at[k, j, side, 1 + p],
                        )
                    )
            for p in range(2):
                found.append(
                    pltpu.make_async_copy(
                        kept_ref.at[k, side * 2 + p],
                        fetched.at[k, side, p, :, pl.ds(SUB, height), :],
                        kept_sems.at[k, side, p],
                    )
                )
        return found

    for k in range(comps):
        for copy in outer(k):
            copy.start()

    blank = jnp.zeros((SUB, LANES), f32)
    for j in range(tiles):
        for place in computed:
            place[j, SUB + height : 2 * SUB + height, :] = blank

    def clear(i, _):
        for side in range(2):
            for j in range(tiles):
                for p in range(4):
                    field[i, side, p, j, SUB + height : 2 * SUB + height, :] = blank
                for p in range(2):
                    fetched[i, side, p, j, SUB + height : 2 * SUB + height, :] = blank
        return 0

    lax.fori_loop(0, comps, clear, 0)
    for unit, value in enumerate(start_band(sums)):
        stage[0, unit, 0:TALL, 0:WIDE] = value
    gates = [jnp.where(edge_ref[side] == 0, 0.0, 1.0) for side in range(2)]

    def save(k):
        return [
            pltpu.make_async_copy(
                stage.at[k, side * 2 + p],
                out_ref.at[k, side * (width - 2) + p],
                out_sems.at[k, side, p],
            )
            for side in range(2)
            for p in range(2)
        ]

    def component(k, _):
        for copy in outer(k):
            copy.wait()
        swept = (
            (computed[0], computed[1], fetched.at[k, 0, 0], fetched.at[k, 0, 1]),
            (fetched.at[k, 1, 0], fetched.at[k, 1, 1], computed[2], computed[3]),
        )
        for p in range(2):
            jobs = []
            for side in range(2):

                def put(j, y, value, side=side):
                    if p == side:
                        value = value * gates[side]
                    computed[side * 2 + p][j, pl.ds(SUB + y * TALL, TALL), :] = value

                jobs.append((field.at[k, side, p + 1], field.at[k, side, p], field.at[k, side, p + 2], put))
            sweep_planes(jobs, height, depth, sums)
        for p in range(2):
            jobs = []
            for side in range(2):

                def put(j, y, value, side=side):
                    value = value * (share * share)
                    span = slice(j * LANES, (j + 1) * LANES)
                    stage[k, side * 2 + p, y * TALL : (y + 1) * TALL, span] = value

                jobs.append((swept[side][p + 1], swept[side][p], swept[side][p + 2], put))
            sweep_planes(jobs, height, depth, sums)
        for copy in save(k):
            copy.start()
        return 0

    lax.fori_loop(0, comps, component, 0)
    for k in range(comps):
        for copy in save(k):
            copy.wait()


def finish_body(
    base_ref, returned_ref, vertex_ref, left_ref, right_ref, out_ref,
    wall, left, right, split, high_sc, low_sc, rows_sc, ones_sc, sems, *, per,
):
    comps, width, _, depth = wall.shape
    tiles = depth // LANES
    rows = vertex_ref.shape[0]
    count = left.shape[0]
    start = left_ref.shape[0] - count
    fetch = [pltpu.make_async_copy(base_ref.at[k, :, pl.ds(0, SUB), :], wall.at[k], sems.at[k]) for k in range(comps)]
    beside = [
        pltpu.make_async_copy(left_ref.at[pl.ds(start, count), :], left, sems.at[comps]),
        pltpu.make_async_copy(right_ref.at[pl.ds(start, count), :], right, sems.at[comps + 1]),
    ]
    for copy in beside + fetch:
        copy.start()
    whole = returned_ref[...]
    top = whole.astype(bf16).astype(f32)
    split[0] = top
    split[1] = whole - top
    for copy in beside:
        copy.wait()

    def spread(row, size):
        tile = jnp.broadcast_to(row, (TALL, LANES)).astype(bf16)
        return jnp.concatenate([tile] * (size // TALL), axis=0)

    def lines(size):
        return lax.broadcasted_iota(jnp.int32, (size, LANES), 0)

    def gathered(vertices, group, home, lows):
        size = home.shape[0]
        shift = lows.bit_length() - 1
        vertices = jnp.concatenate(vertices, axis=0) if isinstance(vertices, list) else vertices
        high_sc[...] = lax.shift_right_arithmetic(vertices, shift).astype(f32)
        low_sc[...] = jnp.bitwise_and(vertices, lows - 1).astype(f32)
        home = home.astype(f32).astype(bf16)
        line = lines(lows).astype(f32).astype(bf16)
        one = jnp.ones((lows, LANES), bf16)
        nothing = jnp.zeros((lows, LANES), bf16)
        empty = jnp.zeros((size, LANES), bf16)
        for row in range(rows):
            match = line == spread(low_sc[row : row + 1, :], lows)
            ones_sc[row, :lows] = jnp.where(match, one, nothing)
            here = home == spread(high_sc[row : row + 1, :], size)
            for term in range(2):
                for k in range(comps):
                    value = spread(slot_row(split.at[term], k, row, per, group), size)
                    at = (term * comps + k) * size
                    rows_sc[row, at : at + size] = jnp.where(here, value, empty)
        total = lax.dot_general(
            jnp.concatenate([rows_sc[row, : 2 * comps * size] for row in range(rows)], axis=1),
            jnp.concatenate([ones_sc[row, :lows] for row in range(rows)], axis=1),
            (((1,), (1,)), ((), ())),
            preferred_element_type=f32,
        )
        total = total[: comps * size] + total[comps * size :]
        return [total[k * size : (k + 1) * size] for k in range(comps)]

    blocks = depth // WIDE
    line = lines(width * blocks)
    own = gathered(vertex_ref[...], 0, (line % width) * blocks + line // width, WIDE)
    line = lines(TALL)

    def unfold(ref):
        return [ref[at : at + 1, j * LANES : (j + 1) * LANES].astype(jnp.int32) for at in range(count) for j in range(tiles)]

    last = gathered(unfold(left), 1, jnp.where(line < tiles, (width - 1) * tiles + line, -1), LANES)
    first = gathered(unfold(right), 2, jnp.where(line < tiles, line, -1), LANES)

    lane = lax.broadcasted_iota(jnp.int32, (width, LANES), 1)
    line = lax.broadcasted_iota(jnp.int32, (width, LANES), 0)
    row = lax.broadcasted_iota(jnp.int32, (SUB, LANES), 0)
    flush = [pltpu.make_async_copy(wall.at[k], out_ref.at[k, :, pl.ds(0, SUB), :], sems.at[comps + 2 + k]) for k in range(comps)]
    per_wide = WIDE // LANES
    for k in range(comps):
        parts = []
        for j in range(tiles):
            block, lanes = j // per_wide * width, j % per_wide * LANES
            parts.append(own[k][block : block + width, lanes : lanes + LANES])
        down = [pltpu.roll(p, 1, 1) for p in parts]
        up = [pltpu.roll(p, LANES - 1, 1) for p in parts]
        fetch[k].wait()
        for j in range(tiles):
            mid = parts[j]
            back = jnp.where(lane == 0, down[j - 1] if j else 0.0, down[j])
            fore = jnp.where(lane == LANES - 1, up[j + 1] if j + 1 < tiles else 0.0, up[j])
            prev = jnp.where(line == 0, last[k][j : j + 1], pltpu.roll(mid, 1, 0))
            after = jnp.where(line == width - 1, first[k][j : j + 1], pltpu.roll(mid, width - 1, 0))
            near = ((prev + after) + (back + fore)) * (share * share)
            one = mid * (1.2 * share) + near
            two = mid * (share * share)
            span = slice(j * LANES, (j + 1) * LANES)
            for x in range(width):
                add = jnp.where(row == 1, one[x : x + 1], jnp.where(row == 2, two[x : x + 1], 0.0))
                wall[k, x, :, span] = jnp.where(row == 0, mid[x : x + 1], wall[k, x, :, span] + add)
        flush[k].start()
    for copy in flush:
        copy.wait()


def exchange(packed, per, cap, beside=False):
    if per:
        return lax.all_to_all(packed, "dev", split_axis=0, concat_axis=0, tiled=True)
    count = lax.axis_size("dev")
    split = packed.reshape(3, count, cap)
    if beside:
        blank = jnp.zeros((3, 1, cap), f32)
        before = jnp.concatenate([blank, split[:, :-1]], axis=1)
        after = jnp.concatenate([split[:, 1:], blank], axis=1)
        split = jnp.concatenate([split, before, after], axis=0)
    moved = lax.all_to_all(split, "dev", split_axis=1, concat_axis=1, tiled=True)
    return moved.reshape((split.shape[0],) + packed.shape[1:])


def local(
    displacement,
    send_node,
    member_slot,
    inverse_part,
    source_coord,
    target_coord,
    unity_weight,
    result_pick,
    receive_vertex,
    mesh_before,
):
    count = lax.axis_size("dev")
    place = lax.axis_index("dev")
    send_cap = send_node.shape[0] // count
    result_cap = result_pick.shape[0] // count
    send_per = send_cap // LANES if send_cap % LANES == 0 else 0
    result_per = result_cap // LANES if result_cap % LANES == 0 else 0
    clusters, points = member_slot.shape
    verts = unity_weight.shape[1]
    comps, width, height, depth = mesh_before.shape
    tiles = depth // LANES
    count_rows = receive_vertex.shape[0] // depth

    def packed_shape(per, size, parts=1):
        shape = (count, 3 * per * parts, LANES) if per else (3, size // LANES, LANES)
        return jax.ShapeDtypeStruct(shape, f32)

    up = [(i, i + 1) for i in range(count - 1)]
    down = [(i + 1, i) for i in range(count - 1)]

    field = in_hbm(mesh_before)
    side = (comps * 2 * height + count_rows, depth)
    node_rows = send_node.reshape(-1, LANES)
    small = (
        receive_vertex.reshape(-1, LANES),
        member_slot,
        unity_weight,
        result_pick.reshape(-1, LANES),
        jnp.transpose(source_coord, (1, 0, 2)),
        jnp.transpose(target_coord, (1, 0, 2)),
    )
    outgoing, head, tail, vertices, slots, weight, picks, source, target = pl.pallas_call(
        lambda *refs: pick_body(*refs, per=send_per),
        out_shape=(packed_shape(send_per, send_node.shape[0]), pltpu.HBM(side, f32), pltpu.HBM(side, f32))
        + tuple(pltpu.VMEM(x.shape, x.dtype) for x in small),
        in_specs=[HBM] * 9,
        out_specs=(VMEM, HBM, HBM) + (VMEM,) * 6,
        scratch_shapes=[
            pltpu.VMEM(displacement.shape, f32),
            pltpu.VMEM(node_rows.shape, jnp.int32),
            pltpu.VMEM(side, f32),
            pltpu.VMEM(side, f32),
            pltpu.SemaphoreType.DMA((10,)),
            pltpu.SemaphoreType.DMA((2, comps, 2)),
        ],
        compiler_params=params(6),
        name="pick_nodes",
    )(in_hbm(displacement), in_hbm(node_rows), field, *map(in_hbm, small))
    arrived = exchange(outgoing, send_per, send_cap)
    halo_left = lax.ppermute(tail, "dev", up)
    halo_right = lax.ppermute(head, "dev", down)

    edges = jnp.stack([place, count - 1 - place]).astype(jnp.int32)
    turns = 4
    if width % turns or width < 2 * turns or depth % (2 * WIDE) or height % TALL or tiles > TALL:
        raise ValueError("mesh shape")

    def with_sums(body):
        places = 12 * (depth // WIDE // 2)
        sums = tuple(tuple(pltpu.ACC(unit)((TALL, WIDE), f32) for _ in range(places)) for unit in range(2))
        return lambda *refs: pl.run_scoped(lambda *sums: body(*refs, sums), *sums)

    tall = height + 2 * SUB
    outgoing_results = pl.pallas_call(
        lambda *refs: result_body(*refs, per_in=send_per, per_out=result_per),
        out_shape=packed_shape(result_per, result_pick.shape[0], 3),
        in_specs=[VMEM] * 4 + [HBM] + [VMEM] * 2,
        out_specs=VMEM,
        scratch_shapes=[
            pltpu.VMEM(inverse_part.shape, bf16),
            pltpu.VMEM((clusters, SUB, points), f32),
            pltpu.VMEM((clusters, SUB, verts), f32),
            pltpu.SemaphoreType.DMA((clusters,)),
        ],
        compiler_params=params(24),
        name="cluster_results",
    )(arrived, slots, source, target, in_hbm(inverse_part), weight, picks)
    returned = exchange(outgoing_results, result_per, result_cap, True)

    base, kept = pl.pallas_call(
        with_sums(mesh_body),
        out_shape=(
            jax.ShapeDtypeStruct(mesh_before.shape, f32),
            pltpu.HBM((comps, 4, tiles, height, LANES), f32),
        ),
        in_specs=[ANY, HBM],
        out_specs=(HBM, HBM),
        scratch_shapes=[
            pltpu.VMEM((comps, width, tiles, tall, LANES), f32),
            tuple(pltpu.VMEM((tiles, tall, LANES), f32) for _ in range(turns)),
            pltpu.VMEM((2 * turns, height, depth), f32),
            pltpu.VMEM((comps, 4, tiles, height, LANES), f32),
            pltpu.SemaphoreType.DMA((comps, width // turns, tiles)),
            pltpu.SemaphoreType.DMA((2 * turns,)),
            pltpu.SemaphoreType.DMA((comps,)),
        ],
        compiler_params=params(24),
        name="sweeps",
    )(outgoing_results, field)

    outer = pl.pallas_call(
        with_sums(edges_body),
        out_shape=jax.ShapeDtypeStruct(mesh_before.shape, f32),
        in_specs=[HBM, SMEM, HBM, HBM, ANY, ANY],
        out_specs=HBM,
        scratch_shapes=[
            pltpu.VMEM((comps, 2, 4, tiles, tall, LANES), f32),
            pltpu.VMEM((comps, 2, 2, tiles, tall, LANES), f32),
            tuple(pltpu.VMEM((tiles, tall, LANES), f32) for _ in range(4)),
            pltpu.VMEM((comps, 4, height, depth), f32),
            pltpu.SemaphoreType.DMA((comps, tiles, 2, 3)),
            pltpu.SemaphoreType.DMA((comps, 2, 2)),
            pltpu.SemaphoreType.DMA((comps, 2, 2)),
        ],
        input_output_aliases={0: 0},
        compiler_params=params(20),
        name="edges",
    )(in_hbm(base), edges, field, in_hbm(kept), halo_left, halo_right)

    slot_rows = receive_vertex.shape[0] // LANES
    size = width * (depth // WIDE)
    return pl.pallas_call(
        lambda *refs: finish_body(*refs, per=result_per),
        out_shape=jax.ShapeDtypeStruct(mesh_before.shape, f32),
        in_specs=[HBM, VMEM, VMEM, ANY, ANY],
        out_specs=HBM,
        scratch_shapes=[
            pltpu.VMEM((comps, width, SUB, depth), f32),
            pltpu.VMEM((count_rows, depth), f32),
            pltpu.VMEM((count_rows, depth), f32),
            pltpu.VMEM((2,) + returned.shape, f32),
            pltpu.VMEM((slot_rows, LANES), f32),
            pltpu.VMEM((slot_rows, LANES), f32),
            pltpu.VMEM((slot_rows, 2 * comps * max(size, TALL), LANES), bf16),
            pltpu.VMEM((slot_rows, WIDE, LANES), bf16),
            pltpu.SemaphoreType.DMA((2 * comps + 2,)),
        ],
        input_output_aliases={0: 0},
        compiler_params=params(24),
        name="finish",
    )(in_hbm(outer), returned, vertices, halo_left, halo_right)


def solution(mesh):
    in_specs = (
        P(None, "dev"),
        P("dev"),
        P("dev", None),
        P("dev", None, None),
        P("dev", None, None),
        P("dev", None, None),
        P("dev", None),
        P("dev"),
        P("dev"),
        P(None, "dev", None, None),
    )
    out_specs = P(None, "dev", None, None)

    return jax.shard_map(local, mesh=mesh, in_specs=in_specs, out_specs=out_specs, check_vma=False)
```

```python
import math

import jax
import jax.numpy as jnp
from jax import lax
from jax.experimental import pallas as pl
from jax.experimental.pallas import tpu as pltpu
from jax.sharding import PartitionSpec as P


LANES = 128
SUB = 8
TALL = 16
WIDE = 256
share = 0.8 / 6.0
keep = 0.2 / share
sharpness = 8.0
VMEM = pl.BlockSpec(memory_space=pltpu.VMEM)
ANY = pl.BlockSpec(memory_space=pl.ANY)
HBM = pl.BlockSpec(memory_space=pltpu.HBM)
SMEM = pl.BlockSpec(memory_space=pltpu.SMEM)
f32 = jnp.float32
bf16 = jnp.bfloat16


def in_hbm(value):
    return pltpu.with_memory_space_constraint(value, pltpu.HBM)


def params(limit, **more):
    return pltpu.CompilerParams(vmem_limit_bytes=limit << 20, **more)


def lane_gather(row, lane):
    return jnp.take_along_axis(row, lane, axis=1, mode="promise_in_bounds")


def gather_rows(row_of, blocks, index_of, groups):
    index = [index_of(g) for g in range(groups)]
    high = [lax.shift_right_arithmetic(i, 7) for i in index]
    low = [jnp.bitwise_and(i, LANES - 1) for i in index]
    out = [[jnp.zeros((SUB, LANES), f32) for _ in range(3)] for _ in range(groups)]
    for block in range(blocks):
        rows = [jnp.broadcast_to(row_of(k, block), (SUB, LANES)) for k in range(3)]
        for g in range(groups):
            here = high[g] == block
            for k in range(3):
                out[g][k] = jnp.where(here, lane_gather(rows[k], low[g]), out[g][k])
    return out


def slot_row(ref, k, row, per, group=0):
    if per:
        at = group * 3 * per + k * per + row % per
        return ref[row // per, at : at + 1, :]
    return ref[group * 3 + k, row : row + 1, :]


def store_rows(out_ref, g, values, per, beside=False):
    for k in range(3):
        for s in range(SUB):
            row = g * SUB + s
            value = values[k][s : s + 1, :]
            if per:
                d, at = row // per, k * per + row % per
                out_ref[d, at : at + 1, :] = value
                if beside and d + 1 < out_ref.shape[0]:
                    out_ref[d + 1, 3 * per + at : 3 * per + at + 1, :] = value
                if beside and d > 0:
                    out_ref[d - 1, 6 * per + at : 6 * per + at + 1, :] = value
            else:
                out_ref[k, row : row + 1, :] = value


def pick_body(
    table_hbm, index_hbm, mesh_ref, vertex_hbm, slot_hbm, weight_hbm, pick_hbm, source_hbm, target_hbm,
    out_ref, head_out, tail_out, vertex_ref, slot_ref, weight_ref, pick_ref, source_ref, target_ref,
    table_ref, index_ref, head, tail, sems, side_sems, *, per,
):
    comps, width, height, depth = mesh_ref.shape
    tiles = depth // LANES
    pairs = (
        (index_hbm, index_ref), (table_hbm, table_ref), (vertex_hbm, vertex_ref), (slot_hbm, slot_ref),
        (weight_hbm, weight_ref), (pick_hbm, pick_ref), (source_hbm, source_ref), (target_hbm, target_ref),
    )
    needed = [pltpu.make_async_copy(a, b, sems.at[i]) for i, (a, b) in enumerate(pairs)]
    side, side_out = [], []
    for k in range(comps):
        for p in range(2):
            rows = pl.ds((k * 2 + p) * height, height)
            side_out.append(pltpu.make_async_copy(head.at[rows], head_out.at[rows], side_sems.at[2, k, p]))
            side_out.append(pltpu.make_async_copy(tail.at[rows], tail_out.at[rows], side_sems.at[3, k, p]))
            side.append(pltpu.make_async_copy(mesh_ref.at[k, p], head.at[rows], side_sems.at[0, k, p]))
            side.append(
                pltpu.make_async_copy(mesh_ref.at[k, width - 2 + p], tail.at[rows], side_sems.at[1, k, p])
            )
    for copy in needed[:3] + side + needed[3:]:
        copy.start()
    for copy in needed[:2]:
        copy.wait()
    groups = index_ref.shape[0] // SUB
    blocks = table_ref.shape[1] // LANES
    half = max(1, groups // 2)
    for first in range(0, groups, half):
        got = gather_rows(
            lambda k, b: table_ref[k : k + 1, b * LANES : (b + 1) * LANES],
            blocks,
            lambda g: index_ref[(first + g) * SUB : (first + g + 1) * SUB, :],
            half,
        )
        for g in range(half):
            store_rows(out_ref, first + g, got[g], per)
        if first == 0:
            needed[2].wait()
            start = comps * 2 * height
            for row in range(vertex_ref.shape[0]):
                value = vertex_ref[row : row + 1, :].astype(f32)
                at, j = start + row // tiles, row % tiles * LANES
                head[at : at + 1, j : j + LANES] = value
                tail[at : at + 1, j : j + LANES] = value
            rest = pl.ds(start, head.shape[0] - start)
            leave = [
                pltpu.make_async_copy(head.at[rest], head_out.at[rest], sems.at[8]),
                pltpu.make_async_copy(tail.at[rest], tail_out.at[rest], sems.at[9]),
            ]
            for copy in leave:
                copy.start()
            for before, after in zip(side, side_out):
                before.wait()
                after.start()
            leave = leave + side_out
    for copy in needed[3:] + leave:
        copy.wait()


def pieces(value, count=3):
    found = []
    for _ in range(count):
        top = value.astype(bf16).astype(f32)
        found.append(top)
        value = value - top
    return found


def factor(points, target):
    square = points * points
    norm = jnp.broadcast_to(jnp.sum(square, axis=0, keepdims=True), square.shape)
    row = lax.broadcasted_iota(jnp.int32, square.shape, 0)
    a, b, c = pieces(norm)
    p, q, r = pieces(points)
    if target:
        edge = jnp.where(row < 3, -1.0, jnp.where(row == 3, -a, jnp.where(row == 4, -b, jnp.where(row == 5, -c, 0.0))))
        blocks = [2.0 * p, 2.0 * q, 2.0 * p, 2.0 * q, 2.0 * r, 2.0 * p, edge]
    else:
        edge = jnp.where(row == 0, a, jnp.where(row == 1, b, jnp.where(row == 2, c, jnp.where(row < 6, 1.0, 0.0))))
        blocks = [p, p, q, q, p, r, edge]
    blocks.append(jnp.zeros(square.shape, f32))
    return jnp.concatenate(blocks, axis=0)


def rbf_factors(source, target):
    scale = math.sqrt(sharpness * math.log2(math.e))

    def centred(rows):
        blank = jnp.zeros((SUB - 3, rows[0].shape[1]), f32)
        return jnp.concatenate([(row - 0.5) * scale for row in rows] + [blank], axis=0)

    return jnp.transpose(factor(centred(source), False)).astype(bf16), factor(centred(target), True).astype(bf16)


def result_body(
    arrived_ref, slot_ref, source_ref, target_ref, inverse_ref, weight_ref, pick_ref,
    out_ref, inverse, members, results, sems, *, per_in, per_out,
):
    clusters, points = slot_ref.shape
    verts = weight_ref.shape[1]
    blocks = (arrived_ref.shape[0] * per_in) if per_in else arrived_ref.shape[1]
    per_cluster = verts // LANES
    groups = pick_ref.shape[0] // SUB
    fold = points // LANES // SUB
    copies = [pltpu.make_async_copy(inverse_ref.at[c], inverse.at[c], sems.at[c]) for c in range(clusters)]
    for copy in copies:
        copy.start()
    members[...] = jnp.zeros(members.shape, f32)

    def gather_members(c):
        got = gather_rows(
            lambda k, b: slot_row(arrived_ref, k, b, per_in),
            blocks,
            lambda g: jnp.concatenate(
                [slot_ref[c : c + 1, (g * SUB + j) * LANES : (g * SUB + j + 1) * LANES] for j in range(SUB)], axis=0
            ),
            fold,
        )
        for g in range(fold):
            for j in range(SUB):
                at = (g * SUB + j) * LANES
                for k in range(3):
                    members[c, k : k + 1, at : at + LANES] = got[g][k][j : j + 1, :]

    def evaluate(c):
        turned, right = rbf_factors(*(tuple(ref[k, c : c + 1, :] for k in range(3)) for ref in (source_ref, target_ref)))

        def block(at):
            value = jnp.exp2(jnp.dot(turned[at : at + WIDE], right, preferred_element_type=f32))
            high = value.astype(bf16)
            return high, (value - high.astype(f32)).astype(bf16)

        ready = block(0)
        mine = members[c]
        copies[c].wait()
        coupling = lax.dot_general(
            mine.astype(bf16), inverse[c], (((1,), (1,)), ((), ())), preferred_element_type=f32
        )
        coefficient = mine + coupling
        c_high = coefficient.astype(bf16)
        c_low = (coefficient - c_high.astype(f32)).astype(bf16)
        both = jnp.concatenate([c_high, c_low], axis=0)
        first = jnp.zeros((2 * SUB, verts), f32)
        second = jnp.zeros((SUB, verts), f32)
        for at in range(0, points, WIDE):
            high, low = ready
            if at + WIDE < points:
                ready = block(at + WIDE)
            first = first + jnp.dot(both[:, at : at + WIDE], high, preferred_element_type=f32)
            second = second + jnp.dot(c_high[:, at : at + WIDE], low, preferred_element_type=f32)
        total = first[:SUB] + (first[SUB:] + second)
        results[c] = total * weight_ref[c : c + 1, :]

    for c in range(clusters):
        gather_members(c)
        evaluate(c)
    if per_out:
        blank = jnp.zeros((3 * per_out, LANES), f32)
        out_ref[0, 3 * per_out : 6 * per_out, :] = blank
        out_ref[out_ref.shape[0] - 1, 6 * per_out : 9 * per_out, :] = blank
    half = max(1, groups // 2)
    for start in range(0, groups, half):
        got = gather_rows(
            lambda k, b: results[
                b // per_cluster, k : k + 1, (b % per_cluster) * LANES : (b % per_cluster + 1) * LANES
            ],
            clusters * per_cluster,
            lambda g: pick_ref[(start + g) * SUB : (start + g + 1) * SUB, :],
            half,
        )
        for g in range(half):
            store_rows(out_ref, start + g, got[g], per_out, True)


def columns(j):
    return pl.ds(j * LANES, LANES)


def start_band(sums):
    line = lax.broadcasted_iota(jnp.int32, (WIDE, WIDE), 0)
    column = lax.broadcasted_iota(jnp.int32, (WIDE, WIDE), 1)
    apart = jnp.abs(line - column)
    band = jnp.where(apart == 0, keep, jnp.where(apart == 1, 1.0, 0.0)).astype(bf16)
    ends = []
    for unit in range(len(sums)):
        pltpu.matmul_push_rhs(band, 0, unit)
        pltpu.matmul_acc_lhs(sums[unit][0], jnp.zeros((TALL, WIDE), bf16), load_staged_rhs=0)
        ends.append(pltpu.matmul_pop(sums[unit][0]))
    return ends


def sweep_planes(jobs, height, depth, sums):
    tiles, strips = depth // LANES, height // TALL
    wides, part = depth // WIDE, WIDE // LANES
    units = len(sums)
    halves = wides // units
    lane = lax.broadcasted_iota(jnp.int32, (TALL, LANES), 1)
    row = lax.broadcasted_iota(jnp.int32, (TALL, LANES), 0)

    def place(spot, h):
        return sums[h % units][spot * halves + h // units]

    def multiply(todo):
        later = []
        for center, y, spot in todo:
            for h in range(wides):
                value = jnp.concatenate(
                    [center[j, pl.ds(SUB + y * TALL, TALL), :] for j in range(h * part, (h + 1) * part)], axis=1
                )
                high = value.astype(bf16)
                pltpu.matmul_acc_lhs(place(spot, h), high)
                later.append((place(spot, h), (value - high.astype(f32)).astype(bf16)))
        for total, low in later:
            pltpu.matmul_acc_lhs(total, low)

    def complete(center, before, after, y, spot, put):
        at = SUB + y * TALL
        beside = [pltpu.matmul_pop(place(spot, h)) for h in range(wides)]
        for j in range(tiles):
            lower = center[j, pl.ds(at - 1, TALL), :]
            if y == 0:
                lower = jnp.where(row < 2, 0.0, lower)
            near = (before[j, pl.ds(at, TALL), :] + after[j, pl.ds(at, TALL), :]) + (
                center[j, pl.ds(at + 1, TALL), :] + lower
            )
            h, p = j // part, j % part
            value = near + beside[h][:, p * LANES : (p + 1) * LANES]
            if p == 0 and h:
                value = value + jnp.where(lane == 0, pltpu.roll(center[j - 1, pl.ds(at, TALL), :], 1, 1), 0.0)
            if p == part - 1 and j + 1 < tiles:
                other = pltpu.roll(center[j + 1, pl.ds(at, TALL), :], LANES - 1, 1)
                value = value + jnp.where(lane == LANES - 1, other, 0.0)
            if y == 0:
                value = jnp.where(row == 0, 0.0, value)
            put(j, y, value)

    group = 3
    for y in range(0, strips + group, group):
        base = y // group % 2 * 2 * group
        if y < strips:
            multiply([(job[0], y + n, base + n * 2 + i) for n in range(group) for i, job in enumerate(jobs)])
        if y >= group:
            for n in range(group):
                for i, (center, before, after, put) in enumerate(jobs):
                    complete(center, before, after, y - group + n, 2 * group - base + n * 2 + i, put)


def mesh_body(_, mesh_ref, out_ref, kept_out, field, ring, stage, kept, in_sems, out_sems, kept_sems, sums):
    comps, width, height, depth = mesh_ref.shape
    tiles = depth // LANES
    turns = len(ring)
    quads = width // turns - 1

    def load(k, b):
        return [
            pltpu.make_async_copy(
                mesh_ref.at[k, pl.ds(b * turns, turns), :, columns(j)],
                field.at[k, pl.ds(b * turns, turns), j, pl.ds(SUB, height), :],
                in_sems.at[k, b, j],
            )
            for j in range(tiles)
        ]

    for k in range(comps):
        for b in range(width // turns):
            for copy in load(k, b):
                copy.start()

    blank = jnp.zeros((SUB, LANES), f32)
    for j in range(tiles):
        for plane in ring:
            plane[j, SUB + height : 2 * SUB + height, :] = blank

    def clear(i, _):
        for j in range(tiles):
            field[i // width, i % width, j, SUB + height : 2 * SUB + height, :] = blank
        return 0

    lax.fori_loop(0, comps * width, clear, 0)
    for unit, value in enumerate(start_band(sums)):
        stage[unit, 0:TALL, 0:WIDE] = value

    def flush(k, x, slot):
        return pltpu.make_async_copy(stage.at[slot], out_ref.at[k, x], out_sems.at[slot])

    def keep_planes(k):
        return pltpu.make_async_copy(kept.at[k], kept_out.at[k], kept_sems.at[k])

    def work(k, x, phase, slot=None, copy_to=None):
        def put_first(j, y, value):
            ring[phase % turns][j, pl.ds(SUB + y * TALL, TALL), :] = value
            if copy_to is not None:
                kept[k, copy_to, j, pl.ds(y * TALL, TALL), :] = value

        def put_second(j, y, value):
            stage[slot, y * TALL : (y + 1) * TALL, j * LANES : (j + 1) * LANES] = value * (share * share)

        jobs = [(field.at[k, x], field.at[k, x - 1], field.at[k, x + 1], put_first)]
        if slot is not None:
            jobs.append((ring[(phase - 2) % turns], ring[(phase - 3) % turns], ring[(phase - 1) % turns], put_second))
        sweep_planes(jobs, height, depth, sums)

    def component(k, _):
        for b in range(2):
            for copy in load(k, b):
                copy.wait()
        for phase in range(3):
            work(k, phase + 1, phase, None, phase if phase < 2 else None)

        def quad(i, _):
            @pl.when(i + 2 < width // turns)
            def _():
                for copy in load(k, i + 2):
                    copy.wait()

            turn = k * quads + i
            slots = (turn % 2) * turns

            @pl.when(turn >= 2)
            def _():
                for sub in range(turns):
                    flush(k, 0, slots + sub).wait()

            for sub in range(turns):
                place = {1: 2, 2: 3}.get(sub)
                work(k, jnp.minimum(i * turns + sub + 4, width - 2), sub + 3, slots + sub, place)
            for sub in range(turns):
                flush(k, i * turns + sub + 2, slots + sub).start()
            return 0

        lax.fori_loop(0, quads, quad, 0)
        keep_planes(k).start()
        return 0

    lax.fori_loop(0, comps, component, 0)
    for slot in range(2 * turns):
        flush(0, 0, slot).wait()
    for k in range(comps):
        keep_planes(k).wait()


def edges_body(
    base_ref, edge_ref, mesh_ref, kept_ref, left_ref, right_ref, out_ref,
    field, fetched, computed, stage, in_sems, kept_sems, out_sems, sums,
):
    comps, width, height, depth = mesh_ref.shape
    tiles = depth // LANES

    def outer(k):
        found = []
        for side, ref in enumerate((left_ref, right_ref)):
            own, other = (2, 0) if side == 0 else (0, 2)
            for j in range(tiles):
                found.append(
                    pltpu.make_async_copy(
                        mesh_ref.at[k, pl.ds(side * (width - 2), 2), :, columns(j)],
                        field.at[k, side, pl.ds(own, 2), j, pl.ds(SUB, height), :],
                        in_sems.at[k, j, side, 0],
                    )
                )
                for p in range(2):
                    found.append(
                        pltpu.make_async_copy(
                            ref.at[pl.ds((k * 2 + p) * height, height), columns(j)],
                            field.at[k, side, other + p, j, pl.ds(SUB, height), :],
                            in_sems.at[k, j, side, 1 + p],
                        )
                    )
            for p in range(2):
                found.append(
                    pltpu.make_async_copy(
                        kept_ref.at[k, side * 2 + p],
                        fetched.at[k, side, p, :, pl.ds(SUB, height), :],
                        kept_sems.at[k, side, p],
                    )
                )
        return found

    for k in range(comps):
        for copy in outer(k):
            copy.start()

    blank = jnp.zeros((SUB, LANES), f32)
    for j in range(tiles):
        for place in computed:
            place[j, SUB + height : 2 * SUB + height, :] = blank

    def clear(i, _):
        for side in range(2):
            for j in range(tiles):
                for p in range(4):
                    field[i, side, p, j, SUB + height : 2 * SUB + height, :] = blank
                for p in range(2):
                    fetched[i, side, p, j, SUB + height : 2 * SUB + height, :] = blank
        return 0

    lax.fori_loop(0, comps, clear, 0)
    for unit, value in enumerate(start_band(sums)):
        stage[0, unit, 0:TALL, 0:WIDE] = value
    gates = [jnp.where(edge_ref[side] == 0, 0.0, 1.0) for side in range(2)]

    def save(k):
        return [
            pltpu.make_async_copy(
                stage.at[k, side * 2 + p],
                out_ref.at[k, side * (width - 2) + p],
                out_sems.at[k, side, p],
            )
            for side in range(2)
            for p in range(2)
        ]

    def component(k, _):
        for copy in outer(k):
            copy.wait()
        swept = (
            (computed[0], computed[1], fetched.at[k, 0, 0], fetched.at[k, 0, 1]),
            (fetched.at[k, 1, 0], fetched.at[k, 1, 1], computed[2], computed[3]),
        )
        for p in range(2):
            jobs = []
            for side in range(2):

                def put(j, y, value, side=side):
                    if p == side:
                        value = value * gates[side]
                    computed[side * 2 + p][j, pl.ds(SUB + y * TALL, TALL), :] = value

                jobs.append((field.at[k, side, p + 1], field.at[k, side, p], field.at[k, side, p + 2], put))
            sweep_planes(jobs, height, depth, sums)
        for p in range(2):
            jobs = []
            for side in range(2):

                def put(j, y, value, side=side):
                    value = value * (share * share)
                    span = slice(j * LANES, (j + 1) * LANES)
                    stage[k, side * 2 + p, y * TALL : (y + 1) * TALL, span] = value

                jobs.append((swept[side][p + 1], swept[side][p], swept[side][p + 2], put))
            sweep_planes(jobs, height, depth, sums)
        for copy in save(k):
            copy.start()
        return 0

    lax.fori_loop(0, comps, component, 0)
    for k in range(comps):
        for copy in save(k):
            copy.wait()


def finish_body(
    base_ref, returned_ref, vertex_ref, left_ref, right_ref, out_ref,
    wall, left, right, split, high_sc, low_sc, sems, *, per,
):
    comps, width, _, depth = wall.shape
    tiles = depth // LANES
    rows = vertex_ref.shape[0]
    count = left.shape[0]
    start = left_ref.shape[0] - count
    fetch = [pltpu.make_async_copy(base_ref.at[k, :, pl.ds(0, SUB), :], wall.at[k], sems.at[k]) for k in range(comps)]
    beside = [
        pltpu.make_async_copy(left_ref.at[pl.ds(start, count), :], left, sems.at[comps]),
        pltpu.make_async_copy(right_ref.at[pl.ds(start, count), :], right, sems.at[comps + 1]),
    ]
    for copy in beside + fetch:
        copy.start()
    whole = returned_ref[...]
    top = whole.astype(bf16).astype(f32)
    split[0] = top
    split[1] = whole - top
    for copy in beside:
        copy.wait()

    def spread(row, size):
        tile = jnp.broadcast_to(row, (TALL, LANES)).astype(bf16)
        return jnp.concatenate([tile] * (size // TALL), axis=0)

    def lines(size):
        return lax.broadcasted_iota(jnp.int32, (size, LANES), 0)

    def gathered(vertices, group, home, lows):
        size = home.shape[0]
        shift = lows.bit_length() - 1
        vertices = jnp.concatenate(vertices, axis=0) if isinstance(vertices, list) else vertices
        high_sc[...] = lax.shift_right_arithmetic(vertices, shift).astype(f32)
        low_sc[...] = jnp.bitwise_and(vertices, lows - 1).astype(f32)
        home = home.astype(f32).astype(bf16)
        line = lines(lows).astype(f32).astype(bf16)
        one = jnp.ones((lows, LANES), bf16)
        nothing = jnp.zeros((lows, LANES), bf16)
        empty = jnp.zeros((size, LANES), bf16)
        total = None
        for first in range(0, rows, 4):
            wide, tall = [], []
            for row in range(first, min(rows, first + 4)):
                wide.append(jnp.where(line == spread(low_sc[row : row + 1, :], lows), one, nothing))
                here = home == spread(high_sc[row : row + 1, :], size)
                parts = []
                for term in range(2):
                    for k in range(comps):
                        value = spread(slot_row(split.at[term], k, row, per, group), size)
                        parts.append(jnp.where(here, value, empty))
                tall.append(jnp.concatenate(parts, axis=0))
            part = lax.dot_general(
                jnp.concatenate(tall, axis=1),
                jnp.concatenate(wide, axis=1),
                (((1,), (1,)), ((), ())),
                preferred_element_type=f32,
            )
            total = part if total is None else total + part
        total = total[: comps * size] + total[comps * size :]
        return [total[k * size : (k + 1) * size] for k in range(comps)]

    blocks = depth // WIDE
    line = lines(width * blocks)
    own = gathered(vertex_ref[...], 0, (line % width) * blocks + line // width, WIDE)
    line = lines(TALL)

    def unfold(ref):
        return [ref[at : at + 1, j * LANES : (j + 1) * LANES].astype(jnp.int32) for at in range(count) for j in range(tiles)]

    last = gathered(unfold(left), 1, jnp.where(line < tiles, (width - 1) * tiles + line, -1), LANES)
    first = gathered(unfold(right), 2, jnp.where(line < tiles, line, -1), LANES)

    lane = lax.broadcasted_iota(jnp.int32, (width, LANES), 1)
    line = lax.broadcasted_iota(jnp.int32, (width, LANES), 0)
    row = lax.broadcasted_iota(jnp.int32, (SUB, LANES), 0)
    flush = [pltpu.make_async_copy(wall.at[k], out_ref.at[k, :, pl.ds(0, SUB), :], sems.at[comps + 2 + k]) for k in range(comps)]
    per_wide = WIDE // LANES
    for k in range(comps):
        parts = []
        for j in range(tiles):
            block, lanes = j // per_wide * width, j % per_wide * LANES
            parts.append(own[k][block : block + width, lanes : lanes + LANES])
        down = [pltpu.roll(p, 1, 1) for p in parts]
        up = [pltpu.roll(p, LANES - 1, 1) for p in parts]
        fetch[k].wait()
        for j in range(tiles):
            mid = parts[j]
            back = jnp.where(lane == 0, down[j - 1] if j else 0.0, down[j])
            fore = jnp.where(lane == LANES - 1, up[j + 1] if j + 1 < tiles else 0.0, up[j])
            prev = jnp.where(line == 0, last[k][j : j + 1], pltpu.roll(mid, 1, 0))
            after = jnp.where(line == width - 1, first[k][j : j + 1], pltpu.roll(mid, width - 1, 0))
            near = ((prev + after) + (back + fore)) * (share * share)
            one = mid * (1.2 * share) + near
            two = mid * (share * share)
            span = slice(j * LANES, (j + 1) * LANES)
            for x in range(width):
                add = jnp.where(row == 1, one[x : x + 1], jnp.where(row == 2, two[x : x + 1], 0.0))
                wall[k, x, :, span] = jnp.where(row == 0, mid[x : x + 1], wall[k, x, :, span] + add)
        flush[k].start()
    for copy in flush:
        copy.wait()


def exchange(packed, per, cap, beside=False):
    if per:
        return lax.all_to_all(packed, "dev", split_axis=0, concat_axis=0, tiled=True)
    count = lax.axis_size("dev")
    split = packed.reshape(3, count, cap)
    if beside:
        blank = jnp.zeros((3, 1, cap), f32)
        before = jnp.concatenate([blank, split[:, :-1]], axis=1)
        after = jnp.concatenate([split[:, 1:], blank], axis=1)
        split = jnp.concatenate([split, before, after], axis=0)
    moved = lax.all_to_all(split, "dev", split_axis=1, concat_axis=1, tiled=True)
    return moved.reshape((split.shape[0],) + packed.shape[1:])


def local(
    displacement,
    send_node,
    member_slot,
    inverse_part,
    source_coord,
    target_coord,
    unity_weight,
    result_pick,
    receive_vertex,
    mesh_before,
):
    count = lax.axis_size("dev")
    place = lax.axis_index("dev")
    send_cap = send_node.shape[0] // count
    result_cap = result_pick.shape[0] // count
    send_per = send_cap // LANES if send_cap % LANES == 0 else 0
    result_per = result_cap // LANES if result_cap % LANES == 0 else 0
    clusters, points = member_slot.shape
    verts = unity_weight.shape[1]
    comps, width, height, depth = mesh_before.shape
    tiles = depth // LANES
    count_rows = receive_vertex.shape[0] // depth

    def packed_shape(per, size, parts=1):
        shape = (count, 3 * per * parts, LANES) if per else (3, size // LANES, LANES)
        return jax.ShapeDtypeStruct(shape, f32)

    up = [(i, i + 1) for i in range(count - 1)]
    down = [(i + 1, i) for i in range(count - 1)]

    field = in_hbm(mesh_before)
    side = (comps * 2 * height + count_rows, depth)
    node_rows = send_node.reshape(-1, LANES)
    small = (
        receive_vertex.reshape(-1, LANES),
        member_slot,
        unity_weight,
        result_pick.reshape(-1, LANES),
        jnp.transpose(source_coord, (1, 0, 2)),
        jnp.transpose(target_coord, (1, 0, 2)),
    )
    outgoing, head, tail, vertices, slots, weight, picks, source, target = pl.pallas_call(
        lambda *refs: pick_body(*refs, per=send_per),
        out_shape=(packed_shape(send_per, send_node.shape[0]), pltpu.HBM(side, f32), pltpu.HBM(side, f32))
        + tuple(pltpu.VMEM(x.shape, x.dtype) for x in small),
        in_specs=[HBM] * 9,
        out_specs=(VMEM, HBM, HBM) + (VMEM,) * 6,
        scratch_shapes=[
            pltpu.VMEM(displacement.shape, f32),
            pltpu.VMEM(node_rows.shape, jnp.int32),
            pltpu.VMEM(side, f32),
            pltpu.VMEM(side, f32),
            pltpu.SemaphoreType.DMA((10,)),
            pltpu.SemaphoreType.DMA((4, comps, 2)),
        ],
        compiler_params=params(6),
        name="pick_nodes",
    )(in_hbm(displacement), in_hbm(node_rows), field, *map(in_hbm, small))
    arrived = exchange(outgoing, send_per, send_cap)
    halo_left = lax.ppermute(tail, "dev", up)
    halo_right = lax.ppermute(head, "dev", down)

    edges = jnp.stack([place, count - 1 - place]).astype(jnp.int32)
    turns = 4
    if width % turns or width < 2 * turns or depth % (2 * WIDE) or height % TALL or tiles > TALL:
        raise ValueError("mesh shape")

    def with_sums(body):
        places = 12 * (depth // WIDE // 2)
        sums = tuple(tuple(pltpu.ACC(unit)((TALL, WIDE), f32) for _ in range(places)) for unit in range(2))
        return lambda *refs: pl.run_scoped(lambda *sums: body(*refs, sums), *sums)

    tall = height + 2 * SUB
    outgoing_results = pl.pallas_call(
        lambda *refs: result_body(*refs, per_in=send_per, per_out=result_per),
        out_shape=packed_shape(result_per, result_pick.shape[0], 3),
        in_specs=[VMEM] * 4 + [HBM] + [VMEM] * 2,
        out_specs=VMEM,
        scratch_shapes=[
            pltpu.VMEM(inverse_part.shape, bf16),
            pltpu.VMEM((clusters, SUB, points), f32),
            pltpu.VMEM((clusters, SUB, verts), f32),
            pltpu.SemaphoreType.DMA((clusters,)),
        ],
        compiler_params=params(24),
        name="cluster_results",
    )(arrived, slots, source, target, in_hbm(inverse_part), weight, picks)
    returned = exchange(outgoing_results, result_per, result_cap, True)

    base, kept = pl.pallas_call(
        with_sums(mesh_body),
        out_shape=(
            jax.ShapeDtypeStruct(mesh_before.shape, f32),
            pltpu.HBM((comps, 4, tiles, height, LANES), f32),
        ),
        in_specs=[ANY, HBM],
        out_specs=(HBM, HBM),
        scratch_shapes=[
            pltpu.VMEM((comps, width, tiles, tall, LANES), f32),
            tuple(pltpu.VMEM((tiles, tall, LANES), f32) for _ in range(turns)),
            pltpu.VMEM((2 * turns, height, depth), f32),
            pltpu.VMEM((comps, 4, tiles, height, LANES), f32),
            pltpu.SemaphoreType.DMA((comps, width // turns, tiles)),
            pltpu.SemaphoreType.DMA((2 * turns,)),
            pltpu.SemaphoreType.DMA((comps,)),
        ],
        compiler_params=params(24),
        name="sweeps",
    )(outgoing_results, field)

    outer = pl.pallas_call(
        with_sums(edges_body),
        out_shape=jax.ShapeDtypeStruct(mesh_before.shape, f32),
        in_specs=[HBM, SMEM, HBM, HBM, ANY, ANY],
        out_specs=HBM,
        scratch_shapes=[
            pltpu.VMEM((comps, 2, 4, tiles, tall, LANES), f32),
            pltpu.VMEM((comps, 2, 2, tiles, tall, LANES), f32),
            tuple(pltpu.VMEM((tiles, tall, LANES), f32) for _ in range(4)),
            pltpu.VMEM((comps, 4, height, depth), f32),
            pltpu.SemaphoreType.DMA((comps, tiles, 2, 3)),
            pltpu.SemaphoreType.DMA((comps, 2, 2)),
            pltpu.SemaphoreType.DMA((comps, 2, 2)),
        ],
        input_output_aliases={0: 0},
        compiler_params=params(20),
        name="edges",
    )(in_hbm(base), edges, field, in_hbm(kept), halo_left, halo_right)

    slot_rows = receive_vertex.shape[0] // LANES
    return pl.pallas_call(
        lambda *refs: finish_body(*refs, per=result_per),
        out_shape=jax.ShapeDtypeStruct(mesh_before.shape, f32),
        in_specs=[HBM, VMEM, VMEM, ANY, ANY],
        out_specs=HBM,
        scratch_shapes=[
            pltpu.VMEM((comps, width, SUB, depth), f32),
            pltpu.VMEM((count_rows, depth), f32),
            pltpu.VMEM((count_rows, depth), f32),
            pltpu.VMEM((2,) + returned.shape, f32),
            pltpu.VMEM((slot_rows, LANES), f32),
            pltpu.VMEM((slot_rows, LANES), f32),
            pltpu.SemaphoreType.DMA((2 * comps + 2,)),
        ],
        input_output_aliases={0: 0},
        compiler_params=params(24),
        name="finish",
    )(in_hbm(outer), returned, vertices, halo_left, halo_right)


def solution(mesh):
    in_specs = (
        P(None, "dev"),
        P("dev"),
        P("dev", None),
        P("dev", None, None),
        P("dev", None, None),
        P("dev", None, None),
        P("dev", None),
        P("dev"),
        P("dev"),
        P(None, "dev", None, None),
    )
    out_specs = P(None, "dev", None, None)

    return jax.shard_map(local, mesh=mesh, in_specs=in_specs, out_specs=out_specs, check_vma=False)
```

```python
import math

import jax
import jax.numpy as jnp
from jax import lax
from jax.experimental import pallas as pl
from jax.experimental.pallas import tpu as pltpu
from jax.sharding import PartitionSpec as P


LANES = 128
SUB = 8
TALL = 16
WIDE = 256
share = 0.8 / 6.0
keep = 0.2 / share
sharpness = 8.0
VMEM = pl.BlockSpec(memory_space=pltpu.VMEM)
ANY = pl.BlockSpec(memory_space=pl.ANY)
HBM = pl.BlockSpec(memory_space=pltpu.HBM)
SMEM = pl.BlockSpec(memory_space=pltpu.SMEM)
f32 = jnp.float32
bf16 = jnp.bfloat16


def in_hbm(value):
    return pltpu.with_memory_space_constraint(value, pltpu.HBM)


def params(limit, **more):
    return pltpu.CompilerParams(vmem_limit_bytes=limit << 20, **more)


def lane_gather(row, lane):
    return jnp.take_along_axis(row, lane, axis=1, mode="promise_in_bounds")


def gather_rows(row_of, blocks, index_of, groups):
    index = [index_of(g) for g in range(groups)]
    high = [lax.shift_right_arithmetic(i, 7) for i in index]
    low = [jnp.bitwise_and(i, LANES - 1) for i in index]
    out = [[jnp.zeros((SUB, LANES), f32) for _ in range(3)] for _ in range(groups)]
    for block in range(blocks):
        rows = [jnp.broadcast_to(row_of(k, block), (SUB, LANES)) for k in range(3)]
        for g in range(groups):
            here = high[g] == block
            for k in range(3):
                out[g][k] = jnp.where(here, lane_gather(rows[k], low[g]), out[g][k])
    return out


def slot_row(ref, k, row, per, group=0):
    if per:
        at = group * 3 * per + k * per + row % per
        return ref[row // per, at : at + 1, :]
    return ref[group * 3 + k, row : row + 1, :]


def store_rows(out_ref, g, values, per, beside=False):
    for k in range(3):
        for s in range(SUB):
            row = g * SUB + s
            value = values[k][s : s + 1, :]
            if per:
                d, at = row // per, k * per + row % per
                out_ref[d, at : at + 1, :] = value
                if beside and d + 1 < out_ref.shape[0]:
                    out_ref[d + 1, 3 * per + at : 3 * per + at + 1, :] = value
                if beside and d > 0:
                    out_ref[d - 1, 6 * per + at : 6 * per + at + 1, :] = value
            else:
                out_ref[k, row : row + 1, :] = value


def pick_body(
    table_hbm, index_hbm, mesh_ref, vertex_hbm, slot_hbm, weight_hbm, pick_hbm, source_hbm, target_hbm,
    out_ref, head_out, tail_out, vertex_ref, slot_ref, weight_ref, pick_ref, source_ref, target_ref,
    table_ref, index_ref, head, tail, sems, side_sems, *, per,
):
    comps, width, height, depth = mesh_ref.shape
    tiles = depth // LANES
    pairs = (
        (index_hbm, index_ref), (table_hbm, table_ref), (vertex_hbm, vertex_ref), (slot_hbm, slot_ref),
        (weight_hbm, weight_ref), (pick_hbm, pick_ref), (source_hbm, source_ref), (target_hbm, target_ref),
    )
    needed = [pltpu.make_async_copy(a, b, sems.at[i]) for i, (a, b) in enumerate(pairs)]
    side, side_out = [], []
    for k in range(comps):
        for p in range(2):
            rows = pl.ds((k * 2 + p) * height, height)
            side_out.append(pltpu.make_async_copy(head.at[rows], head_out.at[rows], side_sems.at[2, k, p]))
            side_out.append(pltpu.make_async_copy(tail.at[rows], tail_out.at[rows], side_sems.at[3, k, p]))
            side.append(pltpu.make_async_copy(mesh_ref.at[k, p], head.at[rows], side_sems.at[0, k, p]))
            side.append(
                pltpu.make_async_copy(mesh_ref.at[k, width - 2 + p], tail.at[rows], side_sems.at[1, k, p])
            )
    for copy in needed[:3] + side + needed[3:]:
        copy.start()
    for copy in needed[:2]:
        copy.wait()
    groups = index_ref.shape[0] // SUB
    blocks = table_ref.shape[1] // LANES
    half = max(1, groups // 4)
    for first in range(0, groups, half):
        got = gather_rows(
            lambda k, b: table_ref[k : k + 1, b * LANES : (b + 1) * LANES],
            blocks,
            lambda g: index_ref[(first + g) * SUB : (first + g + 1) * SUB, :],
            half,
        )
        for g in range(half):
            store_rows(out_ref, first + g, got[g], per)
        if first == 0:
            needed[2].wait()
            start = comps * 2 * height
            for row in range(vertex_ref.shape[0]):
                value = vertex_ref[row : row + 1, :].astype(f32)
                at, j = start + row // tiles, row % tiles * LANES
                head[at : at + 1, j : j + LANES] = value
                tail[at : at + 1, j : j + LANES] = value
            rest = pl.ds(start, head.shape[0] - start)
            leave = [
                pltpu.make_async_copy(head.at[rest], head_out.at[rest], sems.at[8]),
                pltpu.make_async_copy(tail.at[rest], tail_out.at[rest], sems.at[9]),
            ]
            for copy in leave:
                copy.start()
            for before, after in zip(side, side_out):
                before.wait()
                after.start()
            leave = leave + side_out
    for copy in needed[3:] + leave:
        copy.wait()


def pieces(value, count=3):
    found = []
    for _ in range(count):
        top = value.astype(bf16).astype(f32)
        found.append(top)
        value = value - top
    return found


def factor(points, target):
    square = points * points
    norm = jnp.broadcast_to(jnp.sum(square, axis=0, keepdims=True), square.shape)
    row = lax.broadcasted_iota(jnp.int32, square.shape, 0)
    a, b, c = pieces(norm)
    p, q, r = pieces(points)
    if target:
        edge = jnp.where(row < 3, -1.0, jnp.where(row == 3, -a, jnp.where(row == 4, -b, jnp.where(row == 5, -c, 0.0))))
        blocks = [2.0 * p, 2.0 * q, 2.0 * p, 2.0 * q, 2.0 * r, 2.0 * p, edge]
    else:
        edge = jnp.where(row == 0, a, jnp.where(row == 1, b, jnp.where(row == 2, c, jnp.where(row < 6, 1.0, 0.0))))
        blocks = [p, p, q, q, p, r, edge]
    blocks.append(jnp.zeros(square.shape, f32))
    return jnp.concatenate(blocks, axis=0)


def rbf_factors(source, target):
    scale = math.sqrt(sharpness * math.log2(math.e))

    def centred(rows):
        blank = jnp.zeros((SUB - 3, rows[0].shape[1]), f32)
        return jnp.concatenate([(row - 0.5) * scale for row in rows] + [blank], axis=0)

    return jnp.transpose(factor(centred(source), False)).astype(bf16), factor(centred(target), True).astype(bf16)


def result_body(
    arrived_ref, slot_ref, source_ref, target_ref, inverse_ref, weight_ref, pick_ref,
    out_ref, inverse, members, results, sems, *, per_in, per_out,
):
    clusters, points = slot_ref.shape
    verts = weight_ref.shape[1]
    blocks = (arrived_ref.shape[0] * per_in) if per_in else arrived_ref.shape[1]
    per_cluster = verts // LANES
    groups = pick_ref.shape[0] // SUB
    fold = points // LANES // SUB
    copies = [pltpu.make_async_copy(inverse_ref.at[c], inverse.at[c], sems.at[c]) for c in range(clusters)]
    for copy in copies:
        copy.start()
    members[...] = jnp.zeros(members.shape, f32)

    def gather_members(c):
        got = gather_rows(
            lambda k, b: slot_row(arrived_ref, k, b, per_in),
            blocks,
            lambda g: jnp.concatenate(
                [slot_ref[c : c + 1, (g * SUB + j) * LANES : (g * SUB + j + 1) * LANES] for j in range(SUB)], axis=0
            ),
            fold,
        )
        for g in range(fold):
            for j in range(SUB):
                at = (g * SUB + j) * LANES
                for k in range(3):
                    members[c, k : k + 1, at : at + LANES] = got[g][k][j : j + 1, :]

    def evaluate(c):
        turned, right = rbf_factors(*(tuple(ref[k, c : c + 1, :] for k in range(3)) for ref in (source_ref, target_ref)))

        def block(at):
            value = jnp.exp2(jnp.dot(turned[at : at + WIDE], right, preferred_element_type=f32))
            high = value.astype(bf16)
            return high, (value - high.astype(f32)).astype(bf16)

        ready = block(0)
        mine = members[c]
        copies[c].wait()
        coupling = lax.dot_general(
            mine.astype(bf16), inverse[c], (((1,), (1,)), ((), ())), preferred_element_type=f32
        )
        coefficient = mine + coupling
        c_high = coefficient.astype(bf16)
        c_low = (coefficient - c_high.astype(f32)).astype(bf16)
        both = jnp.concatenate([c_high, c_low], axis=0)
        first = jnp.zeros((2 * SUB, verts), f32)
        second = jnp.zeros((SUB, verts), f32)
        for at in range(0, points, WIDE):
            high, low = ready
            if at + WIDE < points:
                ready = block(at + WIDE)
            first = first + jnp.dot(both[:, at : at + WIDE], high, preferred_element_type=f32)
            second = second + jnp.dot(c_high[:, at : at + WIDE], low, preferred_element_type=f32)
        total = first[:SUB] + (first[SUB:] + second)
        results[c] = total * weight_ref[c : c + 1, :]

    for c in range(clusters):
        gather_members(c)
        evaluate(c)
    if per_out:
        blank = jnp.zeros((3 * per_out, LANES), f32)
        out_ref[0, 3 * per_out : 6 * per_out, :] = blank
        out_ref[out_ref.shape[0] - 1, 6 * per_out : 9 * per_out, :] = blank
    half = max(1, groups // 2)
    for start in range(0, groups, half):
        got = gather_rows(
            lambda k, b: results[
                b // per_cluster, k : k + 1, (b % per_cluster) * LANES : (b % per_cluster + 1) * LANES
            ],
            clusters * per_cluster,
            lambda g: pick_ref[(start + g) * SUB : (start + g + 1) * SUB, :],
            half,
        )
        for g in range(half):
            store_rows(out_ref, start + g, got[g], per_out, True)


def columns(j):
    return pl.ds(j * LANES, LANES)


def start_band(sums):
    line = lax.broadcasted_iota(jnp.int32, (WIDE, WIDE), 0)
    column = lax.broadcasted_iota(jnp.int32, (WIDE, WIDE), 1)
    apart = jnp.abs(line - column)
    band = jnp.where(apart == 0, keep, jnp.where(apart == 1, 1.0, 0.0)).astype(bf16)
    ends = []
    for unit in range(len(sums)):
        pltpu.matmul_push_rhs(band, 0, unit)
        pltpu.matmul_acc_lhs(sums[unit][0], jnp.zeros((TALL, WIDE), bf16), load_staged_rhs=0)
        ends.append(pltpu.matmul_pop(sums[unit][0]))
    return ends


def sweep_planes(jobs, height, depth, sums, turn):
    tiles, strips = depth // LANES, height // TALL
    wides, part = depth // WIDE, WIDE // LANES
    units = len(sums)
    halves = wides // units
    lane = lax.broadcasted_iota(jnp.int32, (TALL, LANES), 1)
    row = lax.broadcasted_iota(jnp.int32, (TALL, LANES), 0)

    def place(spot, h):
        return sums[h % units][spot * halves + h // units]

    def multiply(todo):
        later = []
        for center, y, spot in todo:
            for h in range(wides):
                value = jnp.concatenate(
                    [center[j, pl.ds(SUB + y * TALL, TALL), :] for j in range(h * part, (h + 1) * part)], axis=1
                )
                high = value.astype(bf16)
                pltpu.matmul_acc_lhs(place(spot, h), high)
                later.append((place(spot, h), (value - high.astype(f32)).astype(bf16)))
        for total, low in later:
            pltpu.matmul_acc_lhs(total, low)

    def complete(center, before, after, y, spot, put):
        at = SUB + y * TALL
        beside = [pltpu.matmul_pop(place(spot, h)) for h in range(wides)]
        for j in range(tiles):
            lower = center[j, pl.ds(at - 1, TALL), :]
            if y == 0:
                lower = jnp.where(row < 2, 0.0, lower)
            near = (before[j, pl.ds(at, TALL), :] + after[j, pl.ds(at, TALL), :]) + (
                center[j, pl.ds(at + 1, TALL), :] + lower
            )
            h, p = j // part, j % part
            value = near + beside[h][:, p * LANES : (p + 1) * LANES]
            if p == 0 and h:
                value = value + jnp.where(lane == 0, pltpu.roll(center[j - 1, pl.ds(at, TALL), :], 1, 1), 0.0)
            if p == part - 1 and j + 1 < tiles:
                other = pltpu.roll(center[j + 1, pl.ds(at, TALL), :], LANES - 1, 1)
                value = value + jnp.where(lane == LANES - 1, other, 0.0)
            if y == 0:
                value = jnp.where(row == 0, 0.0, value)
            put(j, y, value)

    spot = turn % 2 * 2 * strips
    multiply([(job[0], y, spot + y * 2 + i) for y in range(strips) for i, job in enumerate(jobs)])
    for y in range(strips):
        for i, (center, before, after, put) in enumerate(jobs):
            complete(center, before, after, y, spot + y * 2 + i, put)


def mesh_body(_, mesh_ref, out_ref, kept_out, field, ring, stage, kept, in_sems, out_sems, kept_sems, sums):
    comps, width, height, depth = mesh_ref.shape
    tiles = depth // LANES
    turns = len(ring)
    quads = width // turns - 1

    def load(k, b):
        return [
            pltpu.make_async_copy(
                mesh_ref.at[k, pl.ds(b * turns, turns), :, columns(j)],
                field.at[k, pl.ds(b * turns, turns), j, pl.ds(SUB, height), :],
                in_sems.at[k, b, j],
            )
            for j in range(tiles)
        ]

    for k in range(comps):
        for b in range(width // turns):
            for copy in load(k, b):
                copy.start()

    blank = jnp.zeros((SUB, LANES), f32)
    for j in range(tiles):
        for plane in ring:
            plane[j, SUB + height : 2 * SUB + height, :] = blank

    def clear(i, _):
        for j in range(tiles):
            field[i // width, i % width, j, SUB + height : 2 * SUB + height, :] = blank
        return 0

    lax.fori_loop(0, comps * width, clear, 0)
    for unit, value in enumerate(start_band(sums)):
        stage[unit, 0:TALL, 0:WIDE] = value

    def flush(k, x, slot):
        return pltpu.make_async_copy(stage.at[slot], out_ref.at[k, x], out_sems.at[slot])

    def keep_planes(k):
        return pltpu.make_async_copy(kept.at[k], kept_out.at[k], kept_sems.at[k])

    def work(k, x, phase, slot=None, copy_to=None):
        def put_first(j, y, value):
            ring[phase % turns][j, pl.ds(SUB + y * TALL, TALL), :] = value
            if copy_to is not None:
                kept[k, copy_to, j, pl.ds(y * TALL, TALL), :] = value

        def put_second(j, y, value):
            stage[slot, y * TALL : (y + 1) * TALL, j * LANES : (j + 1) * LANES] = value * (share * share)

        jobs = [(field.at[k, x], field.at[k, x - 1], field.at[k, x + 1], put_first)]
        if slot is not None:
            jobs.append((ring[(phase - 2) % turns], ring[(phase - 3) % turns], ring[(phase - 1) % turns], put_second))
        sweep_planes(jobs, height, depth, sums, phase)

    def component(k, _):
        for b in range(2):
            for copy in load(k, b):
                copy.wait()
        for phase in range(3):
            work(k, phase + 1, phase, None, phase if phase < 2 else None)

        def quad(i, _):
            @pl.when(i + 2 < width // turns)
            def _():
                for copy in load(k, i + 2):
                    copy.wait()

            turn = k * quads + i
            slots = (turn % 2) * turns

            @pl.when(turn >= 2)
            def _():
                for sub in range(turns):
                    flush(k, 0, slots + sub).wait()

            for sub in range(turns):
                place = {1: 2, 2: 3}.get(sub)
                work(k, jnp.minimum(i * turns + sub + 4, width - 2), sub + 3, slots + sub, place)
            for sub in range(turns):
                flush(k, i * turns + sub + 2, slots + sub).start()
            return 0

        lax.fori_loop(0, quads, quad, 0)
        keep_planes(k).start()
        return 0

    lax.fori_loop(0, comps, component, 0)
    for slot in range(2 * turns):
        flush(0, 0, slot).wait()
    for k in range(comps):
        keep_planes(k).wait()


def edges_body(
    base_ref, edge_ref, mesh_ref, kept_ref, left_ref, right_ref, out_ref,
    field, fetched, computed, stage, in_sems, kept_sems, out_sems, sums,
):
    comps, width, height, depth = mesh_ref.shape
    tiles = depth // LANES

    def outer(k, beside=True, own_planes=True):
        found = []
        for side, ref in enumerate((left_ref, right_ref)):
            own, other = (2, 0) if side == 0 else (0, 2)
            for j in range(tiles if own_planes else 0):
                found.append(
                    pltpu.make_async_copy(
                        mesh_ref.at[k, pl.ds(side * (width - 2), 2), :, columns(j)],
                        field.at[k, side, pl.ds(own, 2), j, pl.ds(SUB, height), :],
                        in_sems.at[k, j, side, 0],
                    )
                )
            for p in range(2 if own_planes else 0):
                found.append(
                    pltpu.make_async_copy(
                        kept_ref.at[k, side * 2 + p],
                        fetched.at[k, side, p, :, pl.ds(SUB, height), :],
                        kept_sems.at[k, side, p],
                    )
                )
            for j in range(tiles if beside else 0):
                for p in range(2):
                    found.append(
                        pltpu.make_async_copy(
                            ref.at[pl.ds((k * 2 + p) * height, height), columns(j)],
                            field.at[k, side, other + p, j, pl.ds(SUB, height), :],
                            in_sems.at[k, j, side, 1 + p],
                        )
                    )
        return found

    for beside in (False, True):
        for k in range(comps):
            for copy in outer(k, beside, not beside):
                copy.start()

    blank = jnp.zeros((SUB, LANES), f32)
    for j in range(tiles):
        for place in computed:
            place[j, SUB + height : 2 * SUB + height, :] = blank

    def clear(i, _):
        for side in range(2):
            for j in range(tiles):
                for p in range(4):
                    field[i, side, p, j, SUB + height : 2 * SUB + height, :] = blank
                for p in range(2):
                    fetched[i, side, p, j, SUB + height : 2 * SUB + height, :] = blank
        return 0

    lax.fori_loop(0, comps, clear, 0)
    for unit, value in enumerate(start_band(sums)):
        stage[0, unit, 0:TALL, 0:WIDE] = value
    gates = [jnp.where(edge_ref[side] == 0, 0.0, 1.0) for side in range(2)]

    def save(k):
        return [
            pltpu.make_async_copy(
                stage.at[k, side * 2 + p],
                out_ref.at[k, side * (width - 2) + p],
                out_sems.at[k, side, p],
            )
            for side in range(2)
            for p in range(2)
        ]

    def component(k, _):
        for copy in outer(k):
            copy.wait()
        swept = (
            (computed[0], computed[1], fetched.at[k, 0, 0], fetched.at[k, 0, 1]),
            (fetched.at[k, 1, 0], fetched.at[k, 1, 1], computed[2], computed[3]),
        )
        for p in range(2):
            jobs = []
            for side in range(2):

                def put(j, y, value, side=side):
                    if p == side:
                        value = value * gates[side]
                    computed[side * 2 + p][j, pl.ds(SUB + y * TALL, TALL), :] = value

                jobs.append((field.at[k, side, p + 1], field.at[k, side, p], field.at[k, side, p + 2], put))
            sweep_planes(jobs, height, depth, sums, p)
        for p in range(2):
            jobs = []
            for side in range(2):

                def put(j, y, value, side=side):
                    value = value * (share * share)
                    span = slice(j * LANES, (j + 1) * LANES)
                    stage[k, side * 2 + p, y * TALL : (y + 1) * TALL, span] = value

                jobs.append((swept[side][p + 1], swept[side][p], swept[side][p + 2], put))
            sweep_planes(jobs, height, depth, sums, p)
        for copy in save(k):
            copy.start()
        return 0

    lax.fori_loop(0, comps, component, 0)
    for k in range(comps):
        for copy in save(k):
            copy.wait()


def finish_body(
    base_ref, returned_ref, vertex_ref, left_ref, right_ref, out_ref,
    wall, left, right, split, high_sc, low_sc, sems, *, per,
):
    comps, width, _, depth = wall.shape
    tiles = depth // LANES
    rows = vertex_ref.shape[0]
    count = left.shape[0]
    start = left_ref.shape[0] - count
    fetch = [pltpu.make_async_copy(base_ref.at[k, :, pl.ds(0, SUB), :], wall.at[k], sems.at[k]) for k in range(comps)]
    beside = [
        pltpu.make_async_copy(left_ref.at[pl.ds(start, count), :], left, sems.at[comps]),
        pltpu.make_async_copy(right_ref.at[pl.ds(start, count), :], right, sems.at[comps + 1]),
    ]
    for copy in beside + fetch:
        copy.start()
    whole = returned_ref[...]
    top = whole.astype(bf16).astype(f32)
    split[0] = top
    split[1] = whole - top
    for copy in beside:
        copy.wait()

    def spread(row, size):
        tile = jnp.broadcast_to(row, (TALL, LANES)).astype(bf16)
        return jnp.concatenate([tile] * (size // TALL), axis=0)

    def lines(size):
        return lax.broadcasted_iota(jnp.int32, (size, LANES), 0)

    def gathered(vertices, group, home, lows):
        size = home.shape[0]
        shift = lows.bit_length() - 1
        vertices = jnp.concatenate(vertices, axis=0) if isinstance(vertices, list) else vertices
        high_sc[...] = lax.shift_right_arithmetic(vertices, shift).astype(f32)
        low_sc[...] = jnp.bitwise_and(vertices, lows - 1).astype(f32)
        home = home.astype(f32).astype(bf16)
        line = lines(lows).astype(f32).astype(bf16)
        one = jnp.ones((lows, LANES), bf16)
        nothing = jnp.zeros((lows, LANES), bf16)
        empty = jnp.zeros((size, LANES), bf16)
        total = None
        for first in range(0, rows, 4):
            wide, tall = [], []
            for row in range(first, min(rows, first + 4)):
                wide.append(jnp.where(line == spread(low_sc[row : row + 1, :], lows), one, nothing))
                here = home == spread(high_sc[row : row + 1, :], size)
                parts = []
                for term in range(2):
                    for k in range(comps):
                        value = spread(slot_row(split.at[term], k, row, per, group), size)
                        parts.append(jnp.where(here, value, empty))
                tall.append(jnp.concatenate(parts, axis=0))
            part = lax.dot_general(
                jnp.concatenate(tall, axis=1),
                jnp.concatenate(wide, axis=1),
                (((1,), (1,)), ((), ())),
                preferred_element_type=f32,
            )
            total = part if total is None else total + part
        total = total[: comps * size] + total[comps * size :]
        return [total[k * size : (k + 1) * size] for k in range(comps)]

    blocks = depth // WIDE
    line = lines(width * blocks)
    own = gathered(vertex_ref[...], 0, (line % width) * blocks + line // width, WIDE)
    line = lines(TALL)

    def unfold(ref):
        return [ref[at : at + 1, j * LANES : (j + 1) * LANES].astype(jnp.int32) for at in range(count) for j in range(tiles)]

    last = gathered(unfold(left), 1, jnp.where(line < tiles, (width - 1) * tiles + line, -1), LANES)
    first = gathered(unfold(right), 2, jnp.where(line < tiles, line, -1), LANES)

    lane = lax.broadcasted_iota(jnp.int32, (width, LANES), 1)
    line = lax.broadcasted_iota(jnp.int32, (width, LANES), 0)
    row = lax.broadcasted_iota(jnp.int32, (SUB, LANES), 0)
    flush = [pltpu.make_async_copy(wall.at[k], out_ref.at[k, :, pl.ds(0, SUB), :], sems.at[comps + 2 + k]) for k in range(comps)]
    per_wide = WIDE // LANES
    for k in range(comps):
        parts = []
        for j in range(tiles):
            block, lanes = j // per_wide * width, j % per_wide * LANES
            parts.append(own[k][block : block + width, lanes : lanes + LANES])
        down = [pltpu.roll(p, 1, 1) for p in parts]
        up = [pltpu.roll(p, LANES - 1, 1) for p in parts]
        fetch[k].wait()
        for j in range(tiles):
            mid = parts[j]
            back = jnp.where(lane == 0, down[j - 1] if j else 0.0, down[j])
            fore = jnp.where(lane == LANES - 1, up[j + 1] if j + 1 < tiles else 0.0, up[j])
            prev = jnp.where(line == 0, last[k][j : j + 1], pltpu.roll(mid, 1, 0))
            after = jnp.where(line == width - 1, first[k][j : j + 1], pltpu.roll(mid, width - 1, 0))
            near = ((prev + after) + (back + fore)) * (share * share)
            one = mid * (1.2 * share) + near
            two = mid * (share * share)
            span = slice(j * LANES, (j + 1) * LANES)
            for x in range(width):
                add = jnp.where(row == 1, one[x : x + 1], jnp.where(row == 2, two[x : x + 1], 0.0))
                wall[k, x, :, span] = jnp.where(row == 0, mid[x : x + 1], wall[k, x, :, span] + add)
        flush[k].start()
    for copy in flush:
        copy.wait()


def exchange(packed, per, cap, beside=False):
    if per:
        return lax.all_to_all(packed, "dev", split_axis=0, concat_axis=0, tiled=True)
    count = lax.axis_size("dev")
    split = packed.reshape(3, count, cap)
    if beside:
        blank = jnp.zeros((3, 1, cap), f32)
        before = jnp.concatenate([blank, split[:, :-1]], axis=1)
        after = jnp.concatenate([split[:, 1:], blank], axis=1)
        split = jnp.concatenate([split, before, after], axis=0)
    moved = lax.all_to_all(split, "dev", split_axis=1, concat_axis=1, tiled=True)
    return moved.reshape((split.shape[0],) + packed.shape[1:])


def local(
    displacement,
    send_node,
    member_slot,
    inverse_part,
    source_coord,
    target_coord,
    unity_weight,
    result_pick,
    receive_vertex,
    mesh_before,
):
    count = lax.axis_size("dev")
    place = lax.axis_index("dev")
    send_cap = send_node.shape[0] // count
    result_cap = result_pick.shape[0] // count
    send_per = send_cap // LANES if send_cap % LANES == 0 else 0
    result_per = result_cap // LANES if result_cap % LANES == 0 else 0
    clusters, points = member_slot.shape
    verts = unity_weight.shape[1]
    comps, width, height, depth = mesh_before.shape
    tiles = depth // LANES
    count_rows = receive_vertex.shape[0] // depth

    def packed_shape(per, size, parts=1):
        shape = (count, 3 * per * parts, LANES) if per else (3, size // LANES, LANES)
        return jax.ShapeDtypeStruct(shape, f32)

    up = [(i, i + 1) for i in range(count - 1)]
    down = [(i + 1, i) for i in range(count - 1)]

    field = in_hbm(mesh_before)
    side = (comps * 2 * height + count_rows, depth)
    node_rows = send_node.reshape(-1, LANES)
    small = (
        receive_vertex.reshape(-1, LANES),
        member_slot,
        unity_weight,
        result_pick.reshape(-1, LANES),
        jnp.transpose(source_coord, (1, 0, 2)),
        jnp.transpose(target_coord, (1, 0, 2)),
    )
    outgoing, head, tail, vertices, slots, weight, picks, source, target = pl.pallas_call(
        lambda *refs: pick_body(*refs, per=send_per),
        out_shape=(packed_shape(send_per, send_node.shape[0]), pltpu.HBM(side, f32), pltpu.HBM(side, f32))
        + tuple(pltpu.VMEM(x.shape, x.dtype) for x in small),
        in_specs=[HBM] * 9,
        out_specs=(VMEM, HBM, HBM) + (VMEM,) * 6,
        scratch_shapes=[
            pltpu.VMEM(displacement.shape, f32),
            pltpu.VMEM(node_rows.shape, jnp.int32),
            pltpu.VMEM(side, f32),
            pltpu.VMEM(side, f32),
            pltpu.SemaphoreType.DMA((10,)),
            pltpu.SemaphoreType.DMA((4, comps, 2)),
        ],
        compiler_params=params(6),
        name="pick_nodes",
    )(in_hbm(displacement), in_hbm(node_rows), field, *map(in_hbm, small))
    arrived = exchange(outgoing, send_per, send_cap)
    halo_left = lax.ppermute(tail, "dev", up)
    halo_right = lax.ppermute(head, "dev", down)

    edges = jnp.stack([place, count - 1 - place]).astype(jnp.int32)
    turns = 4
    if width % turns or width < 2 * turns or depth % (2 * WIDE) or height % TALL or tiles > TALL:
        raise ValueError("mesh shape")

    def with_sums(body):
        places = 4 * (height // TALL) * (depth // WIDE // 2)
        sums = tuple(tuple(pltpu.ACC(unit)((TALL, WIDE), f32) for _ in range(places)) for unit in range(2))
        return lambda *refs: pl.run_scoped(lambda *sums: body(*refs, sums), *sums)

    tall = height + 2 * SUB
    outgoing_results = pl.pallas_call(
        lambda *refs: result_body(*refs, per_in=send_per, per_out=result_per),
        out_shape=packed_shape(result_per, result_pick.shape[0], 3),
        in_specs=[VMEM] * 4 + [HBM] + [VMEM] * 2,
        out_specs=VMEM,
        scratch_shapes=[
            pltpu.VMEM(inverse_part.shape, bf16),
            pltpu.VMEM((clusters, SUB, points), f32),
            pltpu.VMEM((clusters, SUB, verts), f32),
            pltpu.SemaphoreType.DMA((clusters,)),
        ],
        compiler_params=params(24),
        name="cluster_results",
    )(arrived, slots, source, target, in_hbm(inverse_part), weight, picks)
    returned = exchange(outgoing_results, result_per, result_cap, True)

    base, kept = pl.pallas_call(
        with_sums(mesh_body),
        out_shape=(
            jax.ShapeDtypeStruct(mesh_before.shape, f32),
            pltpu.HBM((comps, 4, tiles, height, LANES), f32),
        ),
        in_specs=[ANY, HBM],
        out_specs=(HBM, HBM),
        scratch_shapes=[
            pltpu.VMEM((comps, width, tiles, tall, LANES), f32),
            tuple(pltpu.VMEM((tiles, tall, LANES), f32) for _ in range(turns)),
            pltpu.VMEM((2 * turns, height, depth), f32),
            pltpu.VMEM((comps, 4, tiles, height, LANES), f32),
            pltpu.SemaphoreType.DMA((comps, width // turns, tiles)),
            pltpu.SemaphoreType.DMA((2 * turns,)),
            pltpu.SemaphoreType.DMA((comps,)),
        ],
        compiler_params=params(24),
        name="sweeps",
    )(outgoing_results, field)

    outer = pl.pallas_call(
        with_sums(edges_body),
        out_shape=jax.ShapeDtypeStruct(mesh_before.shape, f32),
        in_specs=[HBM, SMEM, HBM, HBM, ANY, ANY],
        out_specs=HBM,
        scratch_shapes=[
            pltpu.VMEM((comps, 2, 4, tiles, tall, LANES), f32),
            pltpu.VMEM((comps, 2, 2, tiles, tall, LANES), f32),
            tuple(pltpu.VMEM((tiles, tall, LANES), f32) for _ in range(4)),
            pltpu.VMEM((comps, 4, height, depth), f32),
            pltpu.SemaphoreType.DMA((comps, tiles, 2, 3)),
            pltpu.SemaphoreType.DMA((comps, 2, 2)),
            pltpu.SemaphoreType.DMA((comps, 2, 2)),
        ],
        input_output_aliases={0: 0},
        compiler_params=params(20),
        name="edges",
    )(in_hbm(base), edges, field, in_hbm(kept), halo_left, halo_right)

    slot_rows = receive_vertex.shape[0] // LANES
    return pl.pallas_call(
        lambda *refs: finish_body(*refs, per=result_per),
        out_shape=jax.ShapeDtypeStruct(mesh_before.shape, f32),
        in_specs=[HBM, VMEM, VMEM, ANY, ANY],
        out_specs=HBM,
        scratch_shapes=[
            pltpu.VMEM((comps, width, SUB, depth), f32),
            pltpu.VMEM((count_rows, depth), f32),
            pltpu.VMEM((count_rows, depth), f32),
            pltpu.VMEM((2,) + returned.shape, f32),
            pltpu.VMEM((slot_rows, LANES), f32),
            pltpu.VMEM((slot_rows, LANES), f32),
            pltpu.SemaphoreType.DMA((2 * comps + 2,)),
        ],
        input_output_aliases={0: 0},
        compiler_params=params(24),
        name="finish",
    )(in_hbm(outer), returned, vertices, halo_left, halo_right)


def solution(mesh):
    in_specs = (
        P(None, "dev"),
        P("dev"),
        P("dev", None),
        P("dev", None, None),
        P("dev", None, None),
        P("dev", None, None),
        P("dev", None),
        P("dev"),
        P("dev"),
        P(None, "dev", None, None),
    )
    out_specs = P(None, "dev", None, None)

    return jax.shard_map(local, mesh=mesh, in_specs=in_specs, out_specs=out_specs, check_vma=False)
```

```python
import math

import jax
import jax.numpy as jnp
from jax import lax
from jax.experimental import pallas as pl
from jax.experimental.pallas import tpu as pltpu
from jax.sharding import PartitionSpec as P


LANES = 128
SUB = 8
TALL = 16
WIDE = 256
share = 0.8 / 6.0
keep = 0.2 / share
sharpness = 8.0
VMEM = pl.BlockSpec(memory_space=pltpu.VMEM)
ANY = pl.BlockSpec(memory_space=pl.ANY)
HBM = pl.BlockSpec(memory_space=pltpu.HBM)
SMEM = pl.BlockSpec(memory_space=pltpu.SMEM)
f32 = jnp.float32
bf16 = jnp.bfloat16


def in_hbm(value):
    return pltpu.with_memory_space_constraint(value, pltpu.HBM)


def params(limit, **more):
    return pltpu.CompilerParams(vmem_limit_bytes=limit << 20, **more)


def lane_gather(row, lane):
    return jnp.take_along_axis(row, lane, axis=1, mode="promise_in_bounds")


def gather_rows(row_of, blocks, index_of, groups):
    index = [index_of(g) for g in range(groups)]
    high = [lax.shift_right_arithmetic(i, 7) for i in index]
    low = [jnp.bitwise_and(i, LANES - 1) for i in index]
    out = [[jnp.zeros((SUB, LANES), f32) for _ in range(3)] for _ in range(groups)]
    for block in range(blocks):
        rows = [jnp.broadcast_to(row_of(k, block), (SUB, LANES)) for k in range(3)]
        for g in range(groups):
            here = high[g] == block
            for k in range(3):
                out[g][k] = jnp.where(here, lane_gather(rows[k], low[g]), out[g][k])
    return out


def slot_row(ref, k, row, per, group=0):
    if per:
        at = row % per
        return ref[row // per, group * 3 + k, at : at + 1, :]
    return ref[group * 3 + k, row : row + 1, :]


def store_rows(out_ref, g, values, per, beside=False):
    for k in range(3):
        for s in range(SUB):
            row = g * SUB + s
            value = values[k][s : s + 1, :]
            if per:
                d, at = row // per, row % per
                out_ref[d, k, at : at + 1, :] = value
                if beside and d + 1 < out_ref.shape[0]:
                    out_ref[d + 1, 3 + k, at : at + 1, :] = value
                if beside and d > 0:
                    out_ref[d - 1, 6 + k, at : at + 1, :] = value
            else:
                out_ref[k, row : row + 1, :] = value


def pick_body(
    table_hbm, index_hbm, mesh_ref, vertex_hbm, slot_hbm, weight_hbm, pick_hbm, source_hbm, target_hbm,
    out_ref, head_out, tail_out, vertex_ref, slot_ref, weight_ref, pick_ref, source_ref, target_ref,
    table_ref, index_ref, head, tail, sems, side_sems, *, per,
):
    comps, width, height, depth = mesh_ref.shape
    tiles = depth // LANES
    pairs = (
        (index_hbm, index_ref), (table_hbm, table_ref), (vertex_hbm, vertex_ref), (slot_hbm, slot_ref),
        (weight_hbm, weight_ref), (pick_hbm, pick_ref), (source_hbm, source_ref), (target_hbm, target_ref),
    )
    needed = [pltpu.make_async_copy(a, b, sems.at[i]) for i, (a, b) in enumerate(pairs)]
    side, side_out = [], []
    for k in range(comps):
        for p in range(2):
            rows = pl.ds((k * 2 + p) * height, height)
            side_out.append(pltpu.make_async_copy(head.at[rows], head_out.at[rows], side_sems.at[2, k, p]))
            side_out.append(pltpu.make_async_copy(tail.at[rows], tail_out.at[rows], side_sems.at[3, k, p]))
            side.append(pltpu.make_async_copy(mesh_ref.at[k, p], head.at[rows], side_sems.at[0, k, p]))
            side.append(
                pltpu.make_async_copy(mesh_ref.at[k, width - 2 + p], tail.at[rows], side_sems.at[1, k, p])
            )
    for copy in needed[:3] + side + needed[3:]:
        copy.start()
    for copy in needed[:2]:
        copy.wait()
    groups = index_ref.shape[0] // SUB
    blocks = table_ref.shape[1] // LANES
    half = max(1, groups // 8)
    for first in range(0, groups, half):
        got = gather_rows(
            lambda k, b: table_ref[k : k + 1, b * LANES : (b + 1) * LANES],
            blocks,
            lambda g: index_ref[(first + g) * SUB : (first + g + 1) * SUB, :],
            half,
        )
        for g in range(half):
            store_rows(out_ref, first + g, got[g], per)
        if first == 0:
            needed[2].wait()
            start = comps * 2 * height
            for row in range(vertex_ref.shape[0]):
                value = vertex_ref[row : row + 1, :].astype(f32)
                at, j = start + row // tiles, row % tiles * LANES
                head[at : at + 1, j : j + LANES] = value
                tail[at : at + 1, j : j + LANES] = value
            rest = pl.ds(start, head.shape[0] - start)
            leave = [
                pltpu.make_async_copy(head.at[rest], head_out.at[rest], sems.at[8]),
                pltpu.make_async_copy(tail.at[rest], tail_out.at[rest], sems.at[9]),
            ]
            for copy in leave:
                copy.start()
            for before, after in zip(side, side_out):
                before.wait()
                after.start()
            leave = leave + side_out
    for copy in needed[3:] + leave:
        copy.wait()


def pieces(value, count=3):
    found = []
    for _ in range(count):
        top = value.astype(bf16).astype(f32)
        found.append(top)
        value = value - top
    return found


def factor(points, target):
    square = points * points
    norm = jnp.broadcast_to(jnp.sum(square, axis=0, keepdims=True), square.shape)
    row = lax.broadcasted_iota(jnp.int32, square.shape, 0)
    a, b, c = pieces(norm)
    p, q, r = pieces(points)
    if target:
        edge = jnp.where(row < 3, -1.0, jnp.where(row == 3, -a, jnp.where(row == 4, -b, jnp.where(row == 5, -c, 0.0))))
        blocks = [2.0 * p, 2.0 * q, 2.0 * p, 2.0 * q, 2.0 * r, 2.0 * p, edge]
    else:
        edge = jnp.where(row == 0, a, jnp.where(row == 1, b, jnp.where(row == 2, c, jnp.where(row < 6, 1.0, 0.0))))
        blocks = [p, p, q, q, p, r, edge]
    blocks.append(jnp.zeros(square.shape, f32))
    return jnp.concatenate(blocks, axis=0)


def rbf_factors(source, target):
    scale = math.sqrt(sharpness * math.log2(math.e))

    def centred(rows):
        blank = jnp.zeros((SUB - 3, rows[0].shape[1]), f32)
        return jnp.concatenate([(row - 0.5) * scale for row in rows] + [blank], axis=0)

    return jnp.transpose(factor(centred(source), False)).astype(bf16), factor(centred(target), True).astype(bf16)


def result_body(
    arrived_ref, slot_ref, source_ref, target_ref, inverse_ref, weight_ref, pick_ref,
    out_ref, inverse, members, results, sems, *, per_in, per_out,
):
    clusters, points = slot_ref.shape
    verts = weight_ref.shape[1]
    blocks = (arrived_ref.shape[0] * per_in) if per_in else arrived_ref.shape[1]
    per_cluster = verts // LANES
    groups = pick_ref.shape[0] // SUB
    fold = points // LANES // SUB
    copies = [pltpu.make_async_copy(inverse_ref.at[c], inverse.at[c], sems.at[c]) for c in range(clusters)]
    for copy in copies:
        copy.start()
    members[...] = jnp.zeros(members.shape, f32)

    def gather_members(c):
        got = gather_rows(
            lambda k, b: slot_row(arrived_ref, k, b, per_in),
            blocks,
            lambda g: jnp.concatenate(
                [slot_ref[c : c + 1, (g * SUB + j) * LANES : (g * SUB + j + 1) * LANES] for j in range(SUB)], axis=0
            ),
            fold,
        )
        for g in range(fold):
            for j in range(SUB):
                at = (g * SUB + j) * LANES
                for k in range(3):
                    members[c, k : k + 1, at : at + LANES] = got[g][k][j : j + 1, :]

    def evaluate(c):
        turned, right = rbf_factors(*(tuple(ref[k, c : c + 1, :] for k in range(3)) for ref in (source_ref, target_ref)))

        def block(at):
            value = jnp.exp2(jnp.dot(turned[at : at + WIDE], right, preferred_element_type=f32))
            high = value.astype(bf16)
            return high, (value - high.astype(f32)).astype(bf16)

        ready = block(0)
        mine = members[c]
        copies[c].wait()
        coupling = lax.dot_general(
            mine.astype(bf16), inverse[c], (((1,), (1,)), ((), ())), preferred_element_type=f32
        )
        coefficient = mine + coupling
        c_high = coefficient.astype(bf16)
        c_low = (coefficient - c_high.astype(f32)).astype(bf16)
        both = jnp.concatenate([c_high, c_low], axis=0)
        first = jnp.zeros((2 * SUB, verts), f32)
        second = jnp.zeros((SUB, verts), f32)
        for at in range(0, points, WIDE):
            high, low = ready
            if at + WIDE < points:
                ready = block(at + WIDE)
            first = first + jnp.dot(both[:, at : at + WIDE], high, preferred_element_type=f32)
            second = second + jnp.dot(c_high[:, at : at + WIDE], low, preferred_element_type=f32)
        total = first[:SUB] + (first[SUB:] + second)
        results[c] = total * weight_ref[c : c + 1, :]

    for c in range(clusters):
        gather_members(c)
        evaluate(c)
    if per_out:
        blank = jnp.zeros((per_out, LANES), f32)
        for k in range(3):
            out_ref[0, 3 + k] = blank
            out_ref[out_ref.shape[0] - 1, 6 + k] = blank
    half = max(1, groups // 2)
    for start in range(0, groups, half):
        got = gather_rows(
            lambda k, b: results[
                b // per_cluster, k : k + 1, (b % per_cluster) * LANES : (b % per_cluster + 1) * LANES
            ],
            clusters * per_cluster,
            lambda g: pick_ref[(start + g) * SUB : (start + g + 1) * SUB, :],
            half,
        )
        for g in range(half):
            store_rows(out_ref, start + g, got[g], per_out, True)


def columns(j):
    return pl.ds(j * LANES, LANES)


def start_band(sums):
    line = lax.broadcasted_iota(jnp.int32, (WIDE, WIDE), 0)
    column = lax.broadcasted_iota(jnp.int32, (WIDE, WIDE), 1)
    apart = jnp.abs(line - column)
    band = jnp.where(apart == 0, keep, jnp.where(apart == 1, 1.0, 0.0)).astype(bf16)
    ends = []
    for unit in range(len(sums)):
        pltpu.matmul_push_rhs(band, 0, unit)
        pltpu.matmul_acc_lhs(sums[unit][0], jnp.zeros((TALL, WIDE), bf16), load_staged_rhs=0)
        ends.append(pltpu.matmul_pop(sums[unit][0]))
    return ends


def sweep_planes(jobs, height, depth, sums, turn):
    tiles, strips = depth // LANES, height // TALL
    wides, part = depth // WIDE, WIDE // LANES
    units = len(sums)
    halves = wides // units
    lane = lax.broadcasted_iota(jnp.int32, (TALL, LANES), 1)
    row = lax.broadcasted_iota(jnp.int32, (TALL, LANES), 0)

    def place(spot, h):
        return sums[h % units][spot * halves + h // units]

    def multiply(todo):
        later = []
        for center, y, spot in todo:
            for h in range(wides):
                value = jnp.concatenate(
                    [center[j, pl.ds(SUB + y * TALL, TALL), :] for j in range(h * part, (h + 1) * part)], axis=1
                )
                high = value.astype(bf16)
                pltpu.matmul_acc_lhs(place(spot, h), high)
                later.append((place(spot, h), (value - high.astype(f32)).astype(bf16)))
        for total, low in later:
            pltpu.matmul_acc_lhs(total, low)

    def complete(center, before, after, y, spot, put):
        at = SUB + y * TALL
        beside = [pltpu.matmul_pop(place(spot, h)) for h in range(wides)]
        for j in range(tiles):
            lower = center[j, pl.ds(at - 1, TALL), :]
            if y == 0:
                lower = jnp.where(row < 2, 0.0, lower)
            near = (before[j, pl.ds(at, TALL), :] + after[j, pl.ds(at, TALL), :]) + (
                center[j, pl.ds(at + 1, TALL), :] + lower
            )
            h, p = j // part, j % part
            value = near + beside[h][:, p * LANES : (p + 1) * LANES]
            if p == 0 and h:
                value = value + jnp.where(lane == 0, pltpu.roll(center[j - 1, pl.ds(at, TALL), :], 1, 1), 0.0)
            if p == part - 1 and j + 1 < tiles:
                other = pltpu.roll(center[j + 1, pl.ds(at, TALL), :], LANES - 1, 1)
                value = value + jnp.where(lane == LANES - 1, other, 0.0)
            if y == 0:
                value = jnp.where(row == 0, 0.0, value)
            put(j, y, value)

    spot = turn % 2 * 2 * strips
    multiply([(job[0], y, spot + y * 2 + i) for y in range(strips) for i, job in enumerate(jobs)])
    for y in range(strips):
        for i, (center, before, after, put) in enumerate(jobs):
            complete(center, before, after, y, spot + y * 2 + i, put)


def mesh_body(_, mesh_ref, out_ref, kept_out, field, ring, stage, kept, in_sems, out_sems, kept_sems, sums):
    comps, width, height, depth = mesh_ref.shape
    tiles = depth // LANES
    turns = len(ring)
    quads = width // turns - 1

    def load(k, b):
        return [
            pltpu.make_async_copy(
                mesh_ref.at[k, pl.ds(b * turns, turns), :, columns(j)],
                field.at[k, pl.ds(b * turns, turns), j, pl.ds(SUB, height), :],
                in_sems.at[k, b, j],
            )
            for j in range(tiles)
        ]

    for k in range(comps):
        for b in range(width // turns):
            for copy in load(k, b):
                copy.start()

    blank = jnp.zeros((SUB, LANES), f32)
    for j in range(tiles):
        for plane in ring:
            plane[j, SUB + height : 2 * SUB + height, :] = blank

    def clear(i, _):
        for j in range(tiles):
            field[i // width, i % width, j, SUB + height : 2 * SUB + height, :] = blank
        return 0

    lax.fori_loop(0, comps * width, clear, 0)
    for unit, value in enumerate(start_band(sums)):
        stage[unit, 0:TALL, 0:WIDE] = value

    def flush(k, x, slot):
        return pltpu.make_async_copy(stage.at[slot], out_ref.at[k, x], out_sems.at[slot])

    def keep_planes(k):
        return pltpu.make_async_copy(kept.at[k], kept_out.at[k], kept_sems.at[k])

    def work(k, x, phase, slot=None, copy_to=None):
        def put_first(j, y, value):
            ring[phase % turns][j, pl.ds(SUB + y * TALL, TALL), :] = value
            if copy_to is not None:
                kept[k, copy_to, j, pl.ds(y * TALL, TALL), :] = value

        def put_second(j, y, value):
            stage[slot, y * TALL : (y + 1) * TALL, j * LANES : (j + 1) * LANES] = value * (share * share)

        jobs = [(field.at[k, x], field.at[k, x - 1], field.at[k, x + 1], put_first)]
        if slot is not None:
            jobs.append((ring[(phase - 2) % turns], ring[(phase - 3) % turns], ring[(phase - 1) % turns], put_second))
        sweep_planes(jobs, height, depth, sums, phase)

    def component(k, _):
        for b in range(2):
            for copy in load(k, b):
                copy.wait()
        for phase in range(3):
            work(k, phase + 1, phase, None, phase if phase < 2 else None)

        def quad(i, _):
            @pl.when(i + 2 < width // turns)
            def _():
                for copy in load(k, i + 2):
                    copy.wait()

            turn = k * quads + i
            slots = (turn % 2) * turns

            @pl.when(turn >= 2)
            def _():
                for sub in range(turns):
                    flush(k, 0, slots + sub).wait()

            for sub in range(turns):
                place = {1: 2, 2: 3}.get(sub)
                work(k, jnp.minimum(i * turns + sub + 4, width - 2), sub + 3, slots + sub, place)
            for sub in range(turns):
                flush(k, i * turns + sub + 2, slots + sub).start()
            return 0

        lax.fori_loop(0, quads, quad, 0)
        keep_planes(k).start()
        return 0

    lax.fori_loop(0, comps, component, 0)
    for slot in range(2 * turns):
        flush(0, 0, slot).wait()
    for k in range(comps):
        keep_planes(k).wait()


def edges_body(
    base_ref, edge_ref, mesh_ref, kept_ref, left_ref, right_ref, out_ref,
    field, fetched, computed, stage, in_sems, kept_sems, out_sems, sums,
):
    comps, width, height, depth = mesh_ref.shape
    tiles = depth // LANES

    def outer(k, beside=True, own_planes=True):
        found = []
        for side, ref in enumerate((left_ref, right_ref)):
            own, other = (2, 0) if side == 0 else (0, 2)
            for j in range(tiles if own_planes else 0):
                found.append(
                    pltpu.make_async_copy(
                        mesh_ref.at[k, pl.ds(side * (width - 2), 2), :, columns(j)],
                        field.at[k, side, pl.ds(own, 2), j, pl.ds(SUB, height), :],
                        in_sems.at[k, j, side, 0],
                    )
                )
            for p in range(2 if own_planes else 0):
                found.append(
                    pltpu.make_async_copy(
                        kept_ref.at[k, side * 2 + p],
                        fetched.at[k, side, p, :, pl.ds(SUB, height), :],
                        kept_sems.at[k, side, p],
                    )
                )
            for j in range(tiles if beside else 0):
                for p in range(2):
                    found.append(
                        pltpu.make_async_copy(
                            ref.at[pl.ds((k * 2 + p) * height, height), columns(j)],
                            field.at[k, side, other + p, j, pl.ds(SUB, height), :],
                            in_sems.at[k, j, side, 1 + p],
                        )
                    )
        return found

    for beside in (False, True):
        for k in range(comps):
            for copy in outer(k, beside, not beside):
                copy.start()

    blank = jnp.zeros((SUB, LANES), f32)
    for j in range(tiles):
        for place in computed:
            place[j, SUB + height : 2 * SUB + height, :] = blank

    def clear(i, _):
        for side in range(2):
            for j in range(tiles):
                for p in range(4):
                    field[i, side, p, j, SUB + height : 2 * SUB + height, :] = blank
                for p in range(2):
                    fetched[i, side, p, j, SUB + height : 2 * SUB + height, :] = blank
        return 0

    lax.fori_loop(0, comps, clear, 0)
    for unit, value in enumerate(start_band(sums)):
        stage[0, unit, 0:TALL, 0:WIDE] = value
    gates = [jnp.where(edge_ref[side] == 0, 0.0, 1.0) for side in range(2)]

    def save(k):
        return [
            pltpu.make_async_copy(
                stage.at[k, side * 2 + p],
                out_ref.at[k, side * (width - 2) + p],
                out_sems.at[k, side, p],
            )
            for side in range(2)
            for p in range(2)
        ]

    def component(k, _):
        for copy in outer(k):
            copy.wait()
        swept = (
            (computed[0], computed[1], fetched.at[k, 0, 0], fetched.at[k, 0, 1]),
            (fetched.at[k, 1, 0], fetched.at[k, 1, 1], computed[2], computed[3]),
        )
        for p in range(2):
            jobs = []
            for side in range(2):

                def put(j, y, value, side=side):
                    if p == side:
                        value = value * gates[side]
                    computed[side * 2 + p][j, pl.ds(SUB + y * TALL, TALL), :] = value

                jobs.append((field.at[k, side, p + 1], field.at[k, side, p], field.at[k, side, p + 2], put))
            sweep_planes(jobs, height, depth, sums, p)
        for p in range(2):
            jobs = []
            for side in range(2):

                def put(j, y, value, side=side):
                    value = value * (share * share)
                    span = slice(j * LANES, (j + 1) * LANES)
                    stage[k, side * 2 + p, y * TALL : (y + 1) * TALL, span] = value

                jobs.append((swept[side][p + 1], swept[side][p], swept[side][p + 2], put))
            sweep_planes(jobs, height, depth, sums, p)
        for copy in save(k):
            copy.start()
        return 0

    lax.fori_loop(0, comps, component, 0)
    for k in range(comps):
        for copy in save(k):
            copy.wait()


def finish_body(
    base_ref, returned_ref, vertex_ref, left_ref, right_ref, out_ref,
    wall, left, right, split, high_sc, low_sc, sems, *, per,
):
    comps, width, _, depth = wall.shape
    tiles = depth // LANES
    rows = vertex_ref.shape[0]
    count = left.shape[0]
    start = left_ref.shape[0] - count
    fetch = [pltpu.make_async_copy(base_ref.at[k, :, pl.ds(0, SUB), :], wall.at[k], sems.at[k]) for k in range(comps)]
    beside = [
        pltpu.make_async_copy(left_ref.at[pl.ds(start, count), :], left, sems.at[comps]),
        pltpu.make_async_copy(right_ref.at[pl.ds(start, count), :], right, sems.at[comps + 1]),
    ]
    for copy in beside + fetch:
        copy.start()
    whole = returned_ref[...]
    top = whole.astype(bf16).astype(f32)
    split[0] = top
    split[1] = whole - top
    for copy in beside:
        copy.wait()

    def spread(row, size):
        tile = jnp.broadcast_to(row, (TALL, LANES)).astype(bf16)
        return jnp.concatenate([tile] * (size // TALL), axis=0)

    def lines(size):
        return lax.broadcasted_iota(jnp.int32, (size, LANES), 0)

    def gathered(vertices, group, home, lows):
        size = home.shape[0]
        shift = lows.bit_length() - 1
        vertices = jnp.concatenate(vertices, axis=0) if isinstance(vertices, list) else vertices
        high_sc[...] = lax.shift_right_arithmetic(vertices, shift).astype(f32)
        low_sc[...] = jnp.bitwise_and(vertices, lows - 1).astype(f32)
        home = home.astype(f32).astype(bf16)
        line = lines(lows).astype(f32).astype(bf16)
        one = jnp.ones((lows, LANES), bf16)
        nothing = jnp.zeros((lows, LANES), bf16)
        empty = jnp.zeros((size, LANES), bf16)
        total = None
        for first in range(0, rows, 4):
            wide, tall = [], []
            for row in range(first, min(rows, first + 4)):
                wide.append(jnp.where(line == spread(low_sc[row : row + 1, :], lows), one, nothing))
                here = home == spread(high_sc[row : row + 1, :], size)
                parts = []
                for term in range(2):
                    for k in range(comps):
                        value = spread(slot_row(split.at[term], k, row, per, group), size)
                        parts.append(jnp.where(here, value, empty))
                tall.append(jnp.concatenate(parts, axis=0))
            part = lax.dot_general(
                jnp.concatenate(tall, axis=1),
                jnp.concatenate(wide, axis=1),
                (((1,), (1,)), ((), ())),
                preferred_element_type=f32,
            )
            total = part if total is None else total + part
        total = total[: comps * size] + total[comps * size :]
        return [total[k * size : (k + 1) * size] for k in range(comps)]

    blocks = depth // WIDE
    line = lines(width * blocks)
    own = gathered(vertex_ref[...], 0, (line % width) * blocks + line // width, WIDE)
    line = lines(TALL)

    def unfold(ref):
        return [ref[at : at + 1, j * LANES : (j + 1) * LANES].astype(jnp.int32) for at in range(count) for j in range(tiles)]

    last = gathered(unfold(left), 1, jnp.where(line < tiles, (width - 1) * tiles + line, -1), LANES)
    first = gathered(unfold(right), 2, jnp.where(line < tiles, line, -1), LANES)

    lane = lax.broadcasted_iota(jnp.int32, (width, LANES), 1)
    line = lax.broadcasted_iota(jnp.int32, (width, LANES), 0)
    row = lax.broadcasted_iota(jnp.int32, (SUB, LANES), 0)
    flush = [pltpu.make_async_copy(wall.at[k], out_ref.at[k, :, pl.ds(0, SUB), :], sems.at[comps + 2 + k]) for k in range(comps)]
    per_wide = WIDE // LANES
    for k in range(comps):
        parts = []
        for j in range(tiles):
            block, lanes = j // per_wide * width, j % per_wide * LANES
            parts.append(own[k][block : block + width, lanes : lanes + LANES])
        down = [pltpu.roll(p, 1, 1) for p in parts]
        up = [pltpu.roll(p, LANES - 1, 1) for p in parts]
        fetch[k].wait()
        for j in range(tiles):
            mid = parts[j]
            back = jnp.where(lane == 0, down[j - 1] if j else 0.0, down[j])
            fore = jnp.where(lane == LANES - 1, up[j + 1] if j + 1 < tiles else 0.0, up[j])
            prev = jnp.where(line == 0, last[k][j : j + 1], pltpu.roll(mid, 1, 0))
            after = jnp.where(line == width - 1, first[k][j : j + 1], pltpu.roll(mid, width - 1, 0))
            near = ((prev + after) + (back + fore)) * (share * share)
            one = mid * (1.2 * share) + near
            two = mid * (share * share)
            span = slice(j * LANES, (j + 1) * LANES)
            for x in range(width):
                add = jnp.where(row == 1, one[x : x + 1], jnp.where(row == 2, two[x : x + 1], 0.0))
                wall[k, x, :, span] = jnp.where(row == 0, mid[x : x + 1], wall[k, x, :, span] + add)
        flush[k].start()
    for copy in flush:
        copy.wait()


def exchange(packed, per, cap, beside=False):
    if per:
        return lax.all_to_all(packed, "dev", split_axis=0, concat_axis=0, tiled=True)
    count = lax.axis_size("dev")
    split = packed.reshape(3, count, cap)
    if beside:
        blank = jnp.zeros((3, 1, cap), f32)
        before = jnp.concatenate([blank, split[:, :-1]], axis=1)
        after = jnp.concatenate([split[:, 1:], blank], axis=1)
        split = jnp.concatenate([split, before, after], axis=0)
    moved = lax.all_to_all(split, "dev", split_axis=1, concat_axis=1, tiled=True)
    return moved.reshape((split.shape[0],) + packed.shape[1:])


def local(
    displacement,
    send_node,
    member_slot,
    inverse_part,
    source_coord,
    target_coord,
    unity_weight,
    result_pick,
    receive_vertex,
    mesh_before,
):
    count = lax.axis_size("dev")
    place = lax.axis_index("dev")
    send_cap = send_node.shape[0] // count
    result_cap = result_pick.shape[0] // count
    send_per = send_cap // LANES if send_cap % LANES == 0 else 0
    result_per = result_cap // LANES if result_cap % LANES == 0 else 0
    clusters, points = member_slot.shape
    verts = unity_weight.shape[1]
    comps, width, height, depth = mesh_before.shape
    tiles = depth // LANES
    count_rows = receive_vertex.shape[0] // depth

    def packed_shape(per, size, parts=1):
        shape = (count, 3 * parts, per, LANES) if per else (3, size // LANES, LANES)
        return jax.ShapeDtypeStruct(shape, f32)

    up = [(i, i + 1) for i in range(count - 1)]
    down = [(i + 1, i) for i in range(count - 1)]

    field = in_hbm(mesh_before)
    side = (comps * 2 * height + count_rows, depth)
    node_rows = send_node.reshape(-1, LANES)
    small = (
        receive_vertex.reshape(-1, LANES),
        member_slot,
        unity_weight,
        result_pick.reshape(-1, LANES),
        jnp.transpose(source_coord, (1, 0, 2)),
        jnp.transpose(target_coord, (1, 0, 2)),
    )
    outgoing, head, tail, vertices, slots, weight, picks, source, target = pl.pallas_call(
        lambda *refs: pick_body(*refs, per=send_per),
        out_shape=(packed_shape(send_per, send_node.shape[0]), pltpu.HBM(side, f32), pltpu.HBM(side, f32))
        + tuple(pltpu.VMEM(x.shape, x.dtype) for x in small),
        in_specs=[HBM] * 9,
        out_specs=(VMEM, HBM, HBM) + (VMEM,) * 6,
        scratch_shapes=[
            pltpu.VMEM(displacement.shape, f32),
            pltpu.VMEM(node_rows.shape, jnp.int32),
            pltpu.VMEM(side, f32),
            pltpu.VMEM(side, f32),
            pltpu.SemaphoreType.DMA((10,)),
            pltpu.SemaphoreType.DMA((4, comps, 2)),
        ],
        compiler_params=params(6),
        name="pick_nodes",
    )(in_hbm(displacement), in_hbm(node_rows), field, *map(in_hbm, small))
    arrived = exchange(outgoing, send_per, send_cap)
    halo_left = lax.ppermute(tail, "dev", up)
    halo_right = lax.ppermute(head, "dev", down)

    edges = jnp.stack([place, count - 1 - place]).astype(jnp.int32)
    turns = 4
    if width % turns or width < 2 * turns or depth % (2 * WIDE) or height % TALL or tiles > TALL:
        raise ValueError("mesh shape")

    def with_sums(body):
        places = 4 * (height // TALL) * (depth // WIDE // 2)
        sums = tuple(tuple(pltpu.ACC(unit)((TALL, WIDE), f32) for _ in range(places)) for unit in range(2))
        return lambda *refs: pl.run_scoped(lambda *sums: body(*refs, sums), *sums)

    tall = height + 2 * SUB
    outgoing_results = pl.pallas_call(
        lambda *refs: result_body(*refs, per_in=send_per, per_out=result_per),
        out_shape=packed_shape(result_per, result_pick.shape[0], 3),
        in_specs=[VMEM] * 4 + [HBM] + [VMEM] * 2,
        out_specs=VMEM,
        scratch_shapes=[
            pltpu.VMEM(inverse_part.shape, bf16),
            pltpu.VMEM((clusters, SUB, points), f32),
            pltpu.VMEM((clusters, SUB, verts), f32),
            pltpu.SemaphoreType.DMA((clusters,)),
        ],
        compiler_params=params(24),
        name="cluster_results",
    )(arrived, slots, source, target, in_hbm(inverse_part), weight, picks)
    returned = exchange(outgoing_results, result_per, result_cap, True)

    base, kept = pl.pallas_call(
        with_sums(mesh_body),
        out_shape=(
            jax.ShapeDtypeStruct(mesh_before.shape, f32),
            pltpu.HBM((comps, 4, tiles, height, LANES), f32),
        ),
        in_specs=[ANY, HBM],
        out_specs=(HBM, HBM),
        scratch_shapes=[
            pltpu.VMEM((comps, width, tiles, tall, LANES), f32),
            tuple(pltpu.VMEM((tiles, tall, LANES), f32) for _ in range(turns)),
            pltpu.VMEM((2 * turns, height, depth), f32),
            pltpu.VMEM((comps, 4, tiles, height, LANES), f32),
            pltpu.SemaphoreType.DMA((comps, width // turns, tiles)),
            pltpu.SemaphoreType.DMA((2 * turns,)),
            pltpu.SemaphoreType.DMA((comps,)),
        ],
        compiler_params=params(24),
        name="sweeps",
    )(outgoing_results, field)

    outer = pl.pallas_call(
        with_sums(edges_body),
        out_shape=jax.ShapeDtypeStruct(mesh_before.shape, f32),
        in_specs=[HBM, SMEM, HBM, HBM, ANY, ANY],
        out_specs=HBM,
        scratch_shapes=[
            pltpu.VMEM((comps, 2, 4, tiles, tall, LANES), f32),
            pltpu.VMEM((comps, 2, 2, tiles, tall, LANES), f32),
            tuple(pltpu.VMEM((tiles, tall, LANES), f32) for _ in range(4)),
            pltpu.VMEM((comps, 4, height, depth), f32),
            pltpu.SemaphoreType.DMA((comps, tiles, 2, 3)),
            pltpu.SemaphoreType.DMA((comps, 2, 2)),
            pltpu.SemaphoreType.DMA((comps, 2, 2)),
        ],
        input_output_aliases={0: 0},
        compiler_params=params(20),
        name="edges",
    )(in_hbm(base), edges, field, in_hbm(kept), halo_left, halo_right)

    slot_rows = receive_vertex.shape[0] // LANES
    return pl.pallas_call(
        lambda *refs: finish_body(*refs, per=result_per),
        out_shape=jax.ShapeDtypeStruct(mesh_before.shape, f32),
        in_specs=[HBM, VMEM, VMEM, ANY, ANY],
        out_specs=HBM,
        scratch_shapes=[
            pltpu.VMEM((comps, width, SUB, depth), f32),
            pltpu.VMEM((count_rows, depth), f32),
            pltpu.VMEM((count_rows, depth), f32),
            pltpu.VMEM((2,) + returned.shape, f32),
            pltpu.VMEM((slot_rows, LANES), f32),
            pltpu.VMEM((slot_rows, LANES), f32),
            pltpu.SemaphoreType.DMA((2 * comps + 2,)),
        ],
        input_output_aliases={0: 0},
        compiler_params=params(24),
        name="finish",
    )(in_hbm(outer), returned, vertices, halo_left, halo_right)


def solution(mesh):
    in_specs = (
        P(None, "dev"),
        P("dev"),
        P("dev", None),
        P("dev", None, None),
        P("dev", None, None),
        P("dev", None, None),
        P("dev", None),
        P("dev"),
        P("dev"),
        P(None, "dev", None, None),
    )
    out_specs = P(None, "dev", None, None)

    return jax.shard_map(local, mesh=mesh, in_specs=in_specs, out_specs=out_specs, check_vma=False)
```
